32 devices in a mesh: grp: 4 (over y, x), ctx: 8 (over z, core).
Axes of the slice: x: 2, y: 2, z: 4, core: 2. Of those that a mesh axis runs over, the one named last changes fastest.
Arguments:
- hidden_in: bfloat16 [8, 1024, 1024], P('grp', 'ctx'), may hold values from -6 to 6
- grad_out: bfloat16 [8, 1024, 1024], P('grp', 'ctx'), may hold values from -6 to 6
- segments: int32 [8, 1024], P('grp'), may hold values from 0 to 4, as said below
- routes: int32 [8, 1024, 8], P('grp', 'ctx'), may hold values from 0 to 31, all different within a row; in each aligned block of 128 rows (0 to 127, 128 to 255, ..., all dimensions but the last counted through in order) at most 42 rows name the same one
- attn_gain: bfloat16 [2, 1024], P(None, ('grp', 'ctx')), may hold values from 0.5 to 1.5
- w_query: bfloat16 [2, 1024, 1024], P(None, ('grp', 'ctx')), may hold values from -0.1875 to 0.1875
- key_weight: bfloat16 [2, 1024, 512], P(None, ('grp', 'ctx')), may hold values from -0.1875 to 0.1875
- value_weight: bfloat16 [2, 1024, 512], P(None, ('grp', 'ctx')), may hold values from -0.1875 to 0.1875
- w_output: bfloat16 [2, 1024, 1024], P(None, ('grp', 'ctx')), may hold values from -1.5 to 1.5
- ffn_gain: bfloat16 [2, 1024], P(None, ('grp', 'ctx')), may hold values from 0.5 to 1.5
- w_router: bfloat16 [2, 1024, 32], P(None, ('grp', 'ctx')), may hold values from -0.09375 to 0.09375
- w_gate: bfloat16 [2, 32, 1024, 512], P(None, 'grp', 'ctx'), may hold values from -0.1875 to 0.1875
- w_up: bfloat16 [2, 32, 1024, 512], P(None, 'grp', 'ctx'), may hold values from -0.1875 to 0.1875
- w_down: bfloat16 [2, 32, 512, 1024], P(None, 'grp', 'ctx'), may hold values from -0.75 to 0.75
Outputs:
- hidden_out: bfloat16 [8, 1024, 1024], P('grp', 'ctx')
- grad_in: float32 [8, 1024, 1024], P('grp', 'ctx')
- grad_attn_gain: float32 [2, 1024], P(None, ('grp', 'ctx'))
- grad_query: float32 [2, 1024, 1024], P(None, ('grp', 'ctx'))
- grad_key: float32 [2, 1024, 512], P(None, ('grp', 'ctx'))
- grad_value: float32 [2, 1024, 512], P(None, ('grp', 'ctx'))
- grad_output: float32 [2, 1024, 1024], P(None, ('grp', 'ctx'))
- grad_ffn_gain: float32 [2, 1024], P(None, ('grp', 'ctx'))
- grad_router: float32 [2, 1024, 32], P(None, ('grp', 'ctx'))
- grad_gate: float32 [2, 32, 1024, 512], P(None, 'grp', 'ctx')
- grad_up: float32 [2, 32, 1024, 512], P(None, 'grp', 'ctx')
- grad_down: float32 [2, 32, 512, 1024], P(None, 'grp', 'ctx')
The draws below stay inside these ranges and needn't reach their ends.
Inputs may be any that keep to these rules, and one draw needn't show every extreme that they name: `segments`: within each group the ids never fall; the prompt (0) comes first and holds at least half of the group; every id 1 to 4 occurs. `routes`: each token names 8 different experts; among the 128 tokens of one device (aligned blocks) no expert is named more than 42 times.
All inputs are finite; a program needn't handle non-finite values.
Results may differ from the reference program's by a relative error of at most 0.025.
Values may be sent and summed in bfloat16 or wider, within the bound.
A program may use at most 320 MiB of HBM per device.

```python
import math
import jax
import jax.numpy as jnp
import numpy as np
from jax import lax

MODEL_WIDTH = 1024
QUERY_HEADS = 16
KEY_VALUE_HEADS = 8
HEAD_SIZE = 64
E = 32
F = 512
TOP = 8
LAYER_COUNT = 2
NCONT = 4
TOK_MB = 128
GTOK = 1024
GROUPS = 8
CAP = 42


def draw_segments(key, part):
    key_matrix = jax.random.split(key, 2)
    prompt_len = GTOK // 2 + jax.random.randint(key_matrix[0], (GROUPS, 1), 0, GTOK // 4)
    remain = GTOK - prompt_len
    wobble = jax.random.randint(key_matrix[1], (GROUPS, NCONT - 1), -1000, 1001)
    quarter = remain // (4 * NCONT)
    step_ids = jnp.arange(1, NCONT, dtype=jnp.int32)[None, :]
    bounds = prompt_len + step_ids * remain // NCONT + wobble * quarter // 1000
    places = jnp.arange(GTOK, dtype=jnp.int32)[None, :]
    seg_ids = (places >= prompt_len).astype(jnp.int32)
    seg_ids = seg_ids + jnp.sum((places[:, None, :] >= bounds[:, :, None]).astype(jnp.int32), axis=1)
    return seg_ids.astype(jnp.int32)


def shard_levels(rng, dims, pieces, smallest, high):
    gain = 1.0
    for axis_at, shards_of in pieces:
        heights = jax.random.uniform(jax.random.fold_in(jax.random.fold_in(rng, 6), axis_at), (shards_of,), jnp.float32, smallest / len(pieces), high / len(pieces))
        gain = gain * jnp.repeat(jnp.exp(heights), dims[axis_at] // shards_of).reshape((-1,) + (1,) * (len(dims) - 1 - axis_at))
    return gain


def assign_block(own_key, own, number, rows, amount, top, reach, slope):
    order = jax.random.permutation(own_key, amount)
    packed, ordinary = load_shares(amount, rows * top, reach, slope, True), load_shares(amount, rows * top, reach, slope, False)
    places = jnp.arange(amount)

    def named(tallies, turn):
        used = int((tallies > 0).sum())
        fixed = max(1, used // 4)
        moved = fixed + (places - fixed + turn * (used - fixed)) % max(1, amount - fixed)
        return jnp.zeros((amount,), jnp.int32).at[order[jnp.where(places < fixed, places, moved)]].set(jnp.asarray(tallies, jnp.int32))

    tallies = jnp.where(number % 4 == 0, named(packed, number // 4), named(ordinary, number - number // 4 - 1))
    mixed = jax.random.permutation(jax.random.fold_in(own, 3), amount)
    source_of, taker = mixed[0:amount // 2 * 2:2], mixed[1:amount // 2 * 2:2]
    room = jnp.minimum(tallies[source_of] - 1, reach - tallies[taker]) // 2
    room = jnp.where((source_of == order[0]) | (taker == order[0]) | (tallies[taker] == 0), 0, jnp.maximum(room, 0))
    moved = jax.random.randint(jax.random.fold_in(own, 4), (amount // 2,), 0, 1 << 20) % (room + 1)
    tallies = tallies.at[source_of].add(-moved).at[taker].add(moved)
    members = jnp.searchsorted(jnp.cumsum(tallies), jnp.arange(rows * top), side="right").astype(jnp.int32)
    listing = members.reshape(top, rows).T
    listing = listing[jax.random.permutation(jax.random.fold_in(own, 1), rows)]
    turn = jax.random.randint(jax.random.fold_in(own, 2), (rows, 1), 0, top)
    return jnp.take_along_axis(listing, (jnp.arange(top)[None, :] + turn) % top, axis=1)


def load_shares(amount, total, bound, lean, full):
    weights = [(1 << 20) // math.isqrt(grade ** lean) + 1 for grade in range(1, amount + 1)]
    largest = bound if full else min(bound, max(-(-total // amount), total * weights[0] // sum(weights)))
    least = 1 if total - largest >= amount - 1 else 0
    given, rest = [largest] + [least] * (amount - 1), total - largest - least * (amount - 1)
    while rest > 0:
        candidates = [i for i in range(1, amount) if given[i] < largest] or [i for i in range(1, amount) if given[i] < bound]
        mass, budget = sum([weights[i] for i in candidates]), rest
        for i in candidates:
            extra = min(bound - given[i], max(1, budget * weights[i] // mass), rest)
            given[i] = given[i] + extra
            rest = rest - extra
    return np.array(given)


def centred(key, extent, width, limit, shards=(), held_as=jnp.bfloat16):
    entries = jax.random.normal(key, extent, jnp.float32) * width
    if len(shards) > 0:
        entries = shard_levels(key, extent, shards, -0.22, 0.18) * entries
    return jnp.clip(entries, min=-limit, max=limit).astype(held_as)


def setup_inputs(seed: int = 0) -> dict:
    arg_keys = jax.random.split(jax.random.key(seed), 15)
    hidden_in = centred(arg_keys[0], (GROUPS, GTOK, MODEL_WIDTH), 1.0, 6.0, ((0, 4), (1, 8)))
    grad_out = centred(arg_keys[1], (GROUPS, GTOK, MODEL_WIDTH), 1.0, 6.0, ((0, 4), (1, 8)))
    segments = draw_segments(jax.random.fold_in(arg_keys[14], 71), 0)
    routes_keys = jax.random.split(jax.random.fold_in(arg_keys[3], 1), GROUPS * GTOK // TOK_MB)
    routes_turns = jax.random.permutation(jax.random.fold_in(arg_keys[3], 3), GROUPS * GTOK // TOK_MB)
    routes = jax.vmap(lambda own, number: assign_block(jax.random.fold_in(arg_keys[3], 2), own, number, TOK_MB, E, TOP, CAP, 0))(routes_keys, routes_turns).reshape((GROUPS, GTOK, TOP))
    attn_gain = jnp.clip(1.0 + 0.1 * jax.random.normal(arg_keys[4], (LAYER_COUNT, MODEL_WIDTH), jnp.float32), 0.5, 1.5).astype(jnp.bfloat16)
    w_query = centred(arg_keys[5], (LAYER_COUNT, MODEL_WIDTH, QUERY_HEADS * HEAD_SIZE), MODEL_WIDTH ** -0.5, 0.1875, ((1, 32),))
    key_weight = centred(arg_keys[6], (LAYER_COUNT, MODEL_WIDTH, KEY_VALUE_HEADS * HEAD_SIZE), MODEL_WIDTH ** -0.5, 0.1875, ((1, 32),))
    value_weight = centred(arg_keys[7], (LAYER_COUNT, MODEL_WIDTH, KEY_VALUE_HEADS * HEAD_SIZE), MODEL_WIDTH ** -0.5, 0.1875, ((1, 32),))
    w_output = centred(arg_keys[8], (LAYER_COUNT, QUERY_HEADS * HEAD_SIZE, MODEL_WIDTH), (QUERY_HEADS * HEAD_SIZE // 64) ** -0.5, 1.5, ((1, 32),))
    ffn_gain = jnp.clip(1.0 + 0.1 * jax.random.normal(arg_keys[9], (LAYER_COUNT, MODEL_WIDTH), jnp.float32), 0.5, 1.5).astype(jnp.bfloat16)
    w_router = centred(arg_keys[10], (LAYER_COUNT, MODEL_WIDTH, E), (4 * MODEL_WIDTH) ** -0.5, 0.09375, ((1, 32),))
    w_gate = centred(arg_keys[11], (LAYER_COUNT, E, MODEL_WIDTH, F), MODEL_WIDTH ** -0.5, 0.1875, ((1, 4), (2, 8)))
    w_up = centred(arg_keys[12], (LAYER_COUNT, E, MODEL_WIDTH, F), MODEL_WIDTH ** -0.5, 0.1875, ((1, 4), (2, 8)))
    w_down = centred(arg_keys[13], (LAYER_COUNT, E, F, MODEL_WIDTH), (F // 8) ** -0.5, 0.75, ((1, 4), (2, 8)))
    return {"hidden_in": hidden_in, "grad_out": grad_out, "segments": segments, "routes": routes, "attn_gain": attn_gain, "w_query": w_query, "key_weight": key_weight, "value_weight": value_weight, "w_output": w_output, "ffn_gain": ffn_gain, "w_router": w_router, "w_gate": w_gate, "w_up": w_up, "w_down": w_down}


@jax.custom_vjp
def lower_precision(v):
    return lax.optimization_barrier(v.astype(jnp.bfloat16)).astype(jnp.float32)

@jax.custom_vjp
def lower_precision_backward(v):
    return v

def low_keep(v):
    return (lower_precision(v), None)

def low_pass(kept, grad):
    return (grad,)

def back_keep(v):
    return (v, None)

def back_low(kept, grad):
    return (lower_precision(grad),)
lower_precision.defvjp(low_keep, low_pass)
lower_precision_backward.defvjp(back_keep, back_low)
EPSILON = 1e-06
HIGHEST = lax.Precision.HIGHEST

def precise_product(left, right):
    return jnp.dot(left, right, precision=HIGHEST)

def rms_norm(stream, gain_row):
    scale_row = lax.rsqrt(lax.optimization_barrier(jnp.mean(stream * stream, axis=-1, keepdims=True)) + EPSILON)
    return stream * scale_row * gain_row

def positions_of(seg_row):
    length_total = seg_row.shape[0]
    seg_ids = jnp.arange(NCONT + 1, dtype=jnp.int32)
    member = seg_row[:, None] == seg_ids[None, :]
    counts = lax.optimization_barrier(jnp.sum(member.astype(jnp.int32), axis=0, dtype=jnp.int32))
    starts = jnp.cumsum(counts, dtype=jnp.int32) - counts
    own_start = lax.optimization_barrier(jnp.sum(jnp.where(member, starts[None, :], 0), axis=1, dtype=jnp.int32))
    places = jnp.arange(length_total, dtype=jnp.int32)
    return jnp.where(seg_row == 0, places, counts[0] + places - own_start)

def rope_tables(places):
    half_dim = HEAD_SIZE // 2
    freqs = jnp.exp(jnp.arange(half_dim, dtype=jnp.float32) * (-2.0 * math.log(10000.0) / HEAD_SIZE))
    angles = places.astype(jnp.float32)[:, None] * freqs[None, :]
    return (jnp.cos(angles), jnp.sin(angles))

def apply_rotation(value_matrix, cosine_table, sines_lookup):
    half_dim = value_matrix.shape[-1] // 2
    first_half = value_matrix[..., :half_dim]
    second_half = value_matrix[..., half_dim:]
    cos_rows = cosine_table[:, None, :]
    sin_rows = sines_lookup[:, None, :]
    return jnp.concatenate([first_half * cos_rows - second_half * sin_rows, second_half * cos_rows + first_half * sin_rows], axis=-1)

def attention(stream, layer_w, cosine_table, sines_lookup, key_mask):
    gain_row, wq_mat, key_weight_matrix, value_weight_matrix, wo_mat = layer_w
    length_total = stream.shape[0]
    normalized_input = lower_precision(rms_norm(stream, gain_row))
    query_matrix = lower_precision(apply_rotation(lower_precision_backward(precise_product(normalized_input, wq_mat)).reshape(length_total, QUERY_HEADS, HEAD_SIZE), cosine_table, sines_lookup))
    key_matrix = lower_precision(apply_rotation(lower_precision_backward(precise_product(normalized_input, key_weight_matrix)).reshape(length_total, KEY_VALUE_HEADS, HEAD_SIZE), cosine_table, sines_lookup))
    value_matrix = lower_precision(lower_precision_backward(precise_product(normalized_input, value_weight_matrix)).reshape(length_total, KEY_VALUE_HEADS, HEAD_SIZE))
    keys_repeated = jnp.repeat(key_matrix, QUERY_HEADS // KEY_VALUE_HEADS, axis=1)
    values_repeated = jnp.repeat(value_matrix, QUERY_HEADS // KEY_VALUE_HEADS, axis=1)
    raw_scores = lower_precision_backward(jnp.einsum('thd,shd->hts', query_matrix, keys_repeated, precision=HIGHEST))
    scores = jnp.where(key_mask[None, :, :], raw_scores * float(HEAD_SIZE) ** (-0.5), -1e+30)
    probs = lower_precision(jax.nn.softmax(scores, axis=-1))
    mixed = jnp.einsum('hts,shd->thd', probs, values_repeated, precision=HIGHEST).reshape(length_total, QUERY_HEADS * HEAD_SIZE)
    mixed = lower_precision(lower_precision_backward(mixed))
    return lower_precision_backward(precise_product(mixed, wo_mat))

def slot_table(route_rows):
    length_total = route_rows.shape[0]
    block_list = length_total // TOK_MB
    per_block = TOK_MB * TOP
    flat_routes = route_rows.reshape(block_list, per_block)
    one_hot = (flat_routes[:, :, None] == jnp.arange(E, dtype=jnp.int32)[None, None, :]).astype(jnp.int32)
    before = jnp.cumsum(one_hot, axis=1, dtype=jnp.int32) - one_hot
    ranks = lax.optimization_barrier(jnp.sum(one_hot * before, axis=-1, dtype=jnp.int32))
    local_slot = flat_routes * CAP + ranks

    def fill_table(slot_row):
        return jnp.full((E * CAP,), per_block, jnp.int32).at[slot_row].set(jnp.arange(per_block, dtype=jnp.int32))
    return (local_slot, jax.vmap(fill_table)(local_slot))

def experts(stream, layer_w, route_rows):
    gain_row, router_mat, gate_mat, up_mat, down_mat = layer_w
    length_total = stream.shape[0]
    block_list = length_total // TOK_MB
    per_block = TOK_MB * TOP
    normalized_input = lower_precision(rms_norm(stream, gain_row))
    logits = lower_precision_backward(precise_product(normalized_input, router_mat))
    chosen = route_rows[:, :, None] == jnp.arange(E, dtype=jnp.int32)[None, None, :]
    picked = lax.optimization_barrier(jnp.sum(jnp.where(chosen, logits[:, None, :], 0.0), axis=-1))
    gates = jax.nn.softmax(picked, axis=-1)
    local_slot, table = slot_table(route_rows)
    routed = lower_precision_backward(jnp.repeat(normalized_input, TOP, axis=0)).reshape(block_list, per_block, MODEL_WIDTH)
    routed = jnp.concatenate([routed, jnp.zeros((block_list, 1, MODEL_WIDTH), jnp.float32)], axis=1)
    buffers = jax.vmap(lambda rows_block, index_block: rows_block[index_block])(routed, table)
    buffers = buffers.reshape(block_list, E, CAP, MODEL_WIDTH)
    gate_pre = lower_precision_backward(jnp.einsum('becd,edf->becf', buffers, gate_mat, precision=HIGHEST))
    up_pre = lower_precision_backward(jnp.einsum('becd,edf->becf', buffers, up_mat, precision=HIGHEST))
    hidden = lower_precision(jax.nn.silu(gate_pre) * up_pre)
    result = lower_precision(lower_precision_backward(jnp.einsum('becf,efd->becd', hidden, down_mat, precision=HIGHEST)))
    result = result.reshape(block_list, E * CAP, MODEL_WIDTH)
    returned = jax.vmap(lambda rows_block, index_block: rows_block[index_block])(result, local_slot)
    returned = returned.reshape(length_total, TOP, MODEL_WIDTH)
    return jnp.einsum('tj,tjd->td', gates, returned, precision=HIGHEST)

def group_forward(weights, stream, seg_row, route_rows):
    length_total = stream.shape[0]
    cosine_table, sines_lookup = rope_tables(positions_of(seg_row))
    places = jnp.arange(length_total, dtype=jnp.int32)
    key_mask = (places[None, :] <= places[:, None]) & ((seg_row[None, :] == 0) | (seg_row[None, :] == seg_row[:, None]))
    for layer_index in range(LAYER_COUNT):
        attn_w = (weights[0][layer_index], weights[1][layer_index], weights[2][layer_index], weights[3][layer_index], weights[4][layer_index])
        stream = stream + attention(stream, attn_w, cosine_table, sines_lookup, key_mask)
        ffn_w = (weights[5][layer_index], weights[6][layer_index], weights[7][layer_index], weights[8][layer_index], weights[9][layer_index])
        stream = stream + experts(stream, ffn_w, route_rows)
    return stream

def forward(weights, stream, segments, routes):

    def one_group(items):
        return jax.checkpoint(group_forward)(weights, items[0], items[1], items[2])
    return lax.map(one_group, (stream, segments, routes))

def reference(hidden_in, grad_out, segments, routes, attn_gain, w_query, key_weight, value_weight, w_output, ffn_gain, w_router, w_gate, w_up, w_down):
    weights = tuple((item.astype(jnp.float32) for item in (attn_gain, w_query, key_weight, value_weight, w_output, ffn_gain, w_router, w_gate, w_up, w_down)))

    def run_all(weight_set, stream):
        return forward(weight_set, stream, segments, routes)
    result, pullback = jax.vjp(run_all, weights, hidden_in.astype(jnp.float32))
    grad_weights, grad_stream = pullback(grad_out.astype(jnp.float32))
    return (result.astype(jnp.bfloat16), grad_stream, grad_weights[0], grad_weights[1], grad_weights[2], grad_weights[3], grad_weights[4], grad_weights[5], grad_weights[6], grad_weights[7], grad_weights[8], grad_weights[9])
```

```python
import functools
import math

import jax
import jax.numpy as jnp
from jax import lax
from jax.experimental import pallas as pl
from jax.experimental.pallas import tpu as pltpu
from jax.sharding import Mesh, PartitionSpec as P

D = 1024
QUERY_HEADS = 16
KEY_VALUE_HEADS = 8
HS = 64
E = 32
F = 512
TOP = 8
LAYERS = 2
CAP = 42
SLOTS = 48
EPSILON = 1e-06
SCALE = float(HS) ** (-0.5)
QB = 256
BF = jnp.bfloat16
F32 = jnp.float32
MESH = pl.DeviceIdType.MESH
VMEM_BYTES = 60 * 1024 * 1024


def dot(a, b, ca=1, cb=0):
    return lax.dot_general(a, b, (((ca,), (cb,)), ((), ())), preferred_element_type=F32)


def call(kernel, outs, args, flops, in_specs=None, out_specs=None, grid=None, scratch=()):
    nbytes = sum(a.size * a.dtype.itemsize for a in args)
    nbytes += sum(math.prod(o.shape) * jnp.dtype(o.dtype).itemsize for o in outs)
    kw = {} if grid is None else {"grid": grid}
    if in_specs is not None:
        kw["in_specs"] = in_specs
    if out_specs is not None:
        kw["out_specs"] = out_specs
    return pl.pallas_call(
        kernel,
        out_shape=tuple(outs),
        scratch_shapes=list(scratch),
        compiler_params=pltpu.CompilerParams(vmem_limit_bytes=VMEM_BYTES),
        cost_estimate=pl.CostEstimate(
            flops=int(flops), bytes_accessed=int(nbytes), transcendentals=0
        ),
        **kw,
    )(*args)


def sds(shape, dtype):
    return jax.ShapeDtypeStruct(tuple(shape), dtype)


def full(shape):
    n = len(shape)
    return pl.BlockSpec(tuple(shape), lambda *_: (0,) * n)


def exchange(ops, cid, grp_size):
    n = grp_size * 2
    count = len(ops)
    modes = [mode for _, mode in ops]

    def kernel(*refs):
        ins = refs[:count]
        outs = refs[count : 2 * count]
        send, recv, local = refs[2 * count :]
        me = lax.axis_index("grp") * 2 + lax.axis_index("zp")
        barrier = pltpu.get_barrier_semaphore()

        def where(k):
            peer = lax.rem(me + k, n)
            return peer, {"grp": peer // 2, "zp": lax.rem(peer, 2)}

        for k in range(1, n):
            _, place = where(k)
            pl.semaphore_signal(barrier, inc=1, device_id=place, device_id_type=MESH)
        pl.semaphore_wait(barrier, n - 1)
        copies = []
        for k in range(1, n):
            peer, place = where(k)
            for i in range(count):
                src = ins[i] if modes[i] == "gather" else ins[i].at[peer]
                copy = pltpu.make_async_remote_copy(
                    src_ref=src,
                    dst_ref=outs[i].at[me],
                    send_sem=send.at[i, k],
                    recv_sem=recv.at[i, k],
                    device_id=place,
                    device_id_type=MESH,
                )
                copy.start()
                copies.append(copy)
        own = []
        for i in range(count):
            src = ins[i] if modes[i] == "gather" else ins[i].at[me]
            copy = pltpu.make_async_copy(src, outs[i].at[me], local.at[i])
            copy.start()
            own.append(copy)
        for copy in own:
            copy.wait()
        for copy in copies:
            copy.wait()

    shapes = []
    total = 0
    for x, mode in ops:
        shape = (n,) + x.shape if mode == "gather" else x.shape
        shapes.append(sds(shape, x.dtype))
        total += math.prod(shape) * x.dtype.itemsize
    any_spec = pl.BlockSpec(memory_space=pl.ANY)
    return pl.pallas_call(
        kernel,
        out_shape=tuple(shapes),
        in_specs=[any_spec] * count,
        out_specs=tuple([any_spec] * count),
        scratch_shapes=[
            pltpu.SemaphoreType.DMA((count, n)),
            pltpu.SemaphoreType.DMA((count, n)),
            pltpu.SemaphoreType.DMA((count,)),
        ],
        compiler_params=pltpu.CompilerParams(collective_id=cid, has_side_effects=True),
        cost_estimate=pl.CostEstimate(
            flops=0, bytes_accessed=40 * int(total), transcendentals=0
        ),
    )(*[x for x, _ in ops])


def swap_halves(x):
    lane = lax.broadcasted_iota(jnp.int32, x.shape, 1)
    width = x.shape[1]
    up = pltpu.roll(x, width - HS // 2, 1)
    down = pltpu.roll(x, HS // 2, 1)
    return jnp.where((lane & (HS - 1)) < HS // 2, up, down)


def inv_rms_of(x):
    return lax.rsqrt(jnp.mean(x * x, axis=-1, keepdims=True) + EPSILON)


def qkv_forward(stream_parts, packed, cos_t, sin_t, ctx):
    first = len(stream_parts) == 1
    rows = stream_parts[0].shape[0]
    width = 256 * ctx
    tail = (width + D) // 128

    def kernel(*refs):
        if first:
            h_ref, w_ref, t_ref, c_ref, s_ref, out_ref, gains_ref = refs
            x = h_ref[...].astype(F32)
        else:
            h_ref, p_ref, w_ref, t_ref, c_ref, s_ref, out_ref, gains_ref, x_ref = refs
            x = h_ref[...]
            for j in range(p_ref.shape[0]):
                x = x + p_ref[j].astype(F32)
            x_ref[...] = x
        gains = jnp.transpose(t_ref[...].astype(F32))[32:40]
        gains_ref[...] = gains
        normed = (x * inv_rms_of(x) * gains[0:1]).astype(BF)
        cos_v = c_ref[...]
        sin_v = s_ref[...]
        for i in range(ctx):
            y = dot(normed, w_ref[:, 256 * i : 256 * (i + 1)])
            out_ref[i] = (y * cos_v + swap_halves(y) * sin_v).astype(BF)

    args = list(stream_parts) + [packed, packed, cos_t, sin_t]
    in_specs = [full(a.shape) for a in stream_parts] + [
        pl.BlockSpec((D, width), lambda i: (0, 0)),
        pl.BlockSpec((D, 128), lambda i: (0, tail)),
        full(cos_t.shape),
        full(sin_t.shape),
    ]
    outs = [sds((ctx, rows, 256), BF), sds((8, D), F32)]
    if not first:
        outs.append(sds((rows, D), F32))
    return call(
        kernel,
        outs,
        args,
        2 * rows * D * width,
        in_specs=in_specs,
        out_specs=tuple(full(o.shape) for o in outs),
        grid=(1,),
    )


def block_mask(seg_row, seg_col, qb, length):
    keys = (qb + 1) * QB
    qi = lax.broadcasted_iota(jnp.int32, (QB, keys), 0) + qb * QB
    ki = lax.broadcasted_iota(jnp.int32, (QB, keys), 1)
    sr = seg_row[:, :keys]
    return (ki <= qi) & ((sr == 0) | (sr == seg_col))


def attention_forward(x, seg_row, seg_col, ctx, hq, tok):
    micro = x.shape[1] // tok
    length = ctx * tok
    per = QB // tok

    def kernel(x_ref, sr_ref, sc_ref, o_ref, l_ref):
        xs = x_ref[...].reshape(length, 256)
        ks = xs[:, 128:192]
        vs = xs[:, 192:256]
        for qb in range(length // QB):
            keys = (qb + 1) * QB
            rows = slice(qb * QB, (qb + 1) * QB)
            mask = block_mask(sr_ref[0], sc_ref[0, rows, :], qb, length)
            outs = []
            lses = []
            for h in range(hq):
                q = xs[rows, HS * h : HS * (h + 1)]
                s = jnp.where(mask, dot(q, ks[:keys], 1, 1) * SCALE, -1e30)
                top = jnp.max(s, axis=-1, keepdims=True)
                p = jnp.exp(s - top)
                total = jnp.sum(p, axis=-1, keepdims=True)
                o = dot(p.astype(BF), vs[:keys]) / total
                outs.append(o)
                lses.append(jnp.broadcast_to(top + jnp.log(total), (QB, HS)))
            for _ in range(hq, 2):
                outs.append(jnp.zeros((QB, HS), F32))
                lses.append(jnp.zeros((QB, HS), F32))
            o_ref[qb * per : (qb + 1) * per] = (
                jnp.concatenate(outs, axis=1).astype(BF).reshape(per, tok, 128)
            )
            l_ref[0, rows, :] = jnp.concatenate(lses, axis=1)

    return call(
        kernel,
        [sds((ctx, micro * tok, 128), BF), sds((micro, length, 128), F32)],
        [x, seg_row, seg_col],
        2 * micro * hq * length * length * HS,
        in_specs=[
            pl.BlockSpec((ctx, tok, 256), lambda m: (0, m, 0)),
            pl.BlockSpec((1, 1, length), lambda m: (m, 0, 0)),
            pl.BlockSpec((1, length, 1), lambda m: (m, 0, 0)),
        ],
        out_specs=(
            pl.BlockSpec((ctx, tok, 128), lambda m: (0, m, 0)),
            pl.BlockSpec((1, length, 128), lambda m: (m, 0, 0)),
        ),
        grid=(micro,),
    )


def attention_backward(x, d_out, out, lse, seg_row, seg_col, ctx, hq, tok):
    micro = x.shape[1] // tok
    length = ctx * tok
    per = QB // tok

    def kernel(x_ref, d_ref, o_ref, l_ref, sr_ref, sc_ref, dx_ref, dk_ref, dv_ref):
        xs = x_ref[...].reshape(length, 256)
        ks = xs[:, 128:192]
        vs = xs[:, 192:256]
        ds_all = d_ref[...].reshape(length, 128)
        os_all = o_ref[...].reshape(length, 128)
        dk_ref[...] = jnp.zeros((length, HS), F32)
        dv_ref[...] = jnp.zeros((length, HS), F32)
        for qb in range(length // QB):
            keys = (qb + 1) * QB
            rows = slice(qb * QB, (qb + 1) * QB)
            mask = block_mask(sr_ref[0], sc_ref[0, rows, :], qb, length)
            dqs = []
            for h in range(hq):
                cols = slice(HS * h, HS * (h + 1))
                q = xs[rows, cols]
                do = ds_all[rows, cols]
                delta = jnp.sum(
                    do.astype(F32) * os_all[rows, cols].astype(F32), axis=-1, keepdims=True
                )
                s = dot(q, ks[:keys], 1, 1) * SCALE - l_ref[0, rows, HS * h : HS * h + 1]
                p = jnp.exp(jnp.where(mask, s, -1e30))
                dp = dot(do, vs[:keys], 1, 1)
                ds = (p * (dp - delta) * SCALE).astype(BF)
                dqs.append(dot(ds, ks[:keys]))
                dk_ref[:keys] += dot(ds, q, 0, 0)
                dv_ref[:keys] += dot(p.astype(BF), do, 0, 0)
            for _ in range(hq, 2):
                dqs.append(jnp.zeros((QB, HS), F32))
            dx_ref[qb * per : (qb + 1) * per, :, 0:128] = (
                jnp.concatenate(dqs, axis=1).astype(BF).reshape(per, tok, 128)
            )
        dx_ref[:, :, 128:256] = (
            jnp.concatenate([dk_ref[...], dv_ref[...]], axis=1)
            .astype(BF)
            .reshape(ctx, tok, 128)
        )

    return call(
        kernel,
        [sds((ctx, micro * tok, 256), BF)],
        [x, d_out, out, lse, seg_row, seg_col],
        5 * micro * hq * length * length * HS,
        in_specs=[
            pl.BlockSpec((ctx, tok, 256), lambda m: (0, m, 0)),
            pl.BlockSpec((ctx, tok, 128), lambda m: (0, m, 0)),
            pl.BlockSpec((ctx, tok, 128), lambda m: (0, m, 0)),
            pl.BlockSpec((1, length, 128), lambda m: (m, 0, 0)),
            pl.BlockSpec((1, 1, length), lambda m: (m, 0, 0)),
            pl.BlockSpec((1, length, 1), lambda m: (m, 0, 0)),
        ],
        out_specs=(pl.BlockSpec((ctx, tok, 256), lambda m: (0, m, 0)),),
        grid=(micro,),
        scratch=[pltpu.VMEM((length, HS), F32), pltpu.VMEM((length, HS), F32)],
    )[0]


def side_by_side(m_ref, ctx, hq):
    return jnp.concatenate([m_ref[i][:, : HS * hq] for i in range(ctx)], axis=1)


def output_forward(mixed, stream, packed, gains, chosen, ctx, hq, n, held):
    rows = stream.shape[0]
    at = 256 * ctx // D
    tail = (256 * ctx + D) // 128

    def kernel(m_ref, x_ref, w_ref, t_ref, g_ref, c_ref, s_ref, n_ref, gate_ref):
        x = x_ref[...].astype(F32) + dot(side_by_side(m_ref, ctx, hq), w_ref[...])
        s_ref[...] = x
        normed = (x * inv_rms_of(x) * g_ref[1:2]).astype(BF)
        n_ref[...] = normed
        logits = dot(t_ref[...], normed, 0, 1)[:E]
        named = c_ref[...] > 0.0
        logits = jnp.where(named, logits, -1e30)
        top = jnp.max(logits, axis=0, keepdims=True)
        p = jnp.where(named, jnp.exp(logits - top), 0.0)
        gates = p / jnp.sum(p, axis=0, keepdims=True)
        gate_ref[...] = jnp.zeros(gate_ref.shape, F32)
        for j in range(n):
            gate_ref[j, 0:held, :] = gates[held * j : held * (j + 1)]

    outs = [sds((rows, D), F32), sds((rows, D), BF), sds((n, 8, rows), F32)]
    return call(
        kernel,
        outs,
        [mixed, stream, packed, packed, gains, chosen],
        2 * rows * D * D,
        in_specs=[
            full(mixed.shape),
            full(stream.shape),
            pl.BlockSpec((D, D), lambda i: (0, at)),
            pl.BlockSpec((D, 128), lambda i: (0, tail)),
            full(gains.shape),
            full(chosen.shape),
        ],
        out_specs=tuple(full(o.shape) for o in outs),
        grid=(1,),
    )


def norm_back(x, gain, d_normed):
    r = inv_rms_of(x)
    grad_gain = jnp.sum(d_normed * x * r, axis=0, keepdims=True)
    q = d_normed * gain
    dx = r * q - x * (r * r * r) * jnp.mean(x * q, axis=-1, keepdims=True)
    return dx, grad_gain


def output_backward(parts, d_gates, gates, g, stream, normed, mixed, packed, gains, extra, ctx, hq, n, held):
    rows = stream.shape[0]
    at = 256 * ctx // D
    tail = (256 * ctx + D) // 128

    def kernel(p_ref, dg_ref, gt_ref, g_ref, x_ref, nm_ref, m_ref, w_ref, t_ref, gain_ref, ex_ref, g1_ref, dm_ref, gw_ref):
        gates_v = jnp.concatenate([gt_ref[j, 0:held, :] for j in range(n)], axis=0)
        dgate_v = jnp.concatenate([dg_ref[j, 0:held, :] for j in range(n)], axis=0)
        mean = jnp.sum(gates_v * dgate_v, axis=0, keepdims=True)
        d_logits = (gates_v * (dgate_v - mean)).astype(BF)
        d_logits = jnp.concatenate([d_logits, jnp.zeros((128 - E, rows), BF)], axis=0)
        router = t_ref[...]
        d_normed = dot(d_logits, router, 0, 1)
        for j in range(n):
            d_normed = d_normed + p_ref[j].astype(F32)
        x = x_ref[...]
        dx, grad_gain = norm_back(x, gain_ref[1:2], d_normed)
        g1 = g_ref[...].astype(F32) + dx
        g1_ref[...] = g1
        low = g1.astype(BF)
        dm = dot(low, w_ref[...], 1, 1).astype(BF)
        for i in range(ctx):
            part = dm[:, HS * hq * i : HS * hq * (i + 1)]
            if hq < 2:
                part = jnp.concatenate([part, jnp.zeros((rows, 128 - HS * hq), BF)], axis=1)
            dm_ref[i] = part
        gw_ref[:, 0:D] = dot(side_by_side(m_ref, ctx, hq), low, 0, 0).astype(BF)
        grad_router = dot(nm_ref[...], d_logits, 0, 1)
        row = lax.broadcasted_iota(jnp.int32, (128, D), 0)
        cols = jnp.where(row == 33, jnp.broadcast_to(grad_gain, (128, D)), 0.0)
        cols = jnp.where(row == 32, jnp.broadcast_to(ex_ref[0:1, :], (128, D)), cols)
        gw_ref[:, D : D + 128] = (grad_router + jnp.transpose(cols)).astype(BF)

    outs = [sds((rows, D), F32), sds((ctx, rows, 128), BF), sds((D, D + 128), BF)]
    args = [parts, d_gates, gates, g, stream, normed, mixed, packed, packed, gains, extra]
    in_specs = [full(a.shape) for a in args]
    in_specs[7] = pl.BlockSpec((D, D), lambda i: (0, at))
    in_specs[8] = pl.BlockSpec((D, 128), lambda i: (0, tail))
    return call(
        kernel,
        outs,
        args,
        4 * rows * D * D,
        in_specs=in_specs,
        out_specs=tuple(full(o.shape) for o in outs),
        grid=(1,),
    )


def qkv_backward(dx, g1, stream, packed, gains, cos_t, sin_t, ctx):
    rows = g1.shape[0]
    width = 256 * ctx

    def kernel(d_ref, g_ref, x_ref, w_ref, gain_ref, c_ref, s_ref, out_ref, gain_out, gw_ref):
        x = x_ref[...].astype(F32)
        gain = gain_ref[0:1]
        normed = (x * inv_rms_of(x) * gain).astype(BF)
        cos_v = c_ref[...]
        sin_v = s_ref[...]
        d_normed = jnp.zeros((rows, D), F32)
        for i in range(ctx):
            y = d_ref[i].astype(F32)
            lin = (y * cos_v - swap_halves(y) * sin_v).astype(BF)
            cols = slice(256 * i, 256 * (i + 1))
            d_normed = d_normed + dot(lin, w_ref[:, cols], 1, 1)
            gw_ref[:, cols] = dot(normed, lin, 0, 0).astype(BF)
        back, grad_gain = norm_back(x, gain, d_normed)
        out_ref[...] = g_ref[...] + back
        gain_out[...] = jnp.broadcast_to(grad_gain, (8, D))

    outs = [sds((rows, D), F32), sds((8, D), F32), sds((D, width), BF)]
    args = [dx, g1, stream, packed, gains, cos_t, sin_t]
    in_specs = [full(a.shape) for a in args]
    in_specs[3] = pl.BlockSpec((D, width), lambda i: (0, 0))
    return call(
        kernel,
        outs,
        args,
        4 * rows * D * width,
        in_specs=in_specs,
        out_specs=tuple(full(o.shape) for o in outs),
        grid=(1,),
    )


def pick_matrix(slot_row, rows):
    at = lax.broadcasted_iota(jnp.int32, (2 * SLOTS, rows), 0)
    return at == slot_row


def weight_specs(half, ctx, buffers=2):
    def own(e):
        return (0, jnp.minimum(e, half - 1), 0, 0)

    def other(e):
        return (0, jnp.maximum(e - half, 0), 0, 0)

    wide = (ctx, 1, D // ctx, F)
    tall = (ctx, 1, F // ctx, D)
    kinds = [(wide, own), (wide, other)] * 2 + [(tall, own), (tall, other)]
    return [
        pl.BlockSpec(shape, index, pipeline_mode=pl.Buffered(buffers))
        for shape, index in kinds
    ]


def pick_weights(e, half, refs, shape):
    own, other = refs
    return jnp.where(e < half, own[...], other[...]).reshape(shape)


def experts_forward(x, gates, slots, core, weights, ctx, held):
    n, rows, _ = x.shape
    half = held // 2
    lanes = 2 * SLOTS

    def kernel(core_ref, x_ref, g_ref, s_ref, w0, w1, w2, w3, w4, w5, out_ref, acc_ref, row_ref, eo_ref):
        e = pl.program_id(0)
        at = lax.rem(e + core_ref[0] * half, held)
        w_gate = pick_weights(e, half, (w0, w1), (D, F))
        w_up = pick_weights(e, half, (w2, w3), (D, F))
        w_down = pick_weights(e, half, (w4, w5), (F, D))
        for s in range(n):
            pick = pick_matrix(s_ref[s, pl.ds(at, 1), :], rows).astype(BF)
            row_ref[lanes * s : lanes * (s + 1), :] = dot(pick, x_ref[s]).astype(BF)
        rws = row_ref[...]
        ga = dot(rws, w_gate)
        up = dot(rws, w_up)
        hidden = (ga * jax.nn.sigmoid(ga) * up).astype(BF)
        eo_ref[...] = dot(hidden, w_down).astype(BF)
        for s in range(n):
            pick = pick_matrix(s_ref[s, pl.ds(at, 1), :], rows)
            gated = jnp.where(pick, g_ref[s, pl.ds(at, 1), :], 0.0).astype(BF)
            add = dot(gated, eo_ref[lanes * s : lanes * (s + 1), :], 0, 0)

            @pl.when(e == 0)
            def _():
                acc_ref[s] = add.astype(F32)

            @pl.when((e > 0) & (e < held - 1))
            def _():
                acc_ref[s] = (acc_ref[s].astype(F32) + add).astype(F32)

            @pl.when(e == held - 1)
            def _():
                out_ref[s] = (acc_ref[s].astype(F32) + add).astype(BF)

    flops = 2 * held * n * (lanes * D * F * 3 + 2 * lanes * rows * D)
    spec = pl.BlockSpec(memory_space=pltpu.SMEM)
    return call(
        kernel,
        [sds(x.shape, BF)],
        [core, x, gates, slots] + list(weights),
        flops,
        in_specs=[spec, full(x.shape), full(gates.shape), full(slots.shape)]
        + weight_specs(half, ctx),
        out_specs=(full(x.shape),),
        grid=(held,),
        scratch=[
            pltpu.VMEM(x.shape, F32),
            pltpu.VMEM((n * lanes, D), BF),
            pltpu.VMEM((n * lanes, D), BF),
        ],
    )[0]


def experts_backward(x, g, gates, slots, core, weights, ctx, held, with_out):
    n, rows, _ = x.shape
    half = held // 2
    lanes = 2 * SLOTS

    def kernel(core_ref, x_ref, gr_ref, g_ref, s_ref, w0, w1, w2, w3, w4, w5, *rest):
        dx_ref, dg_ref, o0, o1, o2, o3, o4, o5 = rest[:8]
        if with_out:
            out_ref, acc_ref, row_ref, grow_ref = rest[8:]
        else:
            acc_ref, row_ref, grow_ref = rest[8:]
        e = pl.program_id(0)
        at = lax.rem(e + core_ref[0] * half, held)
        w_gate = pick_weights(e, half, (w0, w1), (D, F))
        w_up = pick_weights(e, half, (w2, w3), (D, F))
        w_down = pick_weights(e, half, (w4, w5), (F, D))
        slot_gates = []
        for s in range(n):
            mine = slice(lanes * s, lanes * (s + 1))
            pick = pick_matrix(s_ref[s, pl.ds(at, 1), :], rows)
            low = pick.astype(BF)
            row_ref[mine, :] = dot(low, x_ref[s]).astype(BF)
            grow_ref[mine, :] = dot(low, gr_ref[s]).astype(BF)
            gated = jnp.where(pick, g_ref[s, pl.ds(at, 1), :], 0.0)
            slot_gates.append(jnp.sum(gated, axis=1, keepdims=True))
        gate = jnp.concatenate(slot_gates, axis=0)
        rws = row_ref[...]
        grows = grow_ref[...]
        ga = dot(rws, w_gate)
        up = dot(rws, w_up)
        sig = jax.nn.sigmoid(ga)
        act = ga * sig
        hidden_f = act * up
        hidden = hidden_f.astype(BF)
        dhg = dot(grows, w_down, 1, 1)
        d_gate = jnp.sum(hidden.astype(F32) * dhg, axis=1, keepdims=True)
        dh = dhg * gate
        dga = (dh * up * (sig * (1.0 + ga * (1.0 - sig)))).astype(BF)
        dup = (dh * act).astype(BF)
        if with_out:
            eo = dot(hidden, w_down).astype(BF)
        drow = (dot(dga, w_gate, 1, 1) + dot(dup, w_up, 1, 1)).astype(BF)
        for s in range(n):
            mine = slice(lanes * s, lanes * (s + 1))
            pick = pick_matrix(s_ref[s, pl.ds(at, 1), :], rows)
            dg_ref[s, pl.ds(at, 1), :] = jnp.sum(
                jnp.where(pick, d_gate[mine], 0.0), axis=0, keepdims=True
            )
            todo = [(acc_ref, dx_ref, dot(pick.astype(BF), drow[mine], 0, 0))]
            if with_out:
                gated = jnp.where(pick, g_ref[s, pl.ds(at, 1), :], 0.0).astype(BF)
                todo.append((out_ref, out_ref, dot(gated, eo[mine], 0, 0)))
            for held_ref, final_ref, add in todo:

                @pl.when(e == 0)
                def _():
                    held_ref[s] = add.astype(held_ref.dtype)

                @pl.when((e > 0) & (e < held - 1))
                def _():
                    held_ref[s] = (held_ref[s].astype(F32) + add).astype(held_ref.dtype)

                @pl.when(e == held - 1)
                def _():
                    final_ref[s] = (held_ref[s].astype(F32) + add).astype(BF)

        dslot = (grows.astype(F32) * gate).astype(BF)
        g_gate = dot(rws, dga, 0, 0).astype(BF).reshape(ctx, 1, D // ctx, F)
        g_up = dot(rws, dup, 0, 0).astype(BF).reshape(ctx, 1, D // ctx, F)
        g_down = dot(hidden, dslot, 0, 0).astype(BF).reshape(ctx, 1, F // ctx, D)

        @pl.when(e < half)
        def _():
            o0[...] = g_gate
            o2[...] = g_up
            o4[...] = g_down

        @pl.when(e >= half)
        def _():
            o1[...] = g_gate
            o3[...] = g_up
            o5[...] = g_down

    wide = sds((ctx, half, D // ctx, F), BF)
    tall = sds((ctx, half, F // ctx, D), BF)
    outs = [sds(x.shape, BF), sds(gates.shape, F32), wide, wide, wide, wide, tall, tall]
    out_specs = [full(x.shape), full(gates.shape)] + weight_specs(half, ctx, 1)
    scratch = [
        pltpu.VMEM(x.shape, F32),
        pltpu.VMEM((n * lanes, D), BF),
        pltpu.VMEM((n * lanes, D), BF),
    ]
    if with_out:
        outs.append(sds(x.shape, BF))
        out_specs.append(full(x.shape))
    flops = 2 * held * n * (lanes * D * F * 9 + 3 * lanes * rows * D)
    spec = pl.BlockSpec(memory_space=pltpu.SMEM)
    return call(
        kernel,
        outs,
        [core, x, g, gates, slots] + list(weights),
        flops,
        in_specs=[spec, full(x.shape), full(g.shape), full(gates.shape), full(slots.shape)]
        + weight_specs(half, ctx),
        out_specs=tuple(out_specs),
        grid=(held,),
        scratch=scratch,
    )


def in_chunks(x, most):
    size = max(1, most // x.shape[1])
    return [slice(i, i + size) for i in range(0, x.shape[0], size)]


def experts_forward_all(x, gates, slots, *rest):
    outs = [
        experts_forward(x[c], gates[c], slots[c], *rest) for c in in_chunks(x, 2048)
    ]
    return outs[0] if len(outs) == 1 else jnp.concatenate(outs)


def experts_backward_all(x, g, gates, slots, *rest):
    outs = [
        experts_backward(x[c], g[c], gates[c], slots[c], *rest) for c in in_chunks(x, 2048)
    ]
    if len(outs) == 1:
        return outs[0]
    joined = []
    for k in range(len(outs[0])):
        parts = [o[k] for o in outs]
        if k in (0, 1, 8):
            joined.append(jnp.concatenate(parts))
        else:
            joined.append(sum(p.astype(F32) for p in parts).astype(BF))
    return joined


def per_device(
    grp_size,
    ctx,
    hidden_in,
    grad_out,
    segments,
    routes,
    attn_gain,
    w_query,
    key_weight,
    value_weight,
    w_output,
    ffn_gain,
    w_router,
    w_gate,
    w_up,
    w_down,
):
    micro, tok, _ = hidden_in.shape
    rows = micro * tok
    length = ctx * tok
    hq = QUERY_HEADS // ctx
    dup = ctx // KEY_VALUE_HEADS
    n = grp_size * 2
    held = E // n
    half = held // 2
    every = ("grp", "zq", "zp", "core")
    line = ("zq", "zp", "core")
    core = lax.axis_index("core")
    core_arr = core.astype(jnp.int32).reshape(1)
    ctx_index = (lax.axis_index("zq") * 2 + lax.axis_index("zp")) * 2 + core
    shard = w_query.shape[1]

    def pack(layer):
        wq = w_query[layer].reshape(shard, ctx, HS * hq)
        if hq < 2:
            wq = jnp.pad(wq, ((0, 0), (0, 0), (0, 128 - HS * hq)))
        wk = jnp.repeat(key_weight[layer].reshape(shard, KEY_VALUE_HEADS, HS), dup, axis=1)
        wv = jnp.repeat(value_weight[layer].reshape(shard, KEY_VALUE_HEADS, HS), dup, axis=1)
        qkv = jnp.concatenate([wq, wk, wv], axis=2).reshape(shard, ctx * 256)
        tail = jnp.concatenate(
            [
                w_router[layer],
                attn_gain[layer][:, None],
                ffn_gain[layer][:, None],
                jnp.zeros((shard, 128 - E - 2), BF),
            ],
            axis=1,
        )
        return jnp.concatenate([qkv, w_output[layer], tail], axis=1)

    packed = [
        lax.all_gather(pack(layer), every, axis=0, tiled=True) for layer in range(LAYERS)
    ]

    def to_holders(w):
        quarter = w.reshape(4, half, w.shape[1], w.shape[2])
        return jnp.tile(quarter, (ctx // 4, 1, 1, 1))

    def swap(x):
        return lax.ppermute(x, "core", [(0, 1), (1, 0)])

    def fetch(layer):
        out = []
        for w in (w_gate[layer], w_up[layer], w_down[layer]):
            own = lax.all_to_all(to_holders(w), line, 0, 0, tiled=True)
            out += [own, swap(own)]
        return out

    weights = [fetch(layer) for layer in range(LAYERS)]

    own_segments = lax.dynamic_slice_in_dim(segments, ctx_index * tok, tok, axis=1)
    prompt = jnp.sum((segments == 0).astype(jnp.int32), axis=1, dtype=jnp.int32)
    before = jnp.sum(
        (segments[:, None, :] < own_segments[:, :, None]).astype(jnp.int32),
        axis=2,
        dtype=jnp.int32,
    )
    places = ctx_index * tok + jnp.arange(tok, dtype=jnp.int32)[None, :]
    places = jnp.where(own_segments == 0, places, prompt[:, None] + places - before)
    places = places.reshape(rows).astype(F32)
    lane = jnp.arange(256, dtype=jnp.int32)
    freqs = jnp.exp(
        (lane % (HS // 2)).astype(F32) * (-2.0 * math.log(10000.0) / HS)
    )
    angles = places[:, None] * freqs[None, :]
    turned = (lane < 192)[None, :]
    sign = jnp.where((lane % HS) < HS // 2, -1.0, 1.0)[None, :]
    cos_t = jnp.where(turned, jnp.cos(angles), 1.0)
    sin_t = jnp.where(turned, jnp.sin(angles) * sign, 0.0)
    seg_row = segments[:, None, :]
    seg_col = segments[:, :, None]

    flat = routes.reshape(rows, TOP)
    ids = jnp.arange(E, dtype=jnp.int32)
    chosen = jnp.any(ids[:, None, None] == flat[None, :, :], axis=2)
    marks = chosen.astype(BF).reshape(E, micro, tok)
    earlier = (
        jnp.arange(tok)[:, None] < jnp.arange(tok)[None, :]
    ).astype(BF)
    rank = jnp.einsum("emt,ts->ems", marks, earlier, preferred_element_type=F32)
    slot = rank.astype(jnp.int32) + SLOTS * jnp.arange(micro, dtype=jnp.int32)[None, :, None]
    slot = jnp.where(chosen, slot.reshape(E, rows), -1)
    slot = jnp.pad(
        slot.reshape(n, held, rows), ((0, 0), (0, 8 - held), (0, 0)), constant_values=-1
    )
    chosen_f = chosen.astype(F32)
    last_g = lax.all_gather(grad_out.reshape(rows, D), ("grp", "zp"), axis=0, tiled=False)
    last_g = last_g.reshape(n, rows, D)

    ids_of = iter(range(1, 100))
    saved = []
    parts = (hidden_in.reshape(rows, D),)
    for layer in range(LAYERS):
        got = qkv_forward(parts, packed[layer], cos_t, sin_t, ctx)
        qkv, gains = got[0], got[1]
        stream = parts[0] if layer == 0 else got[2]
        heads = lax.all_to_all(qkv, line, 0, 0, tiled=True)
        out, lse = attention_forward(heads, seg_row, seg_col, ctx, hq, tok)
        mixed = lax.all_to_all(out, line, 0, 0, tiled=True)
        stream1, normed, gates = output_forward(
            mixed, stream, packed[layer], gains, chosen_f, ctx, hq, n, held
        )
        ops = [(normed, "gather"), (gates, "a2a")]
        if layer == 0:
            ops.append((slot, "a2a"))
        moved = exchange(ops, next(ids_of), grp_size)
        if layer == 0:
            slots_here = moved[2]
        saved.append((stream, heads, out, lse, mixed, stream1, normed, gates, gains, moved[0], moved[1]))
        if layer < LAYERS - 1:
            sent = experts_forward_all(
                moved[0], moved[1], slots_here, core_arr, weights[layer], ctx, held
            )
            parts = (stream1, exchange([(sent, "a2a")], next(ids_of), grp_size)[0])

    g = grad_out.reshape(rows, D)
    extra = jnp.zeros((8, D), F32)
    small = [None] * LAYERS
    wide = [None] * LAYERS
    expert = [None] * LAYERS
    for layer in reversed(range(LAYERS)):
        stream, heads, out, lse, mixed, stream1, normed, gates, gains, xs, gates_here = saved[layer]
        last = layer == LAYERS - 1
        if last:
            gs = last_g
        else:
            gs = exchange([(g.astype(BF), "gather")], next(ids_of), grp_size)[0]
        res = experts_backward_all(
            xs, gs, gates_here, slots_here, core_arr, weights[layer], ctx, held, last
        )
        shards = []
        for own, other in ((res[2], res[3]), (res[4], res[5]), (res[6], res[7])):
            total = (own.astype(F32) + swap(other).astype(F32)).astype(BF)
            shards.append(lax.all_to_all(total, line, 0, 0, tiled=True))
        expert[layer] = shards
        if last:
            final_parts = lax.all_to_all(res[8], ("grp", "zp"), 0, 0, tiled=True)
            hidden_out = (
                stream1 + jnp.sum(final_parts.astype(F32), axis=0)
            ).astype(BF).reshape(micro, tok, D)
        d_parts, d_gates = exchange(
            [(res[0], "a2a"), (res[1], "a2a")], next(ids_of), grp_size
        )
        g1, d_mixed, small[layer] = output_backward(
            d_parts, d_gates, gates, g, stream1, normed, mixed, packed[layer], gains, extra,
            ctx, hq, n, held,
        )
        d_out = lax.all_to_all(d_mixed, line, 0, 0, tiled=True)
        dx = attention_backward(heads, d_out, out, lse, seg_row, seg_col, ctx, hq, tok)
        dx = lax.all_to_all(dx, line, 0, 0, tiled=True)
        g, extra, wide[layer] = qkv_backward(
            dx, g1, stream, packed[layer], gains, cos_t, sin_t, ctx
        )
    small = [lax.psum_scatter(s, every, scatter_dimension=0, tiled=True) for s in small]
    wide = [lax.psum_scatter(s, every, scatter_dimension=0, tiled=True) for s in wide]
    first_gain = lax.psum_scatter(extra[0], every, scatter_dimension=0, tiled=True)

    def unpack(layer):
        w = wide[layer].astype(F32).reshape(shard, ctx, 256)
        gq = w[:, :, : HS * hq].reshape(shard, QUERY_HEADS * HS)
        gk = w[:, :, 128:192].reshape(shard, KEY_VALUE_HEADS, dup, HS).sum(axis=2)
        gv = w[:, :, 192:256].reshape(shard, KEY_VALUE_HEADS, dup, HS).sum(axis=2)
        s = small[layer].astype(F32)
        return (
            gq,
            gk.reshape(shard, KEY_VALUE_HEADS * HS),
            gv.reshape(shard, KEY_VALUE_HEADS * HS),
            s[:, :D],
            s[:, D + 33],
            s[:, D : D + E],
        )

    got = [unpack(layer) for layer in range(LAYERS)]

    def stacked(k):
        return jnp.stack([got[layer][k] for layer in range(LAYERS)])

    gain_grad = jnp.stack(
        [first_gain] + [small[layer][:, D + 32].astype(F32) for layer in range(LAYERS - 1)]
    )

    def owned(k):
        out = []
        for layer in range(LAYERS):
            s = expert[layer][k].astype(F32)
            s = s.reshape((ctx // 4, 4 * half) + s.shape[2:]).sum(axis=0)
            out.append(s)
        return jnp.stack(out)

    return (
        hidden_out,
        g.reshape(micro, tok, D),
        gain_grad,
        stacked(0),
        stacked(1),
        stacked(2),
        stacked(3),
        stacked(4),
        stacked(5),
        owned(0),
        owned(1),
        owned(2),
    )


def solution(mesh):
    grp_size = mesh.shape["grp"]
    ctx = mesh.shape["ctx"]
    fine = Mesh(
        mesh.devices.reshape(grp_size, ctx // 4, 2, 2), ("grp", "zq", "zp", "core")
    )
    line = ("zq", "zp", "core")
    every = ("grp",) + line
    row = P("grp", line, None)
    placed = (
        row,
        row,
        P("grp", None),
        row,
        P(None, every),
        P(None, every, None),
        P(None, every, None),
        P(None, every, None),
        P(None, every, None),
        P(None, every),
        P(None, every, None),
        P(None, "grp", line, None),
        P(None, "grp", line, None),
        P(None, "grp", line, None),
    )
    return jax.shard_map(
        functools.partial(per_device, grp_size, ctx),
        mesh=fine,
        in_specs=placed,
        out_specs=(
            row,
            row,
            P(None, every),
            P(None, every, None),
            P(None, every, None),
            P(None, every, None),
            P(None, every, None),
            P(None, every),
            P(None, every, None),
            P(None, "grp", line, None),
            P(None, "grp", line, None),
            P(None, "grp", line, None),
        ),
        check_vma=False,
    )
```

```python
import functools
import math

import jax
import jax.numpy as jnp
from jax import lax
from jax.experimental import pallas as pl
from jax.experimental.pallas import tpu as pltpu
from jax.sharding import Mesh, PartitionSpec as P

D = 1024
QUERY_HEADS = 16
KEY_VALUE_HEADS = 8
HS = 64
E = 32
F = 512
TOP = 8
LAYERS = 2
CAP = 42
SLOTS = 48
EPSILON = 1e-06
SCALE = float(HS) ** (-0.5)
QB = 256
BF = jnp.bfloat16
F32 = jnp.float32
MESH = pl.DeviceIdType.MESH
VMEM_BYTES = 58 * 1024 * 1024


def dot(a, b, ca=1, cb=0):
    return lax.dot_general(a, b, (((ca,), (cb,)), ((), ())), preferred_element_type=F32)


def call(kernel, outs, args, flops, in_specs=None, out_specs=None, grid=None, scratch=()):
    nbytes = sum(a.size * a.dtype.itemsize for a in args)
    nbytes += sum(math.prod(o.shape) * jnp.dtype(o.dtype).itemsize for o in outs)
    kw = {} if grid is None else {"grid": grid}
    if in_specs is not None:
        kw["in_specs"] = in_specs
    if out_specs is not None:
        kw["out_specs"] = out_specs
    return pl.pallas_call(
        kernel,
        out_shape=tuple(outs),
        scratch_shapes=list(scratch),
        compiler_params=pltpu.CompilerParams(vmem_limit_bytes=VMEM_BYTES),
        cost_estimate=pl.CostEstimate(
            flops=int(flops), bytes_accessed=int(nbytes), transcendentals=0
        ),
        **kw,
    )(*args)


def sds(shape, dtype):
    return jax.ShapeDtypeStruct(tuple(shape), dtype)


def full(shape):
    n = len(shape)
    return pl.BlockSpec(tuple(shape), lambda *_: (0,) * n)


def size_of(group, sizes):
    grp_size, ctx, planes = sizes
    return {"g": grp_size, "tok": planes, "line": ctx, "z": ctx // 2, "sib": 2}[group]


def place_in(group, sizes):
    planes = sizes[2]
    n = size_of(group, sizes)
    zp = lax.axis_index("zp")
    zz = lax.axis_index("zq") * planes + zp
    core = lax.axis_index("core")
    if group == "g":
        return n, lax.axis_index("grp"), lambda p: {"grp": p}
    if group == "tok":
        return n, zp, lambda p: {"zp": p}
    if group == "line":
        return (
            n,
            zz * 2 + core,
            lambda p: {
                "zq": p // (2 * planes),
                "zp": lax.rem(p // 2, planes),
                "core": lax.rem(p, 2),
            },
        )
    if group == "z":
        return n, zz, lambda p: {"zq": p // planes, "zp": lax.rem(p, planes)}
    return n, core, lambda p: {"core": p}


def transfer(ops, cid, sizes):
    grp_size, ctx, _ = sizes
    groups = []
    for _, group, what in ops:
        for name in ("z", "g", "sib") if what == "packed" else (group,):
            if name not in groups:
                groups.append(name)
    shapes = []
    sems = []
    total_sems = 0
    for x, group, what in ops:
        sems.append(total_sems)
        if what == "packed":
            shapes.append(sds((grp_size, ctx) + x.shape, x.dtype))
            zs = ctx // 2
            total_sems += zs + zs * grp_size * 2
            continue
        n = size_of(group, sizes)
        total_sems += n
        rest = {"all": (n,) + x.shape, "own": x.shape, "pick": (n,) + x.shape[1:]}
        shapes.append(sds(rest[what], x.dtype))
    count = len(ops)

    def kernel(*refs):
        ins = refs[:count]
        outs = refs[count : count + len(shapes)]
        send, recv, local = refs[count + len(shapes) :]
        barrier = pltpu.get_barrier_semaphore()
        total = 0
        for group in groups:
            n, me, where = place_in(group, sizes)
            for k in range(1, n):
                pl.semaphore_signal(
                    barrier, inc=1, device_id=where(lax.rem(me + k, n)), device_id_type=MESH
                )
            total += n - 1
        pl.semaphore_wait(barrier, total)

        def remote(src, dst, at, place):
            copy = pltpu.make_async_remote_copy(
                src_ref=src,
                dst_ref=dst,
                send_sem=send.at[at],
                recv_sem=recv.at[at],
                device_id=place,
                device_id_type=MESH,
            )
            copy.start()
            return copy

        sib_place = {"core": 1 - lax.axis_index("core")}
        sent = []
        todo = []
        own_copies = []

        def start(i):
            _, group, what = ops[i]
            n, me, where = place_in(group or "g", sizes)
            out = outs[i]
            if what == "packed":
                grp = lax.axis_index("grp")
                core = lax.axis_index("core")
                zs, zz, z_place = place_in("z", sizes)
                copy = pltpu.make_async_copy(ins[i], out.at[grp, zz * 2 + core], local.at[i])
                copy.start()
                along = []
                for k in range(1, zs):
                    along.append(
                        remote(
                            ins[i],
                            out.at[grp, zz * 2 + core],
                            sems[i] + k,
                            z_place(lax.rem(zz + k, zs)),
                        )
                    )
                return (i, along, copy)
            copies = []
            for k in range(1, n):
                peer = lax.rem(me + k, n)
                if what == "all":
                    src = ins[i]
                elif what == "own":
                    src = ins[i].at[peer]
                else:
                    src = ins[i].at[lax.rem(peer, ins[i].shape[0])]
                copies.append(remote(src, out.at[me], sems[i] + k, where(peer)))
            if what == "all":
                src = ins[i]
            elif what == "own":
                src = ins[i].at[me]
            else:
                src = ins[i].at[lax.rem(me, ins[i].shape[0])]
            copy = pltpu.make_async_copy(src, out.at[me], local.at[i])
            copy.start()
            own_copies.append(copy)
            sent.extend(copies)
            return None

        def finish_packed(i, along, own):
            grp = lax.axis_index("grp")
            core = lax.axis_index("core")
            zs, zz, _ = place_in("z", sizes)
            out = outs[i]
            base = sems[i] + zs
            over = []

            def spread(j, at):
                for m in range(1, grp_size):
                    over.append(
                        (
                            remote(
                                out.at[at[0], at[1]],
                                out.at[at[0], at[1]],
                                base + j * grp_size + m,
                                {"grp": lax.rem(grp + m, grp_size)},
                            ),
                            j,
                            m,
                        )
                    )

            def to_core(j, m, at):
                sent.append(
                    remote(
                        out.at[at[0], at[1]],
                        out.at[at[0], at[1]],
                        base + zs * grp_size + j * grp_size + m,
                        sib_place,
                    )
                )

            own.wait()
            for j in range(zs):
                if j > 0:
                    along[j - 1].wait_recv()
                at = (grp, lax.rem(zz - j + zs, zs) * 2 + core)
                spread(j, at)
                to_core(j, 0, at)
            for copy, j, m in over:
                copy.wait_recv()
                at = (
                    lax.rem(grp - m + grp_size, grp_size),
                    lax.rem(zz - j + zs, zs) * 2 + core,
                )
                to_core(j, m, at)
            for copy in along:
                copy.wait_send()
            for copy, _, _ in over:
                copy.wait_send()

        pending = []
        for i in range(count):
            got = start(i)
            if got is not None:
                pending.append(got)
        for item in pending:
            finish_packed(*item)
        for copy in own_copies:
            copy.wait()
        for copy in sent:
            copy.wait()

    total = sum(math.prod(o.shape) * jnp.dtype(o.dtype).itemsize for o in shapes)
    any_spec = pl.BlockSpec(memory_space=pl.ANY)
    return pl.pallas_call(
        kernel,
        out_shape=tuple(shapes),
        in_specs=[any_spec] * count,
        out_specs=tuple([any_spec] * len(shapes)),
        scratch_shapes=[
            pltpu.SemaphoreType.DMA((total_sems,)),
            pltpu.SemaphoreType.DMA((total_sems,)),
            pltpu.SemaphoreType.DMA((count,)),
        ],
        compiler_params=pltpu.CompilerParams(collective_id=cid, has_side_effects=True),
        cost_estimate=pl.CostEstimate(
            flops=0, bytes_accessed=40 * int(total), transcendentals=0
        ),
    )(*[x for x, _, _ in ops])


def swap_halves(x):
    lane = lax.broadcasted_iota(jnp.int32, x.shape, 1)
    width = x.shape[1]
    up = pltpu.roll(x, width - HS // 2, 1)
    down = pltpu.roll(x, HS // 2, 1)
    return jnp.where((lane & (HS - 1)) < HS // 2, up, down)


def inv_rms_of(x):
    return lax.rsqrt(jnp.mean(x * x, axis=-1, keepdims=True) + EPSILON)


def qkv_forward(stream_parts, packed, cos_t, sin_t, ctx):
    first = len(stream_parts) == 1
    rows = stream_parts[0].shape[0]
    width = 256 * ctx
    tail = (width + D) // 128

    def kernel(*refs):
        if first:
            h_ref, w_ref, t_ref, c_ref, s_ref, out_ref, gains_ref = refs
            x = h_ref[...].astype(F32)
        else:
            h_ref, p_ref, w_ref, t_ref, c_ref, s_ref, out_ref, gains_ref, x_ref = refs
            x = h_ref[...]
            for j in range(p_ref.shape[0]):
                x = x + p_ref[j].astype(F32)
            x_ref[...] = x
        gains = jnp.transpose(t_ref[...].astype(F32))[32:40]
        gains_ref[...] = gains
        normed = (x * inv_rms_of(x) * gains[0:1]).astype(BF)
        cos_v = c_ref[...]
        sin_v = s_ref[...]
        for i in range(ctx):
            y = dot(normed, w_ref[:, 256 * i : 256 * (i + 1)])
            out_ref[i] = (y * cos_v + swap_halves(y) * sin_v).astype(BF)

    args = list(stream_parts) + [packed, packed, cos_t, sin_t]
    in_specs = [full(a.shape) for a in stream_parts] + [
        pl.BlockSpec((D, width), lambda i: (0, 0)),
        pl.BlockSpec((D, 128), lambda i: (0, tail)),
        full(cos_t.shape),
        full(sin_t.shape),
    ]
    outs = [sds((ctx, rows, 256), BF), sds((8, D), F32)]
    if not first:
        outs.append(sds((rows, D), F32))
    return call(
        kernel,
        outs,
        args,
        2 * rows * D * width,
        in_specs=in_specs,
        out_specs=tuple(full(o.shape) for o in outs),
        grid=(1,),
    )


def block_mask(seg_row, seg_col, qb, length):
    keys = (qb + 1) * QB
    qi = lax.broadcasted_iota(jnp.int32, (QB, keys), 0) + qb * QB
    ki = lax.broadcasted_iota(jnp.int32, (QB, keys), 1)
    sr = seg_row[:, :keys]
    return (ki <= qi) & ((sr == 0) | (sr == seg_col))


def attention_forward(x, seg_row, seg_col, ctx, hq, tok):
    micro = x.shape[1] // tok
    length = ctx * tok
    per = QB // tok

    def kernel(x_ref, sr_ref, sc_ref, o_ref, l_ref):
        xs = x_ref[...].reshape(length, 256)
        ks = xs[:, 128:192]
        vs = xs[:, 192:256]
        for qb in range(length // QB):
            keys = (qb + 1) * QB
            rows = slice(qb * QB, (qb + 1) * QB)
            mask = block_mask(sr_ref[0], sc_ref[0, rows, :], qb, length)
            outs = []
            lses = []
            for h in range(hq):
                q = xs[rows, HS * h : HS * (h + 1)]
                s = jnp.where(mask, dot(q, ks[:keys], 1, 1) * SCALE, -1e30)
                top = jnp.max(s, axis=-1, keepdims=True)
                p = jnp.exp(s - top)
                total = jnp.sum(p, axis=-1, keepdims=True)
                o = dot(p.astype(BF), vs[:keys]) / total
                outs.append(o)
                lses.append(jnp.broadcast_to(top + jnp.log(total), (QB, HS)))
            for _ in range(hq, 2):
                outs.append(jnp.zeros((QB, HS), F32))
                lses.append(jnp.zeros((QB, HS), F32))
            o_ref[qb * per : (qb + 1) * per] = (
                jnp.concatenate(outs, axis=1).astype(BF).reshape(per, tok, 128)
            )
            l_ref[0, rows, :] = jnp.concatenate(lses, axis=1)

    return call(
        kernel,
        [sds((ctx, micro * tok, 128), BF), sds((micro, length, 128), F32)],
        [x, seg_row, seg_col],
        2 * micro * hq * length * length * HS,
        in_specs=[
            pl.BlockSpec((ctx, tok, 256), lambda m: (0, m, 0)),
            pl.BlockSpec((1, 1, length), lambda m: (m, 0, 0)),
            pl.BlockSpec((1, length, 1), lambda m: (m, 0, 0)),
        ],
        out_specs=(
            pl.BlockSpec((ctx, tok, 128), lambda m: (0, m, 0)),
            pl.BlockSpec((1, length, 128), lambda m: (m, 0, 0)),
        ),
        grid=(micro,),
    )


def attention_backward(x, d_out, out, lse, seg_row, seg_col, ctx, hq, tok):
    micro = x.shape[1] // tok
    length = ctx * tok
    per = QB // tok

    def kernel(x_ref, d_ref, o_ref, l_ref, sr_ref, sc_ref, dx_ref, dk_ref, dv_ref):
        xs = x_ref[...].reshape(length, 256)
        ks = xs[:, 128:192]
        vs = xs[:, 192:256]
        ds_all = d_ref[...].reshape(length, 128)
        os_all = o_ref[...].reshape(length, 128)
        dk_ref[...] = jnp.zeros((length, HS), F32)
        dv_ref[...] = jnp.zeros((length, HS), F32)
        for qb in range(length // QB):
            keys = (qb + 1) * QB
            rows = slice(qb * QB, (qb + 1) * QB)
            mask = block_mask(sr_ref[0], sc_ref[0, rows, :], qb, length)
            dqs = []
            for h in range(hq):
                cols = slice(HS * h, HS * (h + 1))
                q = xs[rows, cols]
                do = ds_all[rows, cols]
                delta = jnp.sum(
                    do.astype(F32) * os_all[rows, cols].astype(F32), axis=-1, keepdims=True
                )
                s = dot(q, ks[:keys], 1, 1) * SCALE - l_ref[0, rows, HS * h : HS * h + 1]
                p = jnp.exp(jnp.where(mask, s, -1e30))
                dp = dot(do, vs[:keys], 1, 1)
                ds = (p * (dp - delta) * SCALE).astype(BF)
                dqs.append(dot(ds, ks[:keys]))
                dk_ref[:keys] += dot(ds, q, 0, 0)
                dv_ref[:keys] += dot(p.astype(BF), do, 0, 0)
            for _ in range(hq, 2):
                dqs.append(jnp.zeros((QB, HS), F32))
            dx_ref[qb * per : (qb + 1) * per, :, 0:128] = (
                jnp.concatenate(dqs, axis=1).astype(BF).reshape(per, tok, 128)
            )
        dx_ref[:, :, 128:256] = (
            jnp.concatenate([dk_ref[...], dv_ref[...]], axis=1)
            .astype(BF)
            .reshape(ctx, tok, 128)
        )

    return call(
        kernel,
        [sds((ctx, micro * tok, 256), BF)],
        [x, d_out, out, lse, seg_row, seg_col],
        5 * micro * hq * length * length * HS,
        in_specs=[
            pl.BlockSpec((ctx, tok, 256), lambda m: (0, m, 0)),
            pl.BlockSpec((ctx, tok, 128), lambda m: (0, m, 0)),
            pl.BlockSpec((ctx, tok, 128), lambda m: (0, m, 0)),
            pl.BlockSpec((1, length, 128), lambda m: (m, 0, 0)),
            pl.BlockSpec((1, 1, length), lambda m: (m, 0, 0)),
            pl.BlockSpec((1, length, 1), lambda m: (m, 0, 0)),
        ],
        out_specs=(pl.BlockSpec((ctx, tok, 256), lambda m: (0, m, 0)),),
        grid=(micro,),
        scratch=[pltpu.VMEM((length, HS), F32), pltpu.VMEM((length, HS), F32)],
    )[0]


def side_by_side(m_ref, ctx, hq):
    return jnp.concatenate([m_ref[i][:, : HS * hq] for i in range(ctx)], axis=1)


def output_forward(mixed, stream, packed, gains, chosen, ctx, hq, n, held):
    rows = stream.shape[0]
    at = 256 * ctx // D
    tail = (256 * ctx + D) // 128

    def kernel(m_ref, x_ref, w_ref, t_ref, g_ref, c_ref, s_ref, n_ref, gate_ref):
        x = x_ref[...].astype(F32) + dot(side_by_side(m_ref, ctx, hq), w_ref[...])
        s_ref[...] = x
        normed = (x * inv_rms_of(x) * g_ref[1:2]).astype(BF)
        n_ref[...] = normed
        logits = dot(t_ref[...], normed, 0, 1)[:E]
        named = c_ref[...] > 0.0
        logits = jnp.where(named, logits, -1e30)
        top = jnp.max(logits, axis=0, keepdims=True)
        p = jnp.where(named, jnp.exp(logits - top), 0.0)
        gates = p / jnp.sum(p, axis=0, keepdims=True)
        for j in range(n):
            gate_ref[j] = gates[held * j : held * (j + 1)]

    outs = [sds((rows, D), F32), sds((rows, D), BF), sds((n, held, rows), F32)]
    return call(
        kernel,
        outs,
        [mixed, stream, packed, packed, gains, chosen],
        2 * rows * D * D,
        in_specs=[
            full(mixed.shape),
            full(stream.shape),
            pl.BlockSpec((D, D), lambda i: (0, at)),
            pl.BlockSpec((D, 128), lambda i: (0, tail)),
            full(gains.shape),
            full(chosen.shape),
        ],
        out_specs=tuple(full(o.shape) for o in outs),
        grid=(1,),
    )


def norm_back(x, gain, d_normed):
    r = inv_rms_of(x)
    grad_gain = jnp.sum(d_normed * x * r, axis=0, keepdims=True)
    q = d_normed * gain
    dx = r * q - x * (r * r * r) * jnp.mean(x * q, axis=-1, keepdims=True)
    return dx, grad_gain


def output_backward(parts, d_gates, gates, g, stream, normed, mixed, packed, gains, extra, ctx, hq, n, held):
    rows = stream.shape[0]
    at = 256 * ctx // D
    tail = (256 * ctx + D) // 128

    def kernel(p_ref, dg_ref, gt_ref, g_ref, x_ref, nm_ref, m_ref, w_ref, t_ref, gain_ref, ex_ref, g1_ref, dm_ref, gw_ref):
        gates_v = jnp.concatenate([gt_ref[j] for j in range(n)], axis=0)
        dgate_v = jnp.concatenate([dg_ref[j] for j in range(n)], axis=0)
        mean = jnp.sum(gates_v * dgate_v, axis=0, keepdims=True)
        d_logits = (gates_v * (dgate_v - mean)).astype(BF)
        d_logits = jnp.concatenate([d_logits, jnp.zeros((128 - E, rows), BF)], axis=0)
        router = t_ref[...]
        d_normed = dot(d_logits, router, 0, 1)
        for j in range(n):
            d_normed = d_normed + p_ref[j].astype(F32)
        x = x_ref[...]
        dx, grad_gain = norm_back(x, gain_ref[1:2], d_normed)
        g1 = g_ref[...].astype(F32) + dx
        g1_ref[...] = g1
        low = g1.astype(BF)
        dm = dot(low, w_ref[...], 1, 1).astype(BF)
        for i in range(ctx):
            part = dm[:, HS * hq * i : HS * hq * (i + 1)]
            if hq < 2:
                part = jnp.concatenate([part, jnp.zeros((rows, 128 - HS * hq), BF)], axis=1)
            dm_ref[i] = part
        gw_ref[:, 0:D] = dot(side_by_side(m_ref, ctx, hq), low, 0, 0).astype(BF)
        grad_router = dot(nm_ref[...], d_logits, 0, 1)
        row = lax.broadcasted_iota(jnp.int32, (128, D), 0)
        cols = jnp.where(row == 33, jnp.broadcast_to(grad_gain, (128, D)), 0.0)
        cols = jnp.where(row == 32, jnp.broadcast_to(ex_ref[0:1, :], (128, D)), cols)
        gw_ref[:, D : D + 128] = (grad_router + jnp.transpose(cols)).astype(BF)

    outs = [sds((rows, D), F32), sds((ctx, rows, 128), BF), sds((D, D + 128), BF)]
    args = [parts, d_gates, gates, g, stream, normed, mixed, packed, packed, gains, extra]
    in_specs = [full(a.shape) for a in args]
    in_specs[7] = pl.BlockSpec((D, D), lambda i: (0, at))
    in_specs[8] = pl.BlockSpec((D, 128), lambda i: (0, tail))
    return call(
        kernel,
        outs,
        args,
        4 * rows * D * D,
        in_specs=in_specs,
        out_specs=tuple(full(o.shape) for o in outs),
        grid=(1,),
    )


def qkv_backward(dx, g1, stream, packed, gains, cos_t, sin_t, ctx):
    rows = g1.shape[0]
    width = 256 * ctx

    def kernel(d_ref, g_ref, x_ref, w_ref, gain_ref, c_ref, s_ref, out_ref, gain_out, gw_ref):
        x = x_ref[...].astype(F32)
        gain = gain_ref[0:1]
        normed = (x * inv_rms_of(x) * gain).astype(BF)
        cos_v = c_ref[...]
        sin_v = s_ref[...]
        d_normed = jnp.zeros((rows, D), F32)
        for i in range(ctx):
            y = d_ref[i].astype(F32)
            lin = (y * cos_v - swap_halves(y) * sin_v).astype(BF)
            cols = slice(256 * i, 256 * (i + 1))
            d_normed = d_normed + dot(lin, w_ref[:, cols], 1, 1)
            gw_ref[:, cols] = dot(normed, lin, 0, 0).astype(BF)
        back, grad_gain = norm_back(x, gain, d_normed)
        out_ref[...] = g_ref[...] + back
        gain_out[...] = jnp.broadcast_to(grad_gain, (8, D))

    outs = [sds((rows, D), F32), sds((8, D), F32), sds((D, width), BF)]
    args = [dx, g1, stream, packed, gains, cos_t, sin_t]
    in_specs = [full(a.shape) for a in args]
    in_specs[3] = pl.BlockSpec((D, width), lambda i: (0, 0))
    return call(
        kernel,
        outs,
        args,
        4 * rows * D * width,
        in_specs=in_specs,
        out_specs=tuple(full(o.shape) for o in outs),
        grid=(1,),
    )


def pick_matrix(slot_row, rows):
    at = lax.broadcasted_iota(jnp.int32, (2 * SLOTS, rows), 0)
    return at == slot_row


def weight_specs(buffers):
    return [
        pl.BlockSpec((1,) + shape, lambda e: (e, 0, 0), pipeline_mode=pl.Buffered(buffers))
        for shape in ((D, F), (D, F), (F, D))
    ]


def experts_forward(x, gates, slots, weights, held):
    n, rows, _ = x.shape
    lanes = 2 * SLOTS


    def kernel(x_ref, g_ref, s_ref, w0, w1, w2, out_ref, acc_ref, row_ref, eo_ref):
        e = pl.program_id(0)
        w_gate, w_up, w_down = w0[0], w1[0], w2[0]
        for s in range(n):
            pick = pick_matrix(s_ref[s, pl.ds(e, 1), :], rows).astype(BF)
            row_ref[lanes * s : lanes * (s + 1), :] = dot(pick, x_ref[s]).astype(BF)
        rws = row_ref[...]
        ga = dot(rws, w_gate)
        up = dot(rws, w_up)
        hidden = (ga * jax.nn.sigmoid(ga) * up).astype(BF)
        eo_ref[...] = dot(hidden, w_down).astype(BF)
        for s in range(n):
            pick = pick_matrix(s_ref[s, pl.ds(e, 1), :], rows)
            gated = jnp.where(pick, g_ref[s, pl.ds(e, 1), :], 0.0).astype(BF)
            add = dot(gated, eo_ref[lanes * s : lanes * (s + 1), :], 0, 0)

            @pl.when(e == 0)
            def _():
                acc_ref[s] = add.astype(F32)

            @pl.when((e > 0) & (e < held - 1))
            def _():
                acc_ref[s] = (acc_ref[s].astype(F32) + add).astype(F32)

            @pl.when(e == held - 1)
            def _():
                out_ref[s] = (acc_ref[s].astype(F32) + add).astype(BF)

    flops = 2 * held * n * (lanes * D * F * 3 + 2 * lanes * rows * D)
    return call(
        kernel,
        [sds(x.shape, BF)],
        [x, gates, slots] + list(weights),
        flops,
        in_specs=[full(x.shape), full(gates.shape), full(slots.shape)] + weight_specs(2),
        out_specs=(full(x.shape),),
        grid=(held,),
        scratch=[
            pltpu.VMEM(x.shape, F32),
            pltpu.VMEM((n * lanes, D), BF),
            pltpu.VMEM((n * lanes, D), BF),
        ],
    )[0]


def experts_backward(x, g, gates, slots, weights, held, with_out):
    n, rows, _ = x.shape
    lanes = 2 * SLOTS


    def kernel(x_ref, gr_ref, g_ref, s_ref, w0, w1, w2, *rest):
        dx_ref, dg_ref = rest[:2]
        grad_refs, rest = rest[2:5], rest[5:]
        if with_out:
            out_ref, acc_ref, row_ref, grow_ref = rest
        else:
            acc_ref, row_ref, grow_ref = rest
        e = pl.program_id(0)
        w_gate, w_up, w_down = w0[0], w1[0], w2[0]
        slot_gates = []
        for s in range(n):
            mine = slice(lanes * s, lanes * (s + 1))
            pick = pick_matrix(s_ref[s, pl.ds(e, 1), :], rows)
            low = pick.astype(BF)
            row_ref[mine, :] = dot(low, x_ref[s]).astype(BF)
            grow_ref[mine, :] = dot(low, gr_ref[s]).astype(BF)
            gated = jnp.where(pick, g_ref[s, pl.ds(e, 1), :], 0.0)
            slot_gates.append(jnp.sum(gated, axis=1, keepdims=True))
        gate = jnp.concatenate(slot_gates, axis=0)
        rws = row_ref[...]
        grows = grow_ref[...]
        ga = dot(rws, w_gate)
        up = dot(rws, w_up)
        sig = jax.nn.sigmoid(ga)
        act = ga * sig
        hidden_f = act * up
        hidden = hidden_f.astype(BF)
        dhg = dot(grows, w_down, 1, 1)
        d_gate = jnp.sum(hidden.astype(F32) * dhg, axis=1, keepdims=True)
        dh = dhg * gate
        dga = (dh * up * (sig * (1.0 + ga * (1.0 - sig)))).astype(BF)
        dup = (dh * act).astype(BF)
        if with_out:
            eo = dot(hidden, w_down).astype(BF)
        drow = (dot(dga, w_gate, 1, 1) + dot(dup, w_up, 1, 1)).astype(BF)
        for s in range(n):
            mine = slice(lanes * s, lanes * (s + 1))
            pick = pick_matrix(s_ref[s, pl.ds(e, 1), :], rows)
            dg_ref[s, pl.ds(e, 1), :] = jnp.sum(
                jnp.where(pick, d_gate[mine], 0.0), axis=0, keepdims=True
            )
            todo = [(acc_ref, dx_ref, dot(pick.astype(BF), drow[mine], 0, 0))]
            if with_out:
                gated = jnp.where(pick, g_ref[s, pl.ds(e, 1), :], 0.0).astype(BF)
                todo.append((out_ref, out_ref, dot(gated, eo[mine], 0, 0)))
            for held_ref, final_ref, add in todo:

                @pl.when(e == 0)
                def _():
                    held_ref[s] = add.astype(held_ref.dtype)

                @pl.when((e > 0) & (e < held - 1))
                def _():
                    held_ref[s] = (held_ref[s].astype(F32) + add).astype(held_ref.dtype)

                @pl.when(e == held - 1)
                def _():
                    final_ref[s] = (held_ref[s].astype(F32) + add).astype(BF)

        dslot = (grows.astype(F32) * gate).astype(BF)
        grads = [dot(rws, dga, 0, 0), dot(rws, dup, 0, 0), dot(hidden, dslot, 0, 0)]
        for ref, value in zip(grad_refs, grads):
            ref[0] = value.astype(BF)

    outs = [sds(x.shape, BF), sds(gates.shape, F32)] + [sds(w.shape, BF) for w in weights]
    out_specs = [full(x.shape), full(gates.shape)] + weight_specs(2)
    scratch = [
        pltpu.VMEM(x.shape, F32),
        pltpu.VMEM((n * lanes, D), BF),
        pltpu.VMEM((n * lanes, D), BF),
    ]
    if with_out:
        outs.append(sds(x.shape, BF))
        out_specs.append(full(x.shape))
    flops = 2 * held * n * (lanes * D * F * 9 + 3 * lanes * rows * D)
    return call(
        kernel,
        outs,
        [x, g, gates, slots] + list(weights),
        flops,
        in_specs=[full(x.shape), full(g.shape), full(gates.shape), full(slots.shape)]
        + weight_specs(2),
        out_specs=tuple(out_specs),
        grid=(held,),
        scratch=scratch,
    )


def per_device(
    sizes,
    hidden_in,
    grad_out,
    segments,
    routes,
    attn_gain,
    w_query,
    key_weight,
    value_weight,
    w_output,
    ffn_gain,
    w_router,
    w_gate,
    w_up,
    w_down,
):
    micro, tok, _ = hidden_in.shape
    rows = micro * tok
    grp_size, ctx, planes = sizes
    hq = QUERY_HEADS // ctx
    dup = ctx // KEY_VALUE_HEADS
    held = 2 * grp_size
    every = ("grp", "zq", "zp", "core")
    line = ("zq", "zp", "core")
    core = lax.axis_index("core")
    ctx_index = (lax.axis_index("zq") * planes + lax.axis_index("zp")) * 2 + core
    shard = w_query.shape[1]

    def by_plane(x, axis, back=False):
        dims = (planes, grp_size, 2) if back else (grp_size, planes, 2)
        head, tail = x.shape[:axis], x.shape[axis + 1 :]
        y = jnp.swapaxes(x.reshape(head + dims + tail), axis, axis + 1)
        return y.reshape(x.shape)

    def pack(layer):
        wq = w_query[layer].reshape(shard, ctx, HS * hq)
        if hq < 2:
            wq = jnp.pad(wq, ((0, 0), (0, 0), (0, 128 - HS * hq)))
        wk = jnp.repeat(key_weight[layer].reshape(shard, KEY_VALUE_HEADS, HS), dup, axis=1)
        wv = jnp.repeat(value_weight[layer].reshape(shard, KEY_VALUE_HEADS, HS), dup, axis=1)
        qkv = jnp.concatenate([wq, wk, wv], axis=2).reshape(shard, ctx * 256)
        tail = jnp.concatenate(
            [
                by_plane(w_router[layer], 1),
                attn_gain[layer][:, None],
                ffn_gain[layer][:, None],
                jnp.zeros((shard, 128 - E - 2), BF),
            ],
            axis=1,
        )
        return jnp.concatenate([qkv, w_output[layer], tail], axis=1)

    ids_of = iter(range(1, 100))

    def move(*ops):
        return transfer(ops, next(ids_of), sizes)

    def swap(x):
        return lax.ppermute(x, "core", [(0, 1), (1, 0)])

    def picks(layer, members):
        ws = (w_gate[layer], w_up[layer], w_down[layer])
        return [(ws[k], "line", "pick") for k in members]

    def plane_gather(w):
        w = w.reshape(1, w.shape[0] * w.shape[1], w.shape[2])
        return lax.all_gather(w, ("grp", "core"), axis=0, tiled=True)

    grad_rows = grad_out.reshape(rows, D)
    first, *ready = move((pack(0), None, "packed"), *picks(0, (0, 1, 2)))
    packed = [first.reshape(D, -1), None]
    weights = [[plane_gather(w) for w in ready], []]

    own_segments = lax.dynamic_slice_in_dim(segments, ctx_index * tok, tok, axis=1)
    prompt = jnp.sum((segments == 0).astype(jnp.int32), axis=1, dtype=jnp.int32)
    before = jnp.sum(
        (segments[:, None, :] < own_segments[:, :, None]).astype(jnp.int32),
        axis=2,
        dtype=jnp.int32,
    )
    places = ctx_index * tok + jnp.arange(tok, dtype=jnp.int32)[None, :]
    places = jnp.where(own_segments == 0, places, prompt[:, None] + places - before)
    places = places.reshape(rows).astype(F32)
    lane = jnp.arange(256, dtype=jnp.int32)
    freqs = jnp.exp(
        (lane % (HS // 2)).astype(F32) * (-2.0 * math.log(10000.0) / HS)
    )
    angles = places[:, None] * freqs[None, :]
    turned = (lane < 192)[None, :]
    sign = jnp.where((lane % HS) < HS // 2, -1.0, 1.0)[None, :]
    cos_t = jnp.where(turned, jnp.cos(angles), 1.0)
    sin_t = jnp.where(turned, jnp.sin(angles) * sign, 0.0)
    seg_row = segments[:, None, :]
    seg_col = segments[:, :, None]

    flat = routes.reshape(rows, TOP)
    ids = by_plane(jnp.arange(E, dtype=jnp.int32), 0)
    chosen = jnp.any(ids[:, None, None] == flat[None, :, :], axis=2)
    marks = chosen.astype(BF).reshape(E, micro, tok)
    earlier = (
        jnp.arange(tok)[:, None] < jnp.arange(tok)[None, :]
    ).astype(BF)
    rank = jnp.einsum("emt,ts->ems", marks, earlier, preferred_element_type=F32)
    slot = rank.astype(jnp.int32) + SLOTS * jnp.arange(micro, dtype=jnp.int32)[None, :, None]
    slot = jnp.where(chosen, slot.reshape(E, rows), -1)

    slot = slot.reshape(planes, held, rows)
    chosen_f = chosen.astype(F32)

    last_g = lax.all_gather(grad_rows, "zp", axis=0, tiled=False)

    saved = []
    parts = (hidden_in.reshape(rows, D),)
    for layer in range(LAYERS):
        got = qkv_forward(parts, packed[layer], cos_t, sin_t, ctx)
        qkv, gains = got[0], got[1]
        stream = parts[0] if layer == 0 else got[2]
        heads = lax.all_to_all(qkv, line, 0, 0, tiled=True)
        out, lse = attention_forward(heads, seg_row, seg_col, ctx, hq, tok)
        mixed = lax.all_to_all(out, line, 0, 0, tiled=True)
        stream1, normed, gates = output_forward(
            mixed, stream, packed[layer], gains, chosen_f, ctx, hq, planes, held
        )
        ops = [(normed, "tok", "all"), (gates, "tok", "own")]
        if layer == 0:
            xs, gates_here, slots_here, second, *ready = move(
                *ops, (slot, "tok", "own"), (pack(1), None, "packed"), *picks(1, (0,))
            )
            packed[1] = second.reshape(D, -1)
            weights[1] += [plane_gather(w) for w in ready]
        else:
            xs, gates_here = move(*ops)
        saved.append((stream, heads, out, lse, mixed, stream1, normed, gates, gains, xs, gates_here))
        if layer == 0:
            sent = experts_forward(xs, gates_here, slots_here, weights[0], held)
            came, *ready = move((sent, "tok", "own"), *picks(1, (1, 2)))
            weights[1] += [plane_gather(w) for w in ready]
            parts = (stream1, came)

    def plane_scatter(r):
        r = lax.psum_scatter(r, ("grp", "core"), scatter_dimension=0, tiled=True)
        return r.reshape(ctx, r.shape[1] // ctx, r.shape[2])

    def owned_rows(r):
        r = r.astype(F32).reshape((ctx // (2 * planes), 2 * planes) + r.shape[1:])
        return jnp.sum(r, axis=0)

    g = grad_rows
    extra = jnp.zeros((8, D), F32)
    small = [None] * LAYERS
    wide = [None] * LAYERS
    expert = [None] * LAYERS
    for layer in reversed(range(LAYERS)):
        stream, heads, out, lse, mixed, stream1, normed, gates, gains, xs, gates_here = saved[layer]
        last = layer == LAYERS - 1
        if last:
            gs = last_g
        else:
            gs, last_gate, last_up = move(
                (g.astype(BF), "tok", "all"),
                (expert[1][0], "line", "own"),
                (expert[1][1], "line", "own"),
            )
        res = experts_backward(xs, gs, gates_here, slots_here, weights[layer], held, last)
        expert[layer] = [plane_scatter(r) for r in res[2:5]]
        back = [(res[0], "tok", "own"), (res[1], "tok", "own")]
        if last:
            d_parts, d_gates, final_parts = move(*back, (res[5], "tok", "own"))
            hidden_out = (
                (stream1 + jnp.sum(final_parts.astype(F32), axis=0))
                .astype(BF)
                .reshape(micro, tok, D)
            )
        else:
            d_parts, d_gates, last_down = move(*back, (expert[1][2], "line", "own"))
        g1, d_mixed, small[layer] = output_backward(
            d_parts, d_gates, gates, g, stream1, normed, mixed, packed[layer], gains, extra,
            ctx, hq, planes, held,
        )
        d_out = lax.all_to_all(d_mixed, line, 0, 0, tiled=True)
        dx = attention_backward(heads, d_out, out, lse, seg_row, seg_col, ctx, hq, tok)
        dx = lax.all_to_all(dx, line, 0, 0, tiled=True)
        g, extra, wide[layer] = qkv_backward(
            dx, g1, stream, packed[layer], gains, cos_t, sin_t, ctx
        )
    at_34 = jnp.arange(D + 128) == D + 34
    small[0] = jnp.where(at_34[None, :], extra[0][:, None].astype(BF), small[0])
    joined = [jnp.concatenate([wide[k], small[k]], axis=1) for k in range(LAYERS)]
    last_owned = lax.psum_scatter(joined[1], every, scatter_dimension=0, tiled=True)
    halves = joined[0].reshape(grp_size, ctx // 2, 2, shard, -1)
    theirs = lax.dynamic_index_in_dim(halves, 1 - core, 2, keepdims=False)
    ours = lax.dynamic_index_in_dim(halves, core, 2, keepdims=False)
    chip = (ours.astype(F32) + swap(theirs).astype(F32)).astype(BF)
    plane, first_gate, first_up = move(
        (chip, "g", "own"), (expert[0][0], "line", "own"), (expert[0][1], "line", "own")
    )
    plane = jnp.sum(plane.astype(F32), axis=0).astype(BF)
    column, first_down = move((plane, "z", "own"), (expert[0][2], "line", "own"))
    owned_attn = [jnp.sum(column.astype(F32), axis=0), last_owned.astype(F32)]
    owned_experts = [
        [owned_rows(r) for r in (first_gate, first_up, first_down)],
        [owned_rows(r) for r in (last_gate, last_up, last_down)],
    ]

    def unpack(layer):
        w = owned_attn[layer][:, : 256 * ctx].reshape(shard, ctx, 256)
        gq = w[:, :, : HS * hq].reshape(shard, QUERY_HEADS * HS)
        gk = w[:, :, 128:192].reshape(shard, KEY_VALUE_HEADS, dup, HS).sum(axis=2)
        gv = w[:, :, 192:256].reshape(shard, KEY_VALUE_HEADS, dup, HS).sum(axis=2)
        s = owned_attn[layer][:, 256 * ctx :]
        return (
            gq,
            gk.reshape(shard, KEY_VALUE_HEADS * HS),
            gv.reshape(shard, KEY_VALUE_HEADS * HS),
            s[:, :D],
            s[:, D + 33],
            by_plane(s[:, D : D + E], 1, back=True),
        )

    got = [unpack(layer) for layer in range(LAYERS)]

    def stacked(k):
        return jnp.stack([got[layer][k] for layer in range(LAYERS)])

    gain_grad = jnp.stack(
        [owned_attn[0][:, 256 * ctx + D + 34]]
        + [owned_attn[k][:, 256 * ctx + D + 32] for k in range(LAYERS - 1)]
    )

    def owned(k):
        return jnp.stack([owned_experts[layer][k] for layer in range(LAYERS)])

    return (
        hidden_out,
        g.reshape(micro, tok, D),
        gain_grad,
        stacked(0),
        stacked(1),
        stacked(2),
        stacked(3),
        stacked(4),
        stacked(5),
        owned(0),
        owned(1),
        owned(2),
    )


def solution(mesh):
    grp_size = mesh.shape["grp"]
    ctx = mesh.shape["ctx"]
    planes = E // grp_size // 2
    fine = Mesh(
        mesh.devices.reshape(grp_size, ctx // (2 * planes), planes, 2),
        ("grp", "zq", "zp", "core"),
    )
    line = ("zq", "zp", "core")
    every = ("grp",) + line
    row = P("grp", line, None)
    placed = (
        row,
        row,
        P("grp", None),
        row,
        P(None, every),
        P(None, every, None),
        P(None, every, None),
        P(None, every, None),
        P(None, every, None),
        P(None, every),
        P(None, every, None),
        P(None, "grp", line, None),
        P(None, "grp", line, None),
        P(None, "grp", line, None),
    )
    return jax.shard_map(
        functools.partial(per_device, (grp_size, ctx, planes)),
        mesh=fine,
        in_specs=placed,
        out_specs=(
            row,
            row,
            P(None, every),
            P(None, every, None),
            P(None, every, None),
            P(None, every, None),
            P(None, every, None),
            P(None, every),
            P(None, every, None),
            P(None, "grp", line, None),
            P(None, "grp", line, None),
            P(None, "grp", line, None),
        ),
        check_vma=False,
    )
```

```python
import functools
import math

import jax
import jax.numpy as jnp
from jax import lax
from jax.experimental import pallas as pl
from jax.experimental.pallas import tpu as pltpu
from jax.sharding import Mesh, PartitionSpec as P

D = 1024
QUERY_HEADS = 16
KEY_VALUE_HEADS = 8
HS = 64
E = 32
F = 512
TOP = 8
LAYERS = 2
CAP = 42
SLOTS = 48
EPSILON = 1e-06
SCALE = float(HS) ** (-0.5)
QB = 256
BF = jnp.bfloat16
F32 = jnp.float32
MESH = pl.DeviceIdType.MESH
PIECES = 8
VMEM_BYTES = 58 * 1024 * 1024
TAIL = 3 * D // 128


def dot(a, b, ca=1, cb=0):
    return lax.dot_general(a, b, (((ca,), (cb,)), ((), ())), preferred_element_type=F32)


def call(kernel, outs, args, flops, in_specs=None, out_specs=None, grid=None, scratch=()):
    nbytes = sum(a.size * a.dtype.itemsize for a in args)
    nbytes += sum(math.prod(o.shape) * jnp.dtype(o.dtype).itemsize for o in outs)
    kw = {} if grid is None else {"grid": grid}
    if in_specs is not None:
        kw["in_specs"] = in_specs
    if out_specs is not None:
        kw["out_specs"] = out_specs
    return pl.pallas_call(
        kernel,
        out_shape=tuple(outs),
        scratch_shapes=list(scratch),
        compiler_params=pltpu.CompilerParams(vmem_limit_bytes=VMEM_BYTES),
        cost_estimate=pl.CostEstimate(
            flops=int(flops), bytes_accessed=int(nbytes), transcendentals=0
        ),
        **kw,
    )(*args)


def sds(shape, dtype):
    return jax.ShapeDtypeStruct(tuple(shape), dtype)


def full(shape):
    n = len(shape)
    return pl.BlockSpec(tuple(shape), lambda *_: (0,) * n)


def size_of(group, sizes):
    grp_size, ctx, planes = sizes
    return {"g": grp_size, "tok": planes, "line": ctx, "z": ctx // 2, "sib": 2}[group]


def place_in(group, sizes):
    planes = sizes[2]
    n = size_of(group, sizes)
    zp = lax.axis_index("zp")
    zz = lax.axis_index("zq") * planes + zp
    core = lax.axis_index("core")
    if group == "g":
        return n, lax.axis_index("grp"), lambda p: {"grp": p}
    if group == "tok":
        return n, zp, lambda p: {"zp": p}
    if group == "line":
        return (
            n,
            zz * 2 + core,
            lambda p: {
                "zq": p // (2 * planes),
                "zp": lax.rem(p // 2, planes),
                "core": lax.rem(p, 2),
            },
        )
    if group == "z":
        return n, zz, lambda p: {"zq": p // planes, "zp": lax.rem(p, planes)}
    return n, core, lambda p: {"core": p}


def transfer(ops, cid, sizes):
    grp_size, ctx, _ = sizes
    groups = []
    for _, group, what in ops:
        for name in ("z", "g", "sib") if what == "packed" else (group,):
            if name not in groups:
                groups.append(name)
    shapes = []
    sems = []
    total_sems = 0
    for x, group, what in ops:
        sems.append(total_sems)
        if what == "packed":
            shapes.append(sds((grp_size, ctx) + x.shape, x.dtype))
            zs = ctx // 2
            total_sems += zs + zs * grp_size * 2
            continue
        n = size_of(group, sizes)
        total_sems += PIECES if group == "sib" else n
        rest = x.shape[1:] if group == "sib" else x.shape
        if what != "own":
            rest = (n,) + (x.shape if what == "all" else x.shape[1:])
        shapes.append(sds(rest, x.dtype))
    count = len(ops)

    def kernel(*refs):
        ins = refs[:count]
        outs = refs[count : count + len(shapes)]
        send, recv, local = refs[count + len(shapes) :]
        barrier = pltpu.get_barrier_semaphore()
        total = 0
        for group in groups:
            n, me, where = place_in(group, sizes)
            for k in range(1, n):
                pl.semaphore_signal(
                    barrier, inc=1, device_id=where(lax.rem(me + k, n)), device_id_type=MESH
                )
            total += n - 1
        pl.semaphore_wait(barrier, total)

        def remote(src, dst, at, place):
            copy = pltpu.make_async_remote_copy(
                src_ref=src,
                dst_ref=dst,
                send_sem=send.at[at],
                recv_sem=recv.at[at],
                device_id=place,
                device_id_type=MESH,
            )
            copy.start()
            return copy

        sib_place = {"core": 1 - lax.axis_index("core")}
        sent = []
        own_copies = []

        def start(i):
            _, group, what = ops[i]
            n, me, where = place_in(group or "g", sizes)
            out = outs[i]
            if what == "packed":
                grp = lax.axis_index("grp")
                core = lax.axis_index("core")
                zs, zz, z_place = place_in("z", sizes)
                copy = pltpu.make_async_copy(ins[i], out.at[grp, zz * 2 + core], local.at[i])
                copy.start()
                along = []
                for k in range(1, zs):
                    along.append(
                        remote(
                            ins[i],
                            out.at[grp, zz * 2 + core],
                            sems[i] + k,
                            z_place(lax.rem(zz + k, zs)),
                        )
                    )
                return (i, along, copy)
            if group == "sib":
                size = ins[i].shape[1] // PIECES
                for j in range(PIECES):
                    part = pl.ds(j * size, size)
                    sent.append(
                        remote(ins[i].at[1 - me, part], out.at[part], sems[i] + j, where(1 - me))
                    )
                return None
            copies = []
            for k in range(1, n):
                peer = lax.rem(me + k, n)
                if what == "all":
                    src = ins[i]
                elif what == "own":
                    src = ins[i].at[peer]
                else:
                    src = ins[i].at[lax.rem(peer, ins[i].shape[0])]
                copies.append(remote(src, out.at[me], sems[i] + k, where(peer)))
            if what == "all":
                src = ins[i]
            elif what == "own":
                src = ins[i].at[me]
            else:
                src = ins[i].at[lax.rem(me, ins[i].shape[0])]
            copy = pltpu.make_async_copy(src, out.at[me], local.at[i])
            copy.start()
            own_copies.append(copy)
            sent.extend(copies)
            return None

        def finish_packed(i, along, own):
            grp = lax.axis_index("grp")
            core = lax.axis_index("core")
            zs, zz, _ = place_in("z", sizes)
            out = outs[i]
            base = sems[i] + zs
            over = []

            def spread(j, at):
                for m in range(1, grp_size):
                    over.append(
                        (
                            remote(
                                out.at[at[0], at[1]],
                                out.at[at[0], at[1]],
                                base + j * grp_size + m,
                                {"grp": lax.rem(grp + m, grp_size)},
                            ),
                            j,
                            m,
                        )
                    )

            def to_core(j, m, at):
                sent.append(
                    remote(
                        out.at[at[0], at[1]],
                        out.at[at[0], at[1]],
                        base + zs * grp_size + j * grp_size + m,
                        sib_place,
                    )
                )

            own.wait()
            for j in range(zs):
                if j > 0:
                    along[j - 1].wait_recv()
                at = (grp, lax.rem(zz - j + zs, zs) * 2 + core)
                spread(j, at)
                to_core(j, 0, at)
            for copy, j, m in over:
                copy.wait_recv()
                at = (
                    lax.rem(grp - m + grp_size, grp_size),
                    lax.rem(zz - j + zs, zs) * 2 + core,
                )
                to_core(j, m, at)
            for copy in along:
                copy.wait_send()
            for copy, _, _ in over:
                copy.wait_send()

        pending = []
        for i in range(count):
            got = start(i)
            if got is not None:
                pending.append(got)
        for item in pending:
            finish_packed(*item)
        for copy in own_copies:
            copy.wait()
        for copy in sent:
            copy.wait()

    total = sum(math.prod(o.shape) * jnp.dtype(o.dtype).itemsize for o in shapes)
    any_spec = pl.BlockSpec(memory_space=pl.ANY)
    return pl.pallas_call(
        kernel,
        out_shape=tuple(shapes),
        in_specs=[any_spec] * count,
        out_specs=tuple([any_spec] * len(shapes)),
        scratch_shapes=[
            pltpu.SemaphoreType.DMA((total_sems,)),
            pltpu.SemaphoreType.DMA((total_sems,)),
            pltpu.SemaphoreType.DMA((count,)),
        ],
        compiler_params=pltpu.CompilerParams(collective_id=cid, has_side_effects=True),
        cost_estimate=pl.CostEstimate(
            flops=0, bytes_accessed=40 * int(total), transcendentals=0
        ),
    )(*[x for x, _, _ in ops])


def swap_halves(x):
    lane = lax.broadcasted_iota(jnp.int32, x.shape, 1)
    width = x.shape[1]
    up = pltpu.roll(x, width - HS // 2, 1)
    down = pltpu.roll(x, HS // 2, 1)
    return jnp.where((lane & (HS - 1)) < HS // 2, up, down)


def inv_rms_of(x):
    return lax.rsqrt(jnp.mean(x * x, axis=-1, keepdims=True) + EPSILON)


def in_order(parts):
    return parts[0] if len(parts) == 1 else jnp.concatenate(parts, axis=1)


def qkv_forward(stream_parts, packed, cos_t, sin_t, ctx, hq):
    first = len(stream_parts) == 1
    rows = stream_parts[0].shape[0]
    dup = ctx // KEY_VALUE_HEADS

    def kernel(*refs):
        if first:
            h_ref, w_ref, t_ref, c_ref, s_ref, out_ref, gains_ref = refs
            x = h_ref[...].astype(F32)
        else:
            h_ref, p_ref, w_ref, t_ref, c_ref, s_ref, out_ref, gains_ref, x_ref = refs
            x = h_ref[...]
            for j in range(p_ref.shape[0]):
                x = x + p_ref[j].astype(F32)
            x_ref[...] = x
        gains = jnp.transpose(t_ref[...].astype(F32))[32:40]
        gains_ref[...] = gains
        normed = (x * inv_rms_of(x) * gains[0:1]).astype(BF)
        cos_v = c_ref[...]
        sin_v = s_ref[...]
        parts = []
        for i in range(8):
            y = dot(normed, w_ref[:, 256 * i : 256 * (i + 1)])
            if i < 6:
                y = y * cos_v + swap_halves(y) * sin_v
            parts.append(y.astype(BF))
        queries, keys, values = in_order(parts[:4]), in_order(parts[4:6]), in_order(parts[6:])
        for i in range(ctx):
            mine = [queries[:, HS * hq * i : HS * hq * (i + 1)]]
            if hq < 2:
                mine.append(jnp.zeros((rows, 128 - HS * hq), BF))
            kv = i // dup
            mine.append(keys[:, HS * kv : HS * (kv + 1)])
            mine.append(values[:, HS * kv : HS * (kv + 1)])
            out_ref[i] = in_order(mine)

    args = list(stream_parts) + [packed, packed, cos_t, sin_t]
    in_specs = [full(a.shape) for a in stream_parts] + [
        pl.BlockSpec((D, 2 * D), lambda i: (0, 0)),
        pl.BlockSpec((D, 128), lambda i: (0, TAIL)),
        full(cos_t.shape),
        full(sin_t.shape),
    ]
    outs = [sds((ctx, rows, 256), BF), sds((8, D), F32)]
    if not first:
        outs.append(sds((rows, D), F32))
    return call(
        kernel,
        outs,
        args,
        4 * rows * D * D,
        in_specs=in_specs,
        out_specs=tuple(full(o.shape) for o in outs),
        grid=(1,),
    )


def block_mask(seg_row, seg_col, qb, length):
    keys = (qb + 1) * QB
    qi = lax.broadcasted_iota(jnp.int32, (QB, keys), 0) + qb * QB
    ki = lax.broadcasted_iota(jnp.int32, (QB, keys), 1)
    sr = seg_row[:, :keys]
    return (ki <= qi) & ((sr == 0) | (sr == seg_col))


def attention_forward(x, seg_row, seg_col, ctx, hq, tok):
    micro = x.shape[1] // tok
    length = ctx * tok
    per = QB // tok

    def kernel(x_ref, sr_ref, sc_ref, o_ref, l_ref):
        xs = x_ref[...].reshape(length, 256)
        ks = xs[:, 128:192]
        vs = xs[:, 192:256]
        for qb in range(length // QB):
            keys = (qb + 1) * QB
            rows = slice(qb * QB, (qb + 1) * QB)
            mask = block_mask(sr_ref[0], sc_ref[0, rows, :], qb, length)
            outs = []
            lses = []
            for h in range(hq):
                q = xs[rows, HS * h : HS * (h + 1)]
                s = jnp.where(mask, dot(q, ks[:keys], 1, 1) * SCALE, -1e30)
                top = jnp.max(s, axis=-1, keepdims=True)
                p = jnp.exp(s - top)
                total = jnp.sum(p, axis=-1, keepdims=True)
                o = dot(p.astype(BF), vs[:keys]) / total
                outs.append(o)
                lses.append(jnp.broadcast_to(top + jnp.log(total), (QB, HS)))
            for _ in range(hq, 2):
                outs.append(jnp.zeros((QB, HS), F32))
                lses.append(jnp.zeros((QB, HS), F32))
            o_ref[qb * per : (qb + 1) * per] = (
                jnp.concatenate(outs, axis=1).astype(BF).reshape(per, tok, 128)
            )
            l_ref[0, rows, :] = jnp.concatenate(lses, axis=1)

    return call(
        kernel,
        [sds((ctx, micro * tok, 128), BF), sds((micro, length, 128), F32)],
        [x, seg_row, seg_col],
        2 * micro * hq * length * length * HS,
        in_specs=[
            pl.BlockSpec((ctx, tok, 256), lambda m: (0, m, 0)),
            pl.BlockSpec((1, 1, length), lambda m: (m, 0, 0)),
            pl.BlockSpec((1, length, 1), lambda m: (m, 0, 0)),
        ],
        out_specs=(
            pl.BlockSpec((ctx, tok, 128), lambda m: (0, m, 0)),
            pl.BlockSpec((1, length, 128), lambda m: (m, 0, 0)),
        ),
        grid=(micro,),
    )


def attention_backward(x, d_out, out, lse, seg_row, seg_col, ctx, hq, tok):
    micro = x.shape[1] // tok
    length = ctx * tok
    per = QB // tok

    def kernel(x_ref, d_ref, o_ref, l_ref, sr_ref, sc_ref, dx_ref, dk_ref, dv_ref):
        xs = x_ref[...].reshape(length, 256)
        ks = xs[:, 128:192]
        vs = xs[:, 192:256]
        ds_all = d_ref[...].reshape(length, 128)
        os_all = o_ref[...].reshape(length, 128)
        dk_ref[...] = jnp.zeros((length, HS), F32)
        dv_ref[...] = jnp.zeros((length, HS), F32)
        for qb in range(length // QB):
            keys = (qb + 1) * QB
            rows = slice(qb * QB, (qb + 1) * QB)
            mask = block_mask(sr_ref[0], sc_ref[0, rows, :], qb, length)
            dqs = []
            for h in range(hq):
                cols = slice(HS * h, HS * (h + 1))
                q = xs[rows, cols]
                do = ds_all[rows, cols]
                delta = jnp.sum(
                    do.astype(F32) * os_all[rows, cols].astype(F32), axis=-1, keepdims=True
                )
                s = dot(q, ks[:keys], 1, 1) * SCALE - l_ref[0, rows, HS * h : HS * h + 1]
                p = jnp.exp(jnp.where(mask, s, -1e30))
                dp = dot(do, vs[:keys], 1, 1)
                ds = (p * (dp - delta) * SCALE).astype(BF)
                dqs.append(dot(ds, ks[:keys]))
                dk_ref[:keys] += dot(ds, q, 0, 0)
                dv_ref[:keys] += dot(p.astype(BF), do, 0, 0)
            for _ in range(hq, 2):
                dqs.append(jnp.zeros((QB, HS), F32))
            dx_ref[qb * per : (qb + 1) * per, :, 0:128] = (
                jnp.concatenate(dqs, axis=1).astype(BF).reshape(per, tok, 128)
            )
        dx_ref[:, :, 128:256] = (
            jnp.concatenate([dk_ref[...], dv_ref[...]], axis=1)
            .astype(BF)
            .reshape(ctx, tok, 128)
        )

    return call(
        kernel,
        [sds((ctx, micro * tok, 256), BF)],
        [x, d_out, out, lse, seg_row, seg_col],
        5 * micro * hq * length * length * HS,
        in_specs=[
            pl.BlockSpec((ctx, tok, 256), lambda m: (0, m, 0)),
            pl.BlockSpec((ctx, tok, 128), lambda m: (0, m, 0)),
            pl.BlockSpec((ctx, tok, 128), lambda m: (0, m, 0)),
            pl.BlockSpec((1, length, 128), lambda m: (m, 0, 0)),
            pl.BlockSpec((1, 1, length), lambda m: (m, 0, 0)),
            pl.BlockSpec((1, length, 1), lambda m: (m, 0, 0)),
        ],
        out_specs=(pl.BlockSpec((ctx, tok, 256), lambda m: (0, m, 0)),),
        grid=(micro,),
        scratch=[pltpu.VMEM((length, HS), F32), pltpu.VMEM((length, HS), F32)],
    )[0]


def side_by_side(m_ref, ctx, hq):
    return jnp.concatenate([m_ref[i][:, : HS * hq] for i in range(ctx)], axis=1)


def output_forward(mixed, stream, packed, gains, chosen, ctx, hq, n, held):
    rows = stream.shape[0]

    def kernel(m_ref, x_ref, w_ref, t_ref, g_ref, c_ref, s_ref, n_ref, gate_ref):
        x = x_ref[...].astype(F32) + dot(side_by_side(m_ref, ctx, hq), w_ref[...])
        s_ref[...] = x
        normed = (x * inv_rms_of(x) * g_ref[1:2]).astype(BF)
        n_ref[...] = normed
        logits = dot(t_ref[...], normed, 0, 1)[:E]
        named = c_ref[...] > 0.0
        logits = jnp.where(named, logits, -1e30)
        top = jnp.max(logits, axis=0, keepdims=True)
        p = jnp.where(named, jnp.exp(logits - top), 0.0)
        gates = p / jnp.sum(p, axis=0, keepdims=True)
        for j in range(n):
            gate_ref[j] = gates[held * j : held * (j + 1)]

    outs = [sds((rows, D), F32), sds((rows, D), BF), sds((n, held, rows), F32)]
    return call(
        kernel,
        outs,
        [mixed, stream, packed, packed, gains, chosen],
        2 * rows * D * D,
        in_specs=[
            full(mixed.shape),
            full(stream.shape),
            pl.BlockSpec((D, D), lambda i: (0, 2)),
            pl.BlockSpec((D, 128), lambda i: (0, TAIL)),
            full(gains.shape),
            full(chosen.shape),
        ],
        out_specs=tuple(full(o.shape) for o in outs),
        grid=(1,),
    )


def by_core(x, shard):
    y = x.astype(BF).reshape(x.shape[0] // (2 * shard), 2, shard, x.shape[1])
    return [y[:, c].reshape(x.shape[0] // 2, x.shape[1]) for c in range(2)]


def norm_back(x, gain, d_normed):
    r = inv_rms_of(x)
    grad_gain = jnp.sum(d_normed * x * r, axis=0, keepdims=True)
    q = d_normed * gain
    dx = r * q - x * (r * r * r) * jnp.mean(x * q, axis=-1, keepdims=True)
    return dx, grad_gain


def output_backward(parts, d_gates, gates, g, stream, normed, mixed, packed, gains, ctx, hq, n, shard):
    rows = stream.shape[0]

    def kernel(p_ref, dg_ref, gt_ref, g_ref, x_ref, nm_ref, m_ref, w_ref, t_ref, gain_ref, g1_ref, dm_ref, gw_ref):
        gates_v = jnp.concatenate([gt_ref[j] for j in range(n)], axis=0)
        dgate_v = jnp.concatenate([dg_ref[j] for j in range(n)], axis=0)
        mean = jnp.sum(gates_v * dgate_v, axis=0, keepdims=True)
        d_logits = (gates_v * (dgate_v - mean)).astype(BF)
        d_logits = jnp.concatenate([d_logits, jnp.zeros((128 - E, rows), BF)], axis=0)
        router = t_ref[...]
        d_normed = dot(d_logits, router, 0, 1)
        for j in range(n):
            d_normed = d_normed + p_ref[j].astype(F32)
        x = x_ref[...]
        dx, grad_gain = norm_back(x, gain_ref[1:2], d_normed)
        g1 = g_ref[...].astype(F32) + dx
        g1_ref[...] = g1
        low = g1.astype(BF)
        dm = dot(low, w_ref[...], 1, 1).astype(BF)
        for i in range(ctx):
            part = dm[:, HS * hq * i : HS * hq * (i + 1)]
            if hq < 2:
                part = jnp.concatenate([part, jnp.zeros((rows, 128 - HS * hq), BF)], axis=1)
            dm_ref[i] = part
        grad_out = dot(side_by_side(m_ref, ctx, hq), low, 0, 0)
        for c, value in enumerate(by_core(grad_out, shard)):
            gw_ref[c, :, 0:D] = value
        grad_router = dot(nm_ref[...], d_logits, 0, 1)
        row = lax.broadcasted_iota(jnp.int32, (128, D), 0)
        cols = jnp.where(row == 33, jnp.broadcast_to(grad_gain, (128, D)), 0.0)
        for c, value in enumerate(by_core(grad_router + jnp.transpose(cols), shard)):
            gw_ref[c, :, D : D + 128] = value

    outs = [sds((rows, D), F32), sds((ctx, rows, 128), BF), sds((2, D // 2, D + 128), BF)]
    args = [parts, d_gates, gates, g, stream, normed, mixed, packed, packed, gains]
    in_specs = [full(a.shape) for a in args]
    in_specs[7] = pl.BlockSpec((D, D), lambda i: (0, 2))
    in_specs[8] = pl.BlockSpec((D, 128), lambda i: (0, TAIL))
    return call(
        kernel,
        outs,
        args,
        4 * rows * D * D,
        in_specs=in_specs,
        out_specs=tuple(full(o.shape) for o in outs),
        grid=(1,),
    )


def qkv_backward(dx, g1, stream, packed, gains, cos_t, sin_t, ctx, hq, shard):
    rows = g1.shape[0]
    dup = ctx // KEY_VALUE_HEADS

    def kernel(d_ref, g_ref, x_ref, w_ref, gain_ref, c_ref, s_ref, out_ref, gw_ref):
        x = x_ref[...].astype(F32)
        gain = gain_ref[0:1]
        normed = (x * inv_rms_of(x) * gain).astype(BF)
        cos_v = c_ref[...]
        sin_v = s_ref[...]
        queries = in_order([d_ref[i][:, : HS * hq] for i in range(ctx)])
        both = []
        for head in range(KEY_VALUE_HEADS):
            total = d_ref[head * dup][:, 128:256]
            if dup > 1:
                total = total.astype(F32)
                for r in range(1, dup):
                    total = total + d_ref[head * dup + r][:, 128:256].astype(F32)
            both.append(total)
        keys = in_order([t[:, :HS] for t in both])
        values = in_order([t[:, HS:] for t in both])
        d_normed = jnp.zeros((rows, D), F32)
        for i in range(8):
            if i < 4:
                y = queries[:, 256 * i : 256 * (i + 1)]
            elif i < 6:
                y = keys[:, 256 * (i - 4) : 256 * (i - 3)]
            else:
                y = values[:, 256 * (i - 6) : 256 * (i - 5)]
            if i < 6:
                y = y.astype(F32)
                y = y * cos_v - swap_halves(y) * sin_v
            lin = y.astype(BF)
            cols = slice(256 * i, 256 * (i + 1))
            d_normed = d_normed + dot(lin, w_ref[:, cols], 1, 1)
            for c, value in enumerate(by_core(dot(normed, lin, 0, 0), shard)):
                gw_ref[c, :, cols] = value
        back, grad_gain = norm_back(x, gain, d_normed)
        out_ref[...] = g_ref[...] + back
        row = lax.broadcasted_iota(jnp.int32, (128, D), 0)
        cols = jnp.where(row == 0, jnp.broadcast_to(grad_gain, (128, D)), 0.0)
        for c, value in enumerate(by_core(jnp.transpose(cols), shard)):
            gw_ref[c, :, 2 * D : 2 * D + 128] = value

    outs = [sds((rows, D), F32), sds((2, D // 2, 2 * D + 128), BF)]
    args = [dx, g1, stream, packed, gains, cos_t, sin_t]
    in_specs = [full(a.shape) for a in args]
    in_specs[3] = pl.BlockSpec((D, 2 * D), lambda i: (0, 0))
    return call(
        kernel,
        outs,
        args,
        8 * rows * D * D,
        in_specs=in_specs,
        out_specs=tuple(full(o.shape) for o in outs),
        grid=(1,),
    )


def pick_matrix(slot_row, rows):
    at = lax.broadcasted_iota(jnp.int32, (2 * SLOTS, rows), 0)
    return at == slot_row


def weight_specs(weights):
    return [
        pl.BlockSpec((1,) + w.shape[1:], lambda e: (e, 0, 0, 0)) for w in weights
    ]


def matrices(first_ref, second_ref):
    ctx, depth, _ = first_ref.shape[1:]
    half = F // ctx
    second = second_ref[0]
    return (
        first_ref[0].reshape(D, F),
        second[:, :depth].reshape(D, F),
        second[:, depth : depth + half].reshape(F, D // 2),
        second[:, depth + half :].reshape(F, D // 2),
    )


def experts_forward(x, gates, slots, weights, held):
    n, rows, _ = x.shape
    lanes = 2 * SLOTS


    def kernel(x_ref, g_ref, s_ref, w0, w1, out_ref, acc_ref, row_ref, eo_ref):
        e = pl.program_id(0)
        w_gate, w_up, down_l, down_r = matrices(w0, w1)
        for s in range(n):
            pick = pick_matrix(s_ref[s, pl.ds(e, 1), :], rows).astype(BF)
            row_ref[lanes * s : lanes * (s + 1), :] = dot(pick, x_ref[s]).astype(BF)
        rws = row_ref[...]
        ga = dot(rws, w_gate)
        up = dot(rws, w_up)
        hidden = (ga * jax.nn.sigmoid(ga) * up).astype(BF)
        eo_ref[:, : D // 2] = dot(hidden, down_l).astype(BF)
        eo_ref[:, D // 2 :] = dot(hidden, down_r).astype(BF)
        for s in range(n):
            pick = pick_matrix(s_ref[s, pl.ds(e, 1), :], rows)
            gated = jnp.where(pick, g_ref[s, pl.ds(e, 1), :], 0.0).astype(BF)
            add = dot(gated, eo_ref[lanes * s : lanes * (s + 1), :], 0, 0)

            @pl.when(e == 0)
            def _():
                acc_ref[s] = add.astype(F32)

            @pl.when((e > 0) & (e < held - 1))
            def _():
                acc_ref[s] = (acc_ref[s].astype(F32) + add).astype(F32)

            @pl.when(e == held - 1)
            def _():
                out_ref[s] = (acc_ref[s].astype(F32) + add).astype(BF)

    flops = 2 * held * n * (lanes * D * F * 3 + 2 * lanes * rows * D)
    return call(
        kernel,
        [sds(x.shape, BF)],
        [x, gates, slots] + list(weights),
        flops,
        in_specs=[full(x.shape), full(gates.shape), full(slots.shape)] + weight_specs(weights),
        out_specs=(full(x.shape),),
        grid=(held,),
        scratch=[
            pltpu.VMEM(x.shape, F32),
            pltpu.VMEM((n * lanes, D), BF),
            pltpu.VMEM((n * lanes, D), BF),
        ],
    )[0]


def experts_backward(x, g, gates, slots, weights, held, with_out):
    n, rows, _ = x.shape
    lanes = 2 * SLOTS


    def kernel(x_ref, gr_ref, g_ref, s_ref, w0, w1, *rest):
        dx_ref, dg_ref = rest[:2]
        first_grad, second_grad, *rest = rest[2:]
        if with_out:
            out_ref, acc_ref, row_ref, grow_ref = rest
        else:
            acc_ref, row_ref, grow_ref = rest
        e = pl.program_id(0)
        w_gate, w_up, down_l, down_r = matrices(w0, w1)
        slot_gates = []
        for s in range(n):
            mine = slice(lanes * s, lanes * (s + 1))
            pick = pick_matrix(s_ref[s, pl.ds(e, 1), :], rows)
            low = pick.astype(BF)
            row_ref[mine, :] = dot(low, x_ref[s]).astype(BF)
            grow_ref[mine, :] = dot(low, gr_ref[s]).astype(BF)
            gated = jnp.where(pick, g_ref[s, pl.ds(e, 1), :], 0.0)
            slot_gates.append(jnp.sum(gated, axis=1, keepdims=True))
        gate = jnp.concatenate(slot_gates, axis=0)
        rws = row_ref[...]
        grows = grow_ref[...]
        ga = dot(rws, w_gate)
        up = dot(rws, w_up)
        sig = jax.nn.sigmoid(ga)
        act = ga * sig
        hidden_f = act * up
        hidden = hidden_f.astype(BF)
        dhg = dot(grows[:, : D // 2], down_l, 1, 1) + dot(grows[:, D // 2 :], down_r, 1, 1)
        d_gate = jnp.sum(hidden.astype(F32) * dhg, axis=1, keepdims=True)
        dh = dhg * gate
        dga = (dh * up * (sig * (1.0 + ga * (1.0 - sig)))).astype(BF)
        dup = (dh * act).astype(BF)
        if with_out:
            eo = jnp.concatenate([dot(hidden, down_l), dot(hidden, down_r)], axis=1).astype(BF)
        drow = (dot(dga, w_gate, 1, 1) + dot(dup, w_up, 1, 1)).astype(BF)
        for s in range(n):
            mine = slice(lanes * s, lanes * (s + 1))
            pick = pick_matrix(s_ref[s, pl.ds(e, 1), :], rows)
            dg_ref[s, pl.ds(e, 1), :] = jnp.sum(
                jnp.where(pick, d_gate[mine], 0.0), axis=0, keepdims=True
            )
            todo = [(acc_ref, dx_ref, dot(pick.astype(BF), drow[mine], 0, 0))]
            if with_out:
                gated = jnp.where(pick, g_ref[s, pl.ds(e, 1), :], 0.0).astype(BF)
                todo.append((out_ref, out_ref, dot(gated, eo[mine], 0, 0)))
            for held_ref, final_ref, add in todo:

                @pl.when(e == 0)
                def _():
                    held_ref[s] = add.astype(held_ref.dtype)

                @pl.when((e > 0) & (e < held - 1))
                def _():
                    held_ref[s] = (held_ref[s].astype(F32) + add).astype(held_ref.dtype)

                @pl.when(e == held - 1)
                def _():
                    final_ref[s] = (held_ref[s].astype(F32) + add).astype(BF)

        dslot = (grows.astype(F32) * gate).astype(BF)
        ctx, depth, _ = first_grad.shape[1:]
        part = F // ctx
        first_grad[0] = dot(rws, dga, 0, 0).astype(BF).reshape(ctx, depth, F)
        second_grad[0, :, :depth, :] = dot(rws, dup, 0, 0).astype(BF).reshape(ctx, depth, F)
        for k in range(2):
            cols = dslot[:, D // 2 * k : D // 2 * (k + 1)]
            at_row = depth + part * k
            second_grad[0, :, at_row : at_row + part, :] = (
                dot(hidden, cols, 0, 0).astype(BF).reshape(ctx, part, D // 2)
            )

    outs = [sds(x.shape, BF), sds(gates.shape, F32)] + [sds(w.shape, BF) for w in weights]
    out_specs = [full(x.shape), full(gates.shape)] + weight_specs(weights)
    scratch = [
        pltpu.VMEM(x.shape, F32),
        pltpu.VMEM((n * lanes, D), BF),
        pltpu.VMEM((n * lanes, D), BF),
    ]
    if with_out:
        outs.append(sds(x.shape, BF))
        out_specs.append(full(x.shape))
    flops = 2 * held * n * (lanes * D * F * 9 + 3 * lanes * rows * D)
    return call(
        kernel,
        outs,
        [x, g, gates, slots] + list(weights),
        flops,
        in_specs=[full(x.shape), full(g.shape), full(gates.shape), full(slots.shape)]
        + weight_specs(weights),
        out_specs=tuple(out_specs),
        grid=(held,),
        scratch=scratch,
    )


def per_device(
    sizes,
    hidden_in,
    grad_out,
    segments,
    routes,
    attn_gain,
    w_query,
    key_weight,
    value_weight,
    w_output,
    ffn_gain,
    w_router,
    w_gate,
    w_up,
    w_down,
):
    micro, tok, _ = hidden_in.shape
    rows = micro * tok
    grp_size, ctx, planes = sizes
    hq = QUERY_HEADS // ctx
    held = 2 * grp_size
    every = ("grp", "zq", "zp", "core")
    line = ("zq", "zp", "core")
    core = lax.axis_index("core")
    ctx_index = (lax.axis_index("zq") * planes + lax.axis_index("zp")) * 2 + core
    shard = w_query.shape[1]

    def by_plane(x, axis, back=False):
        dims = (planes, grp_size, 2) if back else (grp_size, planes, 2)
        head, tail = x.shape[:axis], x.shape[axis + 1 :]
        y = jnp.swapaxes(x.reshape(head + dims + tail), axis, axis + 1)
        return y.reshape(x.shape)

    def pack(layer):
        return jnp.concatenate(
            [
                w_query[layer],
                key_weight[layer],
                value_weight[layer],
                w_output[layer],
                by_plane(w_router[layer], 1),
                attn_gain[layer][:, None],
                ffn_gain[layer][:, None],
                jnp.zeros((shard, 128 - E - 2), BF),
            ],
            axis=1,
        )

    ids_of = iter(range(1, 100))

    def move(*ops):
        return transfer(ops, next(ids_of), sizes)

    def swap(x):
        return lax.ppermute(x, "core", [(0, 1), (1, 0)])

    def second_shard(layer):
        down = w_down[layer]
        return jnp.concatenate([w_up[layer], down[:, :, : D // 2], down[:, :, D // 2 :]], axis=1)

    def plane_gather(w):
        return lax.all_gather(w[None], ("grp", "core"), axis=0, tiled=True)

    grad_rows = grad_out.reshape(rows, D)
    (gate_parts,) = move((w_gate[0], "line", "pick"))
    gate_parts, own_pack, own_second = lax.optimization_barrier(
        (gate_parts, pack(0), second_shard(0))
    )
    first, second_parts = move((own_pack, None, "packed"), (own_second, "line", "pick"))
    packed = [first.reshape(D, -1), None]
    weights = [[plane_gather(gate_parts), plane_gather(second_parts)], None]

    own_segments = lax.dynamic_slice_in_dim(segments, ctx_index * tok, tok, axis=1)
    prompt = jnp.sum((segments == 0).astype(jnp.int32), axis=1, dtype=jnp.int32)
    before = jnp.sum(
        (segments[:, None, :] < own_segments[:, :, None]).astype(jnp.int32),
        axis=2,
        dtype=jnp.int32,
    )
    places = ctx_index * tok + jnp.arange(tok, dtype=jnp.int32)[None, :]
    places = jnp.where(own_segments == 0, places, prompt[:, None] + places - before)
    places = places.reshape(rows).astype(F32)
    lane = jnp.arange(256, dtype=jnp.int32)
    freqs = jnp.exp(
        (lane % (HS // 2)).astype(F32) * (-2.0 * math.log(10000.0) / HS)
    )
    angles = places[:, None] * freqs[None, :]
    sign = jnp.where((lane % HS) < HS // 2, -1.0, 1.0)[None, :]
    cos_t = jnp.cos(angles)
    sin_t = jnp.sin(angles) * sign
    seg_row = segments[:, None, :]
    seg_col = segments[:, :, None]

    flat = routes.reshape(rows, TOP)
    ids = by_plane(jnp.arange(E, dtype=jnp.int32), 0)
    chosen = jnp.any(ids[:, None, None] == flat[None, :, :], axis=2)
    marks = chosen.astype(BF).reshape(E, micro, tok)
    earlier = (
        jnp.arange(tok)[:, None] < jnp.arange(tok)[None, :]
    ).astype(BF)
    rank = jnp.einsum("emt,ts->ems", marks, earlier, preferred_element_type=F32)
    slot = rank.astype(jnp.int32) + SLOTS * jnp.arange(micro, dtype=jnp.int32)[None, :, None]
    slot = jnp.where(chosen, slot.reshape(E, rows), -1)

    slot = slot.reshape(planes, held, rows)
    chosen_f = chosen.astype(F32)

    saved = []
    parts = (hidden_in.reshape(rows, D),)
    for layer in range(LAYERS):
        got = qkv_forward(parts, packed[layer], cos_t, sin_t, ctx, hq)
        qkv, gains = got[0], got[1]
        stream = parts[0] if layer == 0 else got[2]
        (heads,) = move((qkv, "line", "own"))
        out, lse = attention_forward(heads, seg_row, seg_col, ctx, hq, tok)
        (mixed,) = move((out, "line", "own"))
        stream1, normed, gates = output_forward(
            mixed, stream, packed[layer], gains, chosen_f, ctx, hq, planes, held
        )
        ops = [(normed, "tok", "all"), (gates, "tok", "own")]
        if layer == 0:
            xs, gates_here, slots_here, late_gate = move(
                *ops, (slot, "tok", "own"), (w_gate[1], "line", "pick")
            )
            late_g, late_second, _ = lax.optimization_barrier(
                (grad_rows, second_shard(1), xs)
            )
            last_g = lax.all_gather(late_g, "zp", axis=0, tiled=False)
            late_gate = plane_gather(late_gate)
        else:
            xs, gates_here = move(*ops)
        saved.append((stream, heads, out, lse, mixed, stream1, normed, gates, gains, xs, gates_here))
        if layer == 0:
            sent = experts_forward(xs, gates_here, slots_here, weights[0], held)
            came, after, late_second = move(
                (sent, "tok", "own"), (pack(1), None, "packed"), (late_second, "line", "pick")
            )
            packed[1] = after.reshape(D, -1)
            weights[1] = [late_gate, plane_gather(late_second)]
            parts = (stream1, came)

    def plane_scatter(r):
        return lax.psum_scatter(r, ("grp", "core"), scatter_dimension=0, tiled=True)[0]

    def owned_rows(r):
        r = r.astype(F32).reshape((ctx // (2 * planes), 2 * planes) + r.shape[1:])
        return jnp.sum(r, axis=0)

    def between_cores(x):
        theirs = lax.dynamic_index_in_dim(x, 1 - core, 0, keepdims=False)
        return with_other(x, swap(theirs))

    def with_other(x, came):
        ours = lax.dynamic_index_in_dim(x, core, 0, keepdims=False)
        return by_owner((ours.astype(F32) + came.astype(F32)).astype(BF))

    def by_owner(x):
        return x.reshape(grp_size, ctx // 2, shard, x.shape[1])

    def over_grp(x):
        return jnp.sum(x.astype(F32), axis=0).astype(BF)

    g = grad_rows
    for layer in reversed(range(LAYERS)):
        stream, heads, out, lse, mixed, stream1, normed, gates, gains, xs, gates_here = saved[layer]
        last = layer == LAYERS - 1
        if last:
            gs = last_g
        else:
            gs, last_small, came = move(
                (g.astype(BF), "tok", "all"), (over_grp(small), "z", "own"), (wide, "sib", "own")
            )
            wide = with_other(wide, came)
            gs, *last_experts = lax.optimization_barrier((gs, *last_experts))
            last_experts = [lax.all_to_all(r, line, 0, 0, tiled=True) for r in last_experts]
            final_parts, _ = lax.optimization_barrier((final_parts, gs))
            final_sum = lax.psum_scatter(final_parts, "zp", scatter_dimension=0, tiled=True)
            hidden_out = (
                (saved[1][5] + final_sum[0].astype(F32)).astype(BF).reshape(micro, tok, D)
            )
        res = experts_backward(xs, gs, gates_here, slots_here, weights[layer], held, last)
        if not last:
            *res, last_second = lax.optimization_barrier((*res, last_experts[1]))
            last_experts[1] = last_second
        experts = [plane_scatter(r) for r in res[2:4]]
        back = [(res[0], "tok", "own"), (res[1], "tok", "own")]
        if last:
            last_experts = experts
            final_parts = res[4]
            d_parts, d_gates = move(*back)
        else:
            d_parts, d_gates, last_wide = move(*back, (wide, "g", "own"))
        g1, d_mixed, small = output_backward(
            d_parts, d_gates, gates, g, stream1, normed, mixed, packed[layer], gains,
            ctx, hq, planes, shard,
        )
        ops = [(d_mixed, "line", "own"), (small, "sib", "own")]
        if last:
            d_out, came = move(*ops)
        else:
            d_out, came, last_wide = move(*ops, (over_grp(last_wide), "z", "own"))
        small = with_other(small, came)
        dx = attention_backward(heads, d_out, out, lse, seg_row, seg_col, ctx, hq, tok)
        dx, small = move((dx, "line", "own"), (small, "g", "own"))
        g, wide = qkv_backward(
            dx, g1, stream, packed[layer], gains, cos_t, sin_t, ctx, hq, shard
        )
    first_wide, first_gate, first_small = move(
        (between_cores(wide), "g", "own"),
        (experts[0], "line", "own"),
        (over_grp(small), "z", "own"),
    )
    first_wide, first_second = move(
        (over_grp(first_wide), "z", "own"), (experts[1], "line", "own")
    )

    def along_z(x):
        return jnp.sum(x.astype(F32), axis=0)

    wides = [along_z(first_wide), along_z(last_wide)]
    smalls = [along_z(first_small), along_z(last_small)]
    def matrices_of(first, second):
        first, second = owned_rows(first), owned_rows(second)
        depth, part = D // ctx, F // ctx
        down = [second[:, depth + part * k : depth + part * (k + 1)] for k in range(2)]
        return first, second[:, :depth], jnp.concatenate(down, axis=2)

    owned_experts = [matrices_of(first_gate, first_second), matrices_of(*last_experts)]

    def unpack(layer):
        w, s = wides[layer], smalls[layer]
        kv = KEY_VALUE_HEADS * HS
        return (
            w[:, :D],
            w[:, D : D + kv],
            w[:, D + kv : 2 * D],
            s[:, :D],
            s[:, D + 33],
            by_plane(s[:, D : D + E], 1, back=True),
        )

    got = [unpack(layer) for layer in range(LAYERS)]

    def stacked(k):
        return jnp.stack([got[layer][k] for layer in range(LAYERS)])

    gain_grad = jnp.stack([w[:, 2 * D] for w in wides])

    def owned(k):
        return jnp.stack([owned_experts[layer][k] for layer in range(LAYERS)])

    return (
        hidden_out,
        g.reshape(micro, tok, D),
        gain_grad,
        stacked(0),
        stacked(1),
        stacked(2),
        stacked(3),
        stacked(4),
        stacked(5),
        owned(0),
        owned(1),
        owned(2),
    )


def solution(mesh):
    grp_size = mesh.shape["grp"]
    ctx = mesh.shape["ctx"]
    planes = E // grp_size // 2
    fine = Mesh(
        mesh.devices.reshape(grp_size, ctx // (2 * planes), planes, 2),
        ("grp", "zq", "zp", "core"),
    )
    line = ("zq", "zp", "core")
    every = ("grp",) + line
    row = P("grp", line, None)
    placed = (
        row,
        row,
        P("grp", None),
        row,
        P(None, every),
        P(None, every, None),
        P(None, every, None),
        P(None, every, None),
        P(None, every, None),
        P(None, every),
        P(None, every, None),
        P(None, "grp", line, None),
        P(None, "grp", line, None),
        P(None, "grp", line, None),
    )
    return jax.shard_map(
        functools.partial(per_device, (grp_size, ctx, planes)),
        mesh=fine,
        in_specs=placed,
        out_specs=(
            row,
            row,
            P(None, every),
            P(None, every, None),
            P(None, every, None),
            P(None, every, None),
            P(None, every, None),
            P(None, every),
            P(None, every, None),
            P(None, "grp", line, None),
            P(None, "grp", line, None),
            P(None, "grp", line, None),
        ),
        check_vma=False,
    )
```

```python
import functools
import math

import jax
import jax.numpy as jnp
from jax import lax
from jax.experimental import pallas as pl
from jax.experimental.pallas import tpu as pltpu
from jax.sharding import Mesh, PartitionSpec as P

D = 1024
QUERY_HEADS = 16
KEY_VALUE_HEADS = 8
HS = 64
E = 32
F = 512
TOP = 8
LAYERS = 2
CAP = 42
SLOTS = 48
EPSILON = 1e-06
SCALE = float(HS) ** (-0.5)
QB = 256
BF = jnp.bfloat16
F32 = jnp.float32
MESH = pl.DeviceIdType.MESH
PIECES = 8
VMEM_BYTES = 58 * 1024 * 1024
TAIL = 3 * D // 128


def dot(a, b, ca=1, cb=0):
    return lax.dot_general(a, b, (((ca,), (cb,)), ((), ())), preferred_element_type=F32)


def call(kernel, outs, args, flops, in_specs=None, out_specs=None, grid=None, scratch=()):
    nbytes = sum(a.size * a.dtype.itemsize for a in args)
    nbytes += sum(math.prod(o.shape) * jnp.dtype(o.dtype).itemsize for o in outs)
    kw = {} if grid is None else {"grid": grid}
    if in_specs is not None:
        kw["in_specs"] = in_specs
    if out_specs is not None:
        kw["out_specs"] = out_specs
    return pl.pallas_call(
        kernel,
        out_shape=tuple(outs),
        scratch_shapes=list(scratch),
        compiler_params=pltpu.CompilerParams(vmem_limit_bytes=VMEM_BYTES),
        cost_estimate=pl.CostEstimate(
            flops=int(flops), bytes_accessed=int(nbytes), transcendentals=0
        ),
        **kw,
    )(*args)


def sds(shape, dtype):
    return jax.ShapeDtypeStruct(tuple(shape), dtype)


def full(shape):
    n = len(shape)
    return pl.BlockSpec(tuple(shape), lambda *_: (0,) * n)


def size_of(group, sizes):
    grp_size, ctx, planes = sizes
    return {"g": grp_size, "tok": planes, "line": ctx, "z": ctx // 2, "sib": 2}[group]


def place_in(group, sizes):
    planes = sizes[2]
    n = size_of(group, sizes)
    zp = lax.axis_index("zp")
    zz = lax.axis_index("zq") * planes + zp
    core = lax.axis_index("core")
    if group == "g":
        return n, lax.axis_index("grp"), lambda p: {"grp": p}
    if group == "tok":
        return n, zp, lambda p: {"zp": p}
    if group == "line":
        return (
            n,
            zz * 2 + core,
            lambda p: {
                "zq": p // (2 * planes),
                "zp": lax.rem(p // 2, planes),
                "core": lax.rem(p, 2),
            },
        )
    if group == "z":
        return n, zz, lambda p: {"zq": p // planes, "zp": lax.rem(p, planes)}
    return n, core, lambda p: {"core": p}


def transfer(ops, cid, sizes):
    grp_size, ctx, _ = sizes
    groups = []
    for _, group, what in ops:
        for name in ("z", "g", "sib") if what == "packed" else (group,):
            if name not in groups:
                groups.append(name)
    shapes = []
    sems = []
    total_sems = 0
    for x, group, what in ops:
        sems.append(total_sems)
        if what == "packed":
            shapes.append(sds((grp_size, ctx) + x.shape, x.dtype))
            zs = ctx // 2
            total_sems += zs + zs * grp_size * 2
            continue
        n = size_of(group, sizes)
        total_sems += PIECES if group == "sib" else 2 * n if what == "all" else n
        rest = x.shape[1:] if group == "sib" else x.shape
        if what != "own":
            rest = (n,) + (x.shape if what == "all" else x.shape[1:])
        shapes.append(sds(rest, x.dtype))
    count = len(ops)

    def kernel(*refs):
        ins = refs[:count]
        outs = refs[count : count + len(shapes)]
        send, recv, local = refs[count + len(shapes) :]
        barrier = pltpu.get_barrier_semaphore()
        total = 0
        for group in groups:
            n, me, where = place_in(group, sizes)
            for k in range(1, n):
                pl.semaphore_signal(
                    barrier, inc=1, device_id=where(lax.rem(me + k, n)), device_id_type=MESH
                )
            total += n - 1
        pl.semaphore_wait(barrier, total)

        def remote(src, dst, at, place):
            copy = pltpu.make_async_remote_copy(
                src_ref=src,
                dst_ref=dst,
                send_sem=send.at[at],
                recv_sem=recv.at[at],
                device_id=place,
                device_id_type=MESH,
            )
            copy.start()
            return copy

        sib_place = {"core": 1 - lax.axis_index("core")}
        sent = []
        own_copies = []

        def start(i):
            _, group, what = ops[i]
            n, me, where = place_in(group or "g", sizes)
            out = outs[i]
            if what == "all":
                copy = pltpu.make_async_copy(ins[i], out.at[me], local.at[i])
                copy.start()
                own_copies.append(copy)

                @pl.when(me < n - 1)
                def _():
                    hop(i, n, ins[i], me, 1).start()

                @pl.when(me > 0)
                def _():
                    hop(i, n, ins[i], me, -1).start()

                return None
            if what == "packed":
                grp = lax.axis_index("grp")
                core = lax.axis_index("core")
                zs, zz, z_place = place_in("z", sizes)
                copy = pltpu.make_async_copy(ins[i], out.at[grp, zz * 2 + core], local.at[i])
                copy.start()
                along = []
                for k in range(1, zs):
                    along.append(
                        remote(
                            ins[i],
                            out.at[grp, zz * 2 + core],
                            sems[i] + k,
                            z_place(lax.rem(zz + k, zs)),
                        )
                    )
                return (i, along, copy)
            if group == "sib":
                size = ins[i].shape[1] // PIECES
                for j in range(PIECES):
                    part = pl.ds(j * size, size)
                    sent.append(
                        remote(ins[i].at[1 - me, part], out.at[part], sems[i] + j, where(1 - me))
                    )
                return None
            copies = []
            for k in range(1, n):
                peer = lax.rem(me + k, n)
                if what == "own":
                    src = ins[i].at[peer]
                else:
                    src = ins[i].at[lax.rem(peer, ins[i].shape[0])]
                copies.append(remote(src, out.at[me], sems[i] + k, where(peer)))
            if what == "own":
                src = ins[i].at[me]
            else:
                src = ins[i].at[lax.rem(me, ins[i].shape[0])]
            copy = pltpu.make_async_copy(src, out.at[me], local.at[i])
            copy.start()
            own_copies.append(copy)
            sent.extend(copies)
            return None

        def hop(i, n, src, block, way):
            _, me, where = place_in(ops[i][1], sizes)
            return pltpu.make_async_remote_copy(
                src_ref=src,
                dst_ref=outs[i].at[block],
                send_sem=send.at[sems[i] + block + (0 if way > 0 else n)],
                recv_sem=recv.at[sems[i] + block],
                device_id=where(me + way),
                device_id_type=MESH,
            )

        def finish_all(i):
            n, me, _ = place_in(ops[i][1], sizes)
            out = outs[i]
            for far in range(1, n):
                low, high = me - far, me + far

                @pl.when(low >= 0)
                def _():
                    hop(i, n, out.at[low], low, 1).wait_recv()

                    @pl.when(me < n - 1)
                    def _():
                        hop(i, n, out.at[low], low, 1).start()

                @pl.when(high <= n - 1)
                def _():
                    hop(i, n, out.at[high], high, -1).wait_recv()

                    @pl.when(me > 0)
                    def _():
                        hop(i, n, out.at[high], high, -1).start()

            for far in range(n):
                low, high = me - far, me + far

                @pl.when((low >= 0) & (me < n - 1))
                def _():
                    hop(i, n, ins[i] if far == 0 else out.at[low], low, 1).wait_send()

                @pl.when((high <= n - 1) & (me > 0))
                def _():
                    hop(i, n, ins[i] if far == 0 else out.at[high], high, -1).wait_send()

        def finish_packed(i, along, own):
            grp = lax.axis_index("grp")
            core = lax.axis_index("core")
            zs, zz, _ = place_in("z", sizes)
            out = outs[i]
            base = sems[i] + zs
            over = []

            def spread(j, at):
                for m in range(1, grp_size):
                    over.append(
                        (
                            remote(
                                out.at[at[0], at[1]],
                                out.at[at[0], at[1]],
                                base + j * grp_size + m,
                                {"grp": lax.rem(grp + m, grp_size)},
                            ),
                            j,
                            m,
                        )
                    )

            def to_core(j, m, at):
                sent.append(
                    remote(
                        out.at[at[0], at[1]],
                        out.at[at[0], at[1]],
                        base + zs * grp_size + j * grp_size + m,
                        sib_place,
                    )
                )

            own.wait()
            for j in range(zs):
                if j > 0:
                    along[j - 1].wait_recv()
                at = (grp, lax.rem(zz - j + zs, zs) * 2 + core)
                spread(j, at)
                to_core(j, 0, at)
            for copy, j, m in over:
                copy.wait_recv()
                at = (
                    lax.rem(grp - m + grp_size, grp_size),
                    lax.rem(zz - j + zs, zs) * 2 + core,
                )
                to_core(j, m, at)
            for copy in along:
                copy.wait_send()
            for copy, _, _ in over:
                copy.wait_send()

        pending = []
        for i in range(count):
            got = start(i)
            if got is not None:
                pending.append(got)
        for item in pending:
            finish_packed(*item)
        for i in range(count):
            if ops[i][2] == "all":
                finish_all(i)
        for copy in own_copies:
            copy.wait()
        for copy in sent:
            copy.wait()

    total = sum(math.prod(o.shape) * jnp.dtype(o.dtype).itemsize for o in shapes)
    any_spec = pl.BlockSpec(memory_space=pl.ANY)
    return pl.pallas_call(
        kernel,
        out_shape=tuple(shapes),
        in_specs=[any_spec] * count,
        out_specs=tuple([any_spec] * len(shapes)),
        scratch_shapes=[
            pltpu.SemaphoreType.DMA((total_sems,)),
            pltpu.SemaphoreType.DMA((total_sems,)),
            pltpu.SemaphoreType.DMA((count,)),
        ],
        compiler_params=pltpu.CompilerParams(collective_id=cid, has_side_effects=True),
        cost_estimate=pl.CostEstimate(
            flops=0, bytes_accessed=40 * int(total), transcendentals=0
        ),
    )(*[x for x, _, _ in ops])


def swap_halves(x):
    lane = lax.broadcasted_iota(jnp.int32, x.shape, 1)
    width = x.shape[1]
    up = pltpu.roll(x, width - HS // 2, 1)
    down = pltpu.roll(x, HS // 2, 1)
    return jnp.where((lane & (HS - 1)) < HS // 2, up, down)


def inv_rms_of(x):
    return lax.rsqrt(jnp.mean(x * x, axis=-1, keepdims=True) + EPSILON)


def in_order(parts):
    return parts[0] if len(parts) == 1 else jnp.concatenate(parts, axis=1)


def qkv_forward(stream_parts, packed, cos_t, sin_t, ctx, hq):
    first = len(stream_parts) == 1
    rows = stream_parts[0].shape[0]
    dup = ctx // KEY_VALUE_HEADS

    def kernel(*refs):
        if first:
            h_ref, w_ref, t_ref, c_ref, s_ref, out_ref, gains_ref = refs
            x = h_ref[...].astype(F32)
        else:
            h_ref, p_ref, w_ref, t_ref, c_ref, s_ref, out_ref, gains_ref, x_ref = refs
            x = h_ref[...]
            for j in range(p_ref.shape[0]):
                x = x + p_ref[j].astype(F32)
            x_ref[...] = x
        gains = jnp.transpose(t_ref[...].astype(F32))[32:40]
        gains_ref[...] = gains
        normed = (x * inv_rms_of(x) * gains[0:1]).astype(BF)
        cos_v = c_ref[...]
        sin_v = s_ref[...]
        parts = []
        for i in range(8):
            y = dot(normed, w_ref[:, 256 * i : 256 * (i + 1)])
            if i < 6:
                y = y * cos_v + swap_halves(y) * sin_v
            parts.append(y.astype(BF))
        queries, keys, values = in_order(parts[:4]), in_order(parts[4:6]), in_order(parts[6:])
        for i in range(ctx):
            mine = [queries[:, HS * hq * i : HS * hq * (i + 1)]]
            if hq < 2:
                mine.append(jnp.zeros((rows, 128 - HS * hq), BF))
            kv = i // dup
            mine.append(keys[:, HS * kv : HS * (kv + 1)])
            mine.append(values[:, HS * kv : HS * (kv + 1)])
            out_ref[i] = in_order(mine)

    args = list(stream_parts) + [packed, packed, cos_t, sin_t]
    in_specs = [full(a.shape) for a in stream_parts] + [
        pl.BlockSpec((D, 2 * D), lambda i: (0, 0)),
        pl.BlockSpec((D, 128), lambda i: (0, TAIL)),
        full(cos_t.shape),
        full(sin_t.shape),
    ]
    outs = [sds((ctx, rows, 256), BF), sds((8, D), F32)]
    if not first:
        outs.append(sds((rows, D), F32))
    return call(
        kernel,
        outs,
        args,
        4 * rows * D * D,
        in_specs=in_specs,
        out_specs=tuple(full(o.shape) for o in outs),
        grid=(1,),
    )


def block_mask(seg_row, seg_col, qb, length):
    keys = (qb + 1) * QB
    qi = lax.broadcasted_iota(jnp.int32, (QB, keys), 0) + qb * QB
    ki = lax.broadcasted_iota(jnp.int32, (QB, keys), 1)
    sr = seg_row[:, :keys]
    return (ki <= qi) & ((sr == 0) | (sr == seg_col))


def attention_forward(x, seg_row, seg_col, ctx, hq, tok):
    micro = x.shape[1] // tok
    length = ctx * tok
    per = QB // tok

    def kernel(x_ref, sr_ref, sc_ref, o_ref, l_ref):
        xs = x_ref[...].reshape(length, 256)
        ks = xs[:, 128:192]
        vs = xs[:, 192:256]
        for qb in range(length // QB):
            keys = (qb + 1) * QB
            rows = slice(qb * QB, (qb + 1) * QB)
            mask = block_mask(sr_ref[0], sc_ref[0, rows, :], qb, length)
            outs = []
            lses = []
            for h in range(hq):
                q = xs[rows, HS * h : HS * (h + 1)]
                s = jnp.where(mask, dot(q, ks[:keys], 1, 1) * SCALE, -1e30)
                top = jnp.max(s, axis=-1, keepdims=True)
                p = jnp.exp(s - top)
                total = jnp.sum(p, axis=-1, keepdims=True)
                o = dot(p.astype(BF), vs[:keys]) / total
                outs.append(o)
                lses.append(jnp.broadcast_to(top + jnp.log(total), (QB, HS)))
            for _ in range(hq, 2):
                outs.append(jnp.zeros((QB, HS), F32))
                lses.append(jnp.zeros((QB, HS), F32))
            o_ref[qb * per : (qb + 1) * per] = (
                jnp.concatenate(outs, axis=1).astype(BF).reshape(per, tok, 128)
            )
            l_ref[0, rows, :] = jnp.concatenate(lses, axis=1)

    return call(
        kernel,
        [sds((ctx, micro * tok, 128), BF), sds((micro, length, 128), F32)],
        [x, seg_row, seg_col],
        2 * micro * hq * length * length * HS,
        in_specs=[
            pl.BlockSpec((ctx, tok, 256), lambda m: (0, m, 0)),
            pl.BlockSpec((1, 1, length), lambda m: (m, 0, 0)),
            pl.BlockSpec((1, length, 1), lambda m: (m, 0, 0)),
        ],
        out_specs=(
            pl.BlockSpec((ctx, tok, 128), lambda m: (0, m, 0)),
            pl.BlockSpec((1, length, 128), lambda m: (m, 0, 0)),
        ),
        grid=(micro,),
    )


def attention_backward(x, d_out, out, lse, seg_row, seg_col, ctx, hq, tok):
    micro = x.shape[1] // tok
    length = ctx * tok
    per = QB // tok

    def kernel(x_ref, d_ref, o_ref, l_ref, sr_ref, sc_ref, dx_ref, dk_ref, dv_ref):
        xs = x_ref[...].reshape(length, 256)
        ks = xs[:, 128:192]
        vs = xs[:, 192:256]
        ds_all = d_ref[...].reshape(length, 128)
        os_all = o_ref[...].reshape(length, 128)
        dk_ref[...] = jnp.zeros((length, HS), F32)
        dv_ref[...] = jnp.zeros((length, HS), F32)
        for qb in range(length // QB):
            keys = (qb + 1) * QB
            rows = slice(qb * QB, (qb + 1) * QB)
            mask = block_mask(sr_ref[0], sc_ref[0, rows, :], qb, length)
            dqs = []
            for h in range(hq):
                cols = slice(HS * h, HS * (h + 1))
                q = xs[rows, cols]
                do = ds_all[rows, cols]
                delta = jnp.sum(
                    do.astype(F32) * os_all[rows, cols].astype(F32), axis=-1, keepdims=True
                )
                s = dot(q, ks[:keys], 1, 1) * SCALE - l_ref[0, rows, HS * h : HS * h + 1]
                p = jnp.exp(jnp.where(mask, s, -1e30))
                dp = dot(do, vs[:keys], 1, 1)
                ds = (p * (dp - delta) * SCALE).astype(BF)
                dqs.append(dot(ds, ks[:keys]))
                dk_ref[:keys] += dot(ds, q, 0, 0)
                dv_ref[:keys] += dot(p.astype(BF), do, 0, 0)
            for _ in range(hq, 2):
                dqs.append(jnp.zeros((QB, HS), F32))
            dx_ref[qb * per : (qb + 1) * per, :, 0:128] = (
                jnp.concatenate(dqs, axis=1).astype(BF).reshape(per, tok, 128)
            )
        dx_ref[:, :, 128:256] = (
            jnp.concatenate([dk_ref[...], dv_ref[...]], axis=1)
            .astype(BF)
            .reshape(ctx, tok, 128)
        )

    return call(
        kernel,
        [sds((ctx, micro * tok, 256), BF)],
        [x, d_out, out, lse, seg_row, seg_col],
        5 * micro * hq * length * length * HS,
        in_specs=[
            pl.BlockSpec((ctx, tok, 256), lambda m: (0, m, 0)),
            pl.BlockSpec((ctx, tok, 128), lambda m: (0, m, 0)),
            pl.BlockSpec((ctx, tok, 128), lambda m: (0, m, 0)),
            pl.BlockSpec((1, length, 128), lambda m: (m, 0, 0)),
            pl.BlockSpec((1, 1, length), lambda m: (m, 0, 0)),
            pl.BlockSpec((1, length, 1), lambda m: (m, 0, 0)),
        ],
        out_specs=(pl.BlockSpec((ctx, tok, 256), lambda m: (0, m, 0)),),
        grid=(micro,),
        scratch=[pltpu.VMEM((length, HS), F32), pltpu.VMEM((length, HS), F32)],
    )[0]


def side_by_side(m_ref, ctx, hq):
    return jnp.concatenate([m_ref[i][:, : HS * hq] for i in range(ctx)], axis=1)


def output_forward(mixed, stream, packed, gains, chosen, ctx, hq, n, held):
    rows = stream.shape[0]

    def kernel(m_ref, x_ref, w_ref, t_ref, g_ref, c_ref, s_ref, n_ref, gate_ref):
        x = x_ref[...].astype(F32) + dot(side_by_side(m_ref, ctx, hq), w_ref[...])
        s_ref[...] = x
        normed = (x * inv_rms_of(x) * g_ref[1:2]).astype(BF)
        n_ref[...] = normed
        logits = dot(t_ref[...], normed, 0, 1)[:E]
        named = c_ref[...] > 0.0
        logits = jnp.where(named, logits, -1e30)
        top = jnp.max(logits, axis=0, keepdims=True)
        p = jnp.where(named, jnp.exp(logits - top), 0.0)
        gates = p / jnp.sum(p, axis=0, keepdims=True)
        for j in range(n):
            gate_ref[j] = gates[held * j : held * (j + 1)]

    outs = [sds((rows, D), F32), sds((rows, D), BF), sds((n, held, rows), F32)]
    return call(
        kernel,
        outs,
        [mixed, stream, packed, packed, gains, chosen],
        2 * rows * D * D,
        in_specs=[
            full(mixed.shape),
            full(stream.shape),
            pl.BlockSpec((D, D), lambda i: (0, 2)),
            pl.BlockSpec((D, 128), lambda i: (0, TAIL)),
            full(gains.shape),
            full(chosen.shape),
        ],
        out_specs=tuple(full(o.shape) for o in outs),
        grid=(1,),
    )


def by_core(x, shard):
    y = x.astype(BF).reshape(x.shape[0] // (2 * shard), 2, shard, x.shape[1])
    return [y[:, c].reshape(x.shape[0] // 2, x.shape[1]) for c in range(2)]


def norm_back(x, gain, d_normed):
    r = inv_rms_of(x)
    grad_gain = jnp.sum(d_normed * x * r, axis=0, keepdims=True)
    q = d_normed * gain
    dx = r * q - x * (r * r * r) * jnp.mean(x * q, axis=-1, keepdims=True)
    return dx, grad_gain


def output_backward(parts, d_gates, gates, g, stream, normed, mixed, packed, gains, ctx, hq, n, shard):
    rows = stream.shape[0]

    def kernel(p_ref, dg_ref, gt_ref, g_ref, x_ref, nm_ref, m_ref, w_ref, t_ref, gain_ref, g1_ref, dm_ref, gw_ref):
        gates_v = jnp.concatenate([gt_ref[j] for j in range(n)], axis=0)
        dgate_v = jnp.concatenate([dg_ref[j] for j in range(n)], axis=0)
        mean = jnp.sum(gates_v * dgate_v, axis=0, keepdims=True)
        d_logits = (gates_v * (dgate_v - mean)).astype(BF)
        d_logits = jnp.concatenate([d_logits, jnp.zeros((128 - E, rows), BF)], axis=0)
        router = t_ref[...]
        d_normed = dot(d_logits, router, 0, 1)
        for j in range(n):
            d_normed = d_normed + p_ref[j].astype(F32)
        x = x_ref[...]
        dx, grad_gain = norm_back(x, gain_ref[1:2], d_normed)
        g1 = g_ref[...].astype(F32) + dx
        g1_ref[...] = g1
        low = g1.astype(BF)
        dm = dot(low, w_ref[...], 1, 1).astype(BF)
        for i in range(ctx):
            part = dm[:, HS * hq * i : HS * hq * (i + 1)]
            if hq < 2:
                part = jnp.concatenate([part, jnp.zeros((rows, 128 - HS * hq), BF)], axis=1)
            dm_ref[i] = part
        grad_out = dot(side_by_side(m_ref, ctx, hq), low, 0, 0)
        for c, value in enumerate(by_core(grad_out, shard)):
            gw_ref[c, :, 0:D] = value
        grad_router = dot(nm_ref[...], d_logits, 0, 1)
        row = lax.broadcasted_iota(jnp.int32, (128, D), 0)
        cols = jnp.where(row == 33, jnp.broadcast_to(grad_gain, (128, D)), 0.0)
        for c, value in enumerate(by_core(grad_router + jnp.transpose(cols), shard)):
            gw_ref[c, :, D : D + 128] = value

    outs = [sds((rows, D), F32), sds((ctx, rows, 128), BF), sds((2, D // 2, D + 128), BF)]
    args = [parts, d_gates, gates, g, stream, normed, mixed, packed, packed, gains]
    in_specs = [full(a.shape) for a in args]
    in_specs[7] = pl.BlockSpec((D, D), lambda i: (0, 2))
    in_specs[8] = pl.BlockSpec((D, 128), lambda i: (0, TAIL))
    return call(
        kernel,
        outs,
        args,
        4 * rows * D * D,
        in_specs=in_specs,
        out_specs=tuple(full(o.shape) for o in outs),
        grid=(1,),
    )


def qkv_backward(dx, g1, stream, packed, gains, cos_t, sin_t, ctx, hq, shard):
    rows = g1.shape[0]
    dup = ctx // KEY_VALUE_HEADS

    def kernel(d_ref, g_ref, x_ref, w_ref, gain_ref, c_ref, s_ref, out_ref, gw_ref):
        x = x_ref[...].astype(F32)
        gain = gain_ref[0:1]
        normed = (x * inv_rms_of(x) * gain).astype(BF)
        cos_v = c_ref[...]
        sin_v = s_ref[...]
        queries = in_order([d_ref[i][:, : HS * hq] for i in range(ctx)])
        both = []
        for head in range(KEY_VALUE_HEADS):
            total = d_ref[head * dup][:, 128:256]
            if dup > 1:
                total = total.astype(F32)
                for r in range(1, dup):
                    total = total + d_ref[head * dup + r][:, 128:256].astype(F32)
            both.append(total)
        keys = in_order([t[:, :HS] for t in both])
        values = in_order([t[:, HS:] for t in both])
        d_normed = jnp.zeros((rows, D), F32)
        for i in range(8):
            if i < 4:
                y = queries[:, 256 * i : 256 * (i + 1)]
            elif i < 6:
                y = keys[:, 256 * (i - 4) : 256 * (i - 3)]
            else:
                y = values[:, 256 * (i - 6) : 256 * (i - 5)]
            if i < 6:
                y = y.astype(F32)
                y = y * cos_v - swap_halves(y) * sin_v
            lin = y.astype(BF)
            cols = slice(256 * i, 256 * (i + 1))
            d_normed = d_normed + dot(lin, w_ref[:, cols], 1, 1)
            for c, value in enumerate(by_core(dot(normed, lin, 0, 0), shard)):
                gw_ref[c, :, cols] = value
        back, grad_gain = norm_back(x, gain, d_normed)
        out_ref[...] = g_ref[...] + back
        row = lax.broadcasted_iota(jnp.int32, (128, D), 0)
        cols = jnp.where(row == 0, jnp.broadcast_to(grad_gain, (128, D)), 0.0)
        for c, value in enumerate(by_core(jnp.transpose(cols), shard)):
            gw_ref[c, :, 2 * D : 2 * D + 128] = value

    outs = [sds((rows, D), F32), sds((2, D // 2, 2 * D + 128), BF)]
    args = [dx, g1, stream, packed, gains, cos_t, sin_t]
    in_specs = [full(a.shape) for a in args]
    in_specs[3] = pl.BlockSpec((D, 2 * D), lambda i: (0, 0))
    return call(
        kernel,
        outs,
        args,
        8 * rows * D * D,
        in_specs=in_specs,
        out_specs=tuple(full(o.shape) for o in outs),
        grid=(1,),
    )


def pick_matrix(slot_row, rows):
    at = lax.broadcasted_iota(jnp.int32, (2 * SLOTS, rows), 0)
    return at == slot_row


def weight_specs(weights):
    return [
        pl.BlockSpec((1,) + w.shape[1:], lambda e: (e, 0, 0, 0)) for w in weights
    ]


def matrices(first_ref, second_ref):
    ctx, depth, _ = first_ref.shape[1:]
    half = F // ctx
    second = second_ref[0]
    return (
        first_ref[0].reshape(D, F),
        second[:, :depth].reshape(D, F),
        second[:, depth : depth + half].reshape(F, D // 2),
        second[:, depth + half :].reshape(F, D // 2),
    )


def experts_forward(x, gates, slots, weights, held):
    n, rows, _ = x.shape
    lanes = 2 * SLOTS


    def kernel(x_ref, g_ref, s_ref, w0, w1, out_ref, acc_ref, row_ref, eo_ref):
        e = pl.program_id(0)
        w_gate, w_up, down_l, down_r = matrices(w0, w1)
        for s in range(n):
            pick = pick_matrix(s_ref[s, pl.ds(e, 1), :], rows).astype(BF)
            row_ref[lanes * s : lanes * (s + 1), :] = dot(pick, x_ref[s]).astype(BF)
        rws = row_ref[...]
        ga = dot(rws, w_gate)
        up = dot(rws, w_up)
        hidden = (ga * jax.nn.sigmoid(ga) * up).astype(BF)
        eo_ref[:, : D // 2] = dot(hidden, down_l).astype(BF)
        eo_ref[:, D // 2 :] = dot(hidden, down_r).astype(BF)
        for s in range(n):
            pick = pick_matrix(s_ref[s, pl.ds(e, 1), :], rows)
            gated = jnp.where(pick, g_ref[s, pl.ds(e, 1), :], 0.0).astype(BF)
            add = dot(gated, eo_ref[lanes * s : lanes * (s + 1), :], 0, 0)

            @pl.when(e == 0)
            def _():
                acc_ref[s] = add.astype(F32)

            @pl.when((e > 0) & (e < held - 1))
            def _():
                acc_ref[s] = (acc_ref[s].astype(F32) + add).astype(F32)

            @pl.when(e == held - 1)
            def _():
                out_ref[s] = (acc_ref[s].astype(F32) + add).astype(BF)

    flops = 2 * held * n * (lanes * D * F * 3 + 2 * lanes * rows * D)
    return call(
        kernel,
        [sds(x.shape, BF)],
        [x, gates, slots] + list(weights),
        flops,
        in_specs=[full(x.shape), full(gates.shape), full(slots.shape)] + weight_specs(weights),
        out_specs=(full(x.shape),),
        grid=(held,),
        scratch=[
            pltpu.VMEM(x.shape, F32),
            pltpu.VMEM((n * lanes, D), BF),
            pltpu.VMEM((n * lanes, D), BF),
        ],
    )[0]


def experts_backward(x, g, gates, slots, weights, held):
    n, rows, _ = x.shape
    lanes = 2 * SLOTS


    def kernel(x_ref, gr_ref, g_ref, s_ref, w0, w1, *rest):
        dx_ref, dg_ref = rest[:2]
        first_grad, second_grad, acc_ref, row_ref, grow_ref = rest[2:]
        e = pl.program_id(0)
        w_gate, w_up, down_l, down_r = matrices(w0, w1)
        slot_gates = []
        for s in range(n):
            mine = slice(lanes * s, lanes * (s + 1))
            pick = pick_matrix(s_ref[s, pl.ds(e, 1), :], rows)
            low = pick.astype(BF)
            row_ref[mine, :] = dot(low, x_ref[s]).astype(BF)
            grow_ref[mine, :] = dot(low, gr_ref[s]).astype(BF)
            gated = jnp.where(pick, g_ref[s, pl.ds(e, 1), :], 0.0)
            slot_gates.append(jnp.sum(gated, axis=1, keepdims=True))
        gate = jnp.concatenate(slot_gates, axis=0)
        rws = row_ref[...]
        grows = grow_ref[...]
        ga = dot(rws, w_gate)
        up = dot(rws, w_up)
        sig = jax.nn.sigmoid(ga)
        act = ga * sig
        hidden_f = act * up
        hidden = hidden_f.astype(BF)
        dhg = dot(grows[:, : D // 2], down_l, 1, 1) + dot(grows[:, D // 2 :], down_r, 1, 1)
        d_gate = jnp.sum(hidden.astype(F32) * dhg, axis=1, keepdims=True)
        dh = dhg * gate
        dga = (dh * up * (sig * (1.0 + ga * (1.0 - sig)))).astype(BF)
        dup = (dh * act).astype(BF)
        drow = (dot(dga, w_gate, 1, 1) + dot(dup, w_up, 1, 1)).astype(BF)
        for s in range(n):
            mine = slice(lanes * s, lanes * (s + 1))
            pick = pick_matrix(s_ref[s, pl.ds(e, 1), :], rows)
            dg_ref[s, pl.ds(e, 1), :] = jnp.sum(
                jnp.where(pick, d_gate[mine], 0.0), axis=0, keepdims=True
            )
            add = dot(pick.astype(BF), drow[mine], 0, 0)

            @pl.when(e == 0)
            def _():
                acc_ref[s] = add

            @pl.when((e > 0) & (e < held - 1))
            def _():
                acc_ref[s] += add

            @pl.when(e == held - 1)
            def _():
                dx_ref[s] = (acc_ref[s] + add).astype(BF)

        dslot = (grows.astype(F32) * gate).astype(BF)
        ctx, depth, _ = first_grad.shape[1:]
        part = F // ctx
        first_grad[0] = dot(rws, dga, 0, 0).astype(BF).reshape(ctx, depth, F)
        second_grad[0, :, :depth, :] = dot(rws, dup, 0, 0).astype(BF).reshape(ctx, depth, F)
        for k in range(2):
            cols = dslot[:, D // 2 * k : D // 2 * (k + 1)]
            at_row = depth + part * k
            second_grad[0, :, at_row : at_row + part, :] = (
                dot(hidden, cols, 0, 0).astype(BF).reshape(ctx, part, D // 2)
            )

    outs = [sds(x.shape, BF), sds(gates.shape, F32)] + [sds(w.shape, BF) for w in weights]
    out_specs = [full(x.shape), full(gates.shape)] + weight_specs(weights)
    scratch = [
        pltpu.VMEM(x.shape, F32),
        pltpu.VMEM((n * lanes, D), BF),
        pltpu.VMEM((n * lanes, D), BF),
    ]
    flops = 2 * held * n * (lanes * D * F * 9 + 3 * lanes * rows * D)
    return call(
        kernel,
        outs,
        [x, g, gates, slots] + list(weights),
        flops,
        in_specs=[full(x.shape), full(g.shape), full(gates.shape), full(slots.shape)]
        + weight_specs(weights),
        out_specs=tuple(out_specs),
        grid=(held,),
        scratch=scratch,
    )


def attention_gradients(*parts):
    shard = parts[0].shape[1]
    kv = KEY_VALUE_HEADS * HS
    widths = (D, kv, kv, D, 128, 128)

    def kernel(w0, w1, s0, s1, *outs):
        for layer, (w_ref, s_ref) in enumerate(((w0, s0), (w1, s1))):
            w = w_ref[0].astype(F32)
            s = s_ref[0].astype(F32)
            for j in range(1, w_ref.shape[0]):
                w = w + w_ref[j].astype(F32)
                s = s + s_ref[j].astype(F32)
            outs[0][layer] = w[:, :D]
            outs[1][layer] = w[:, D : D + kv]
            outs[2][layer] = w[:, D + kv : 2 * D]
            outs[3][layer] = s[:, :D]
            outs[4][layer] = w[:, 2 * D :]
            outs[5][layer] = s[:, D:]

    outs = [sds((LAYERS, shard, w), F32) for w in widths]
    return call(
        kernel,
        outs,
        list(parts),
        0,
        in_specs=[full(x.shape) for x in parts],
        out_specs=tuple(full(o.shape) for o in outs),
        grid=(1,),
    )


def expert_gradients(layers, members):
    pairs = [x for pair in layers for x in pair]
    depth = pairs[0].shape[1]
    part = (pairs[1].shape[1] - depth) // 2
    holders = pairs[0].shape[0] // members

    def kernel(*refs):
        ins, (gate_ref, up_ref, down_ref) = refs[:4], refs[4:]
        for layer in range(LAYERS):
            first, second = [
                functools.reduce(
                    lambda x, y: x + y, [r[j, 0].astype(F32) for j in range(holders)]
                )
                for r in ins[2 * layer : 2 * layer + 2]
            ]
            gate_ref[layer, 0] = first
            up_ref[layer, 0] = second[:depth]
            down_ref[layer, 0, :, : D // 2] = second[depth : depth + part]
            down_ref[layer, 0, :, D // 2 :] = second[depth + part :]

    args = [x.reshape((holders, members) + x.shape[1:]) for x in pairs]
    outs = [
        sds((LAYERS, members, depth, F), F32),
        sds((LAYERS, members, depth, F), F32),
        sds((LAYERS, members, part, D), F32),
    ]
    return call(
        kernel,
        outs,
        args,
        0,
        in_specs=[
            pl.BlockSpec((holders, 1) + x.shape[2:], lambda e: (0, e, 0, 0)) for x in args
        ],
        out_specs=tuple(
            pl.BlockSpec((LAYERS, 1) + o.shape[2:], lambda e: (0, e, 0, 0)) for o in outs
        ),
        grid=(members,),
    )


def per_device(
    sizes,
    hidden_in,
    grad_out,
    segments,
    routes,
    attn_gain,
    w_query,
    key_weight,
    value_weight,
    w_output,
    ffn_gain,
    w_router,
    w_gate,
    w_up,
    w_down,
):
    micro, tok, _ = hidden_in.shape
    rows = micro * tok
    grp_size, ctx, planes = sizes
    hq = QUERY_HEADS // ctx
    held = 2 * grp_size
    every = ("grp", "zq", "zp", "core")
    line = ("zq", "zp", "core")
    core = lax.axis_index("core")
    ctx_index = (lax.axis_index("zq") * planes + lax.axis_index("zp")) * 2 + core
    shard = w_query.shape[1]

    def by_plane(x, axis, back=False):
        dims = (planes, grp_size, 2) if back else (grp_size, planes, 2)
        head, tail = x.shape[:axis], x.shape[axis + 1 :]
        y = jnp.swapaxes(x.reshape(head + dims + tail), axis, axis + 1)
        return y.reshape(x.shape)

    def pack(layer):
        return jnp.concatenate(
            [
                w_query[layer],
                key_weight[layer],
                value_weight[layer],
                w_output[layer],
                by_plane(w_router[layer], 1),
                attn_gain[layer][:, None],
                ffn_gain[layer][:, None],
                jnp.zeros((shard, 128 - E - 2), BF),
            ],
            axis=1,
        )

    ids_of = iter(range(1, 100))

    def move(*ops):
        return transfer(ops, next(ids_of), sizes)

    def swap(x):
        return lax.ppermute(x, "core", [(0, 1), (1, 0)])

    def second_shard(layer):
        down = w_down[layer]
        return jnp.concatenate([w_up[layer], down[:, :, : D // 2], down[:, :, D // 2 :]], axis=1)

    def along_line(w):
        copies = ctx // w.shape[0]
        w = jnp.tile(w, (copies, 1, 1)) if copies > 1 else w
        return lax.all_to_all(w, line, 0, 0, tiled=True)

    def plane_gather(w):
        return lax.all_gather(w[None], ("grp", "core"), axis=0, tiled=True)

    grad_rows = grad_out.reshape(rows, D)
    (gate_parts,) = move((w_gate[0], "line", "pick"))
    gate_parts, own_pack, own_second = lax.optimization_barrier(
        (gate_parts, pack(0), second_shard(0))
    )
    first, second_parts = move((own_pack, None, "packed"), (own_second, "line", "pick"))
    first, late_pack = lax.optimization_barrier((first, pack(1)))
    packed = [first.reshape(D, -1), lax.all_gather(late_pack, every, axis=0, tiled=True)]
    weights = [[plane_gather(gate_parts), plane_gather(second_parts)], None]

    own_segments = lax.dynamic_slice_in_dim(segments, ctx_index * tok, tok, axis=1)
    prompt = jnp.sum((segments == 0).astype(jnp.int32), axis=1, dtype=jnp.int32)
    before = jnp.sum(
        (segments[:, None, :] < own_segments[:, :, None]).astype(jnp.int32),
        axis=2,
        dtype=jnp.int32,
    )
    places = ctx_index * tok + jnp.arange(tok, dtype=jnp.int32)[None, :]
    places = jnp.where(own_segments == 0, places, prompt[:, None] + places - before)
    places = places.reshape(rows).astype(F32)
    lane = jnp.arange(256, dtype=jnp.int32)
    freqs = jnp.exp(
        (lane % (HS // 2)).astype(F32) * (-2.0 * math.log(10000.0) / HS)
    )
    angles = places[:, None] * freqs[None, :]
    sign = jnp.where((lane % HS) < HS // 2, -1.0, 1.0)[None, :]
    cos_t = jnp.cos(angles)
    sin_t = jnp.sin(angles) * sign
    seg_row = segments[:, None, :]
    seg_col = segments[:, :, None]

    flat = routes.reshape(rows, TOP)
    ids = by_plane(jnp.arange(E, dtype=jnp.int32), 0)
    chosen = jnp.any(ids[:, None, None] == flat[None, :, :], axis=2)
    marks = chosen.astype(BF).reshape(E, micro, tok)
    earlier = (
        jnp.arange(tok)[:, None] < jnp.arange(tok)[None, :]
    ).astype(BF)
    rank = jnp.einsum("emt,ts->ems", marks, earlier, preferred_element_type=F32)
    slot = rank.astype(jnp.int32) + SLOTS * jnp.arange(micro, dtype=jnp.int32)[None, :, None]
    slot = jnp.where(chosen, slot.reshape(E, rows), -1)

    slot = slot.reshape(planes, held, rows)
    chosen_f = chosen.astype(F32)

    saved = []
    parts = (hidden_in.reshape(rows, D),)
    for layer in range(LAYERS):
        got = qkv_forward(parts, packed[layer], cos_t, sin_t, ctx, hq)
        qkv, gains = got[0], got[1]
        stream = parts[0] if layer == 0 else got[2]
        (heads,) = move((qkv, "line", "own"))
        out, lse = attention_forward(heads, seg_row, seg_col, ctx, hq, tok)
        (mixed,) = move((out, "line", "own"))
        stream1, normed, gates = output_forward(
            mixed, stream, packed[layer], gains, chosen_f, ctx, hq, planes, held
        )
        ops = [(normed, "tok", "all"), (gates, "tok", "own")]
        if layer == 0:
            xs, gates_here, slots_here, late_gate = move(
                *ops, (slot, "tok", "own"), (w_gate[1], "line", "pick")
            )
            late_second, xs = lax.optimization_barrier((second_shard(1), xs))
            late_second = along_line(late_second)
            late_gate = plane_gather(late_gate)
        else:
            xs, gates_here, last_g = move(*ops, (grad_rows, "tok", "all"))
        saved.append((stream, heads, out, lse, mixed, stream1, normed, gates, gains, xs, gates_here))
        sent = experts_forward(xs, gates_here, slots_here, weights[layer], held)
        if layer == 0:
            sent, late_second = lax.optimization_barrier((sent, late_second))
            (came,) = move((sent, "tok", "own"))
            weights[1] = [late_gate, plane_gather(late_second)]
            parts = (stream1, came)

    sent, last_g = lax.optimization_barrier((sent, last_g))
    final_sum = lax.psum_scatter(sent, "zp", scatter_dimension=0, tiled=True)[0]
    last_stream = stream1

    def plane_scatter(r):
        return lax.psum_scatter(r, ("grp", "core"), scatter_dimension=0, tiled=True)[0]

    def between_cores(x):
        theirs = lax.dynamic_index_in_dim(x, 1 - core, 0, keepdims=False)
        return with_other(x, swap(theirs))

    def with_other(x, came):
        ours = lax.dynamic_index_in_dim(x, core, 0, keepdims=False)
        return by_owner((ours.astype(F32) + came.astype(F32)).astype(BF))

    def by_owner(x):
        return x.reshape(grp_size, ctx // 2, shard, x.shape[1])

    def over_grp(x):
        return jnp.sum(x.astype(F32), axis=0).astype(BF)

    g = grad_rows
    for layer in reversed(range(LAYERS)):
        stream, heads, out, lse, mixed, stream1, normed, gates, gains, xs, gates_here = saved[layer]
        last = layer == LAYERS - 1
        if last:
            gs = last_g
        else:
            gs, last_small, came = move(
                (g.astype(BF), "tok", "all"), (over_grp(small), "z", "own"), (wide, "sib", "own")
            )
            wide = with_other(wide, came)
            gs, last_second = lax.optimization_barrier((gs, last_experts[1]))
            last_second = lax.all_to_all(last_second, line, 0, 0, tiled=True)
        res = experts_backward(xs, gs, gates_here, slots_here, weights[layer], held)
        if not last:
            *res, last_second = lax.optimization_barrier((*res, last_second))
        if last:
            *res, final_sum = lax.optimization_barrier((*res, final_sum))
        second_grads = plane_scatter(res[3])
        back = [(res[0], "tok", "own"), (res[1], "tok", "own")]
        if last:
            d_parts, d_gates = move(*back)
            gate_grads, d_parts = lax.optimization_barrier((res[2], d_parts))
            last_experts = [plane_scatter(gate_grads), second_grads]
        else:
            experts = [plane_scatter(res[2]), second_grads]
            d_parts, d_gates, last_wide = move(*back, (wide, "g", "own"))
        g1, d_mixed, small = output_backward(
            d_parts, d_gates, gates, g, stream1, normed, mixed, packed[layer], gains,
            ctx, hq, planes, shard,
        )
        ops = [(d_mixed, "line", "own"), (small, "sib", "own")]
        if last:
            d_out, came = move(*ops)
        else:
            d_out, came, last_wide = move(*ops, (over_grp(last_wide), "z", "own"))
        small = with_other(small, came)
        dx = attention_backward(heads, d_out, out, lse, seg_row, seg_col, ctx, hq, tok)
        ops = [(dx, "line", "own"), (small, "g", "own")]
        if last:
            dx, small = move(*ops)
        else:
            dx, small, last_gate = move(*ops, (last_experts[0], "line", "own"))
        g, wide = qkv_backward(
            dx, g1, stream, packed[layer], gains, cos_t, sin_t, ctx, hq, shard
        )
    hidden_out = (last_stream + final_sum.astype(F32)).astype(BF).reshape(micro, tok, D)
    first_wide, first_second, first_small = move(
        (between_cores(wide), "g", "own"),
        (experts[1], "line", "own"),
        (over_grp(small), "z", "own"),
    )
    first_wide, first_gate = move(
        (over_grp(first_wide), "z", "own"), (experts[0], "line", "own")
    )

    grads = attention_gradients(first_wide, last_wide, first_small, last_small)
    gq, gk, gv, go, gain_tail, tail = grads
    tops = expert_gradients(
        [(first_gate, first_second), (last_gate, last_second)], 2 * planes
    )
    return (
        hidden_out,
        g.reshape(micro, tok, D),
        gain_tail[:, :, 0],
        gq,
        gk,
        gv,
        go,
        tail[:, :, 33],
        by_plane(tail[:, :, :E], 2, back=True),
        *tops,
    )


def solution(mesh):
    grp_size = mesh.shape["grp"]
    ctx = mesh.shape["ctx"]
    planes = E // grp_size // 2
    fine = Mesh(
        mesh.devices.reshape(grp_size, ctx // (2 * planes), planes, 2),
        ("grp", "zq", "zp", "core"),
    )
    line = ("zq", "zp", "core")
    every = ("grp",) + line
    row = P("grp", line, None)
    placed = (
        row,
        row,
        P("grp", None),
        row,
        P(None, every),
        P(None, every, None),
        P(None, every, None),
        P(None, every, None),
        P(None, every, None),
        P(None, every),
        P(None, every, None),
        P(None, "grp", line, None),
        P(None, "grp", line, None),
        P(None, "grp", line, None),
    )
    return jax.shard_map(
        functools.partial(per_device, (grp_size, ctx, planes)),
        mesh=fine,
        in_specs=placed,
        out_specs=(
            row,
            row,
            P(None, every),
            P(None, every, None),
            P(None, every, None),
            P(None, every, None),
            P(None, every, None),
            P(None, every),
            P(None, every, None),
            P(None, "grp", line, None),
            P(None, "grp", line, None),
            P(None, "grp", line, None),
        ),
        check_vma=False,
    )
```

```python
import functools
import math

import jax
import jax.numpy as jnp
from jax import lax
from jax.experimental import pallas as pl
from jax.experimental.pallas import tpu as pltpu
from jax.sharding import Mesh, PartitionSpec as P

D = 1024
QUERY_HEADS = 16
KEY_VALUE_HEADS = 8
HS = 64
E = 32
F = 512
TOP = 8
LAYERS = 2
CAP = 42
SLOTS = 48
EPSILON = 1e-06
SCALE = float(HS) ** (-0.5)
QB = 256
BF = jnp.bfloat16
F32 = jnp.float32
MESH = pl.DeviceIdType.MESH
PIECES = 8
VMEM_BYTES = 58 * 1024 * 1024
TAIL = 3 * D // 128


def dot(a, b, ca=1, cb=0):
    return lax.dot_general(a, b, (((ca,), (cb,)), ((), ())), preferred_element_type=F32)


def call(kernel, outs, args, flops, in_specs, out_specs, grid, scratch=(), cid=None):
    nbytes = sum(a.size * a.dtype.itemsize for a in args)
    nbytes += sum(math.prod(o.shape) * jnp.dtype(o.dtype).itemsize for o in outs)
    extra = {} if cid is None else {"collective_id": cid, "has_side_effects": True}
    return pl.pallas_call(
        kernel,
        out_shape=tuple(outs),
        scratch_shapes=list(scratch),
        in_specs=in_specs,
        out_specs=out_specs,
        grid=grid,
        compiler_params=pltpu.CompilerParams(vmem_limit_bytes=VMEM_BYTES, **extra),
        cost_estimate=pl.CostEstimate(
            flops=int(flops), bytes_accessed=int(nbytes), transcendentals=0
        ),
    )(*args)


def sds(shape, dtype):
    return jax.ShapeDtypeStruct(tuple(shape), dtype)


def full(shape):
    n = len(shape)
    return pl.BlockSpec(tuple(shape), lambda *_: (0,) * n)


def size_of(group, sizes):
    grp_size, ctx, planes = sizes
    return {"g": grp_size, "tok": planes, "line": ctx, "z": ctx // 2, "sib": 2}[group]


def place_in(group, sizes):
    planes = sizes[2]
    n = size_of(group, sizes)
    zp = lax.axis_index("zp")
    zz = lax.axis_index("zq") * planes + zp
    core = lax.axis_index("core")
    if group == "g":
        return n, lax.axis_index("grp"), lambda p: {"grp": p}
    if group == "tok":
        return n, zp, lambda p: {"zp": p}
    if group == "line":
        return (
            n,
            zz * 2 + core,
            lambda p: {
                "zq": p // (2 * planes),
                "zp": lax.rem(p // 2, planes),
                "core": lax.rem(p, 2),
            },
        )
    if group == "z":
        return n, zz, lambda p: {"zq": p // planes, "zp": lax.rem(p, planes)}
    return n, core, lambda p: {"core": p}


def transfer(ops, cid, sizes):
    grp_size, ctx, _ = sizes
    groups = []
    for _, group, what in ops:
        for name in ("z", "g", "sib") if what == "packed" else (group,):
            if name not in groups:
                groups.append(name)
    shapes = []
    sems = []
    total_sems = 0
    for x, group, what in ops:
        sems.append(total_sems)
        if what == "packed":
            shapes.append(sds((grp_size, ctx) + x.shape, x.dtype))
            zs = ctx // 2
            total_sems += zs + zs * grp_size * 2
            continue
        n = size_of(group, sizes)
        total_sems += PIECES if group == "sib" else 2 * n if what == "all" else n
        rest = x.shape[1:] if group == "sib" else x.shape
        if what != "own":
            rest = (n,) + (x.shape if what == "all" else x.shape[2:])
        shapes.append(sds(rest, x.dtype))
    count = len(ops)

    def kernel(*refs):
        ins = refs[:count]
        outs = refs[count : count + len(shapes)]
        send, recv, local = refs[count + len(shapes) :]
        barrier = pltpu.get_barrier_semaphore()
        total = 0
        for group in groups:
            n, me, where = place_in(group, sizes)
            for k in range(1, n):
                pl.semaphore_signal(
                    barrier, inc=1, device_id=where(lax.rem(me + k, n)), device_id_type=MESH
                )
            total += n - 1
        pl.semaphore_wait(barrier, total)

        def remote(src, dst, at, place):
            copy = pltpu.make_async_remote_copy(
                src_ref=src,
                dst_ref=dst,
                send_sem=send.at[at],
                recv_sem=recv.at[at],
                device_id=place,
                device_id_type=MESH,
            )
            copy.start()
            return copy

        sib_place = {"core": 1 - lax.axis_index("core")}
        sent = []
        own_copies = []

        def start(i):
            _, group, what = ops[i]
            n, me, where = place_in(group or "g", sizes)
            out = outs[i]
            if what == "all":
                copy = pltpu.make_async_copy(ins[i], out.at[me], local.at[i])
                copy.start()
                own_copies.append(copy)

                @pl.when(me < n - 1)
                def _():
                    hop(i, n, ins[i], me, 1).start()

                @pl.when(me > 0)
                def _():
                    hop(i, n, ins[i], me, -1).start()

                return None
            if what == "packed":
                grp = lax.axis_index("grp")
                core = lax.axis_index("core")
                zs, zz, z_place = place_in("z", sizes)
                copy = pltpu.make_async_copy(ins[i], out.at[grp, zz * 2 + core], local.at[i])
                copy.start()
                along = []
                for k in range(1, zs):
                    along.append(
                        remote(
                            ins[i],
                            out.at[grp, zz * 2 + core],
                            sems[i] + k,
                            z_place(lax.rem(zz + k, zs)),
                        )
                    )
                return (i, along, copy)
            if group == "sib":
                size = ins[i].shape[1] // PIECES
                for j in range(PIECES):
                    part = pl.ds(j * size, size)
                    sent.append(
                        remote(ins[i].at[1 - me, part], out.at[part], sems[i] + j, where(1 - me))
                    )
                return None
            copies = []
            for k in range(1, n):
                peer = lax.rem(me + k, n)
                if what == "own":
                    src = ins[i].at[peer]
                else:
                    src = ins[i].at[what, lax.rem(peer, ins[i].shape[1])]
                copies.append(remote(src, out.at[me], sems[i] + k, where(peer)))
            if what == "own":
                src = ins[i].at[me]
            else:
                src = ins[i].at[what, lax.rem(me, ins[i].shape[1])]
            copy = pltpu.make_async_copy(src, out.at[me], local.at[i])
            copy.start()
            own_copies.append(copy)
            sent.extend(copies)
            return None

        def hop(i, n, src, block, way):
            _, me, where = place_in(ops[i][1], sizes)
            return pltpu.make_async_remote_copy(
                src_ref=src,
                dst_ref=outs[i].at[block],
                send_sem=send.at[sems[i] + block + (0 if way > 0 else n)],
                recv_sem=recv.at[sems[i] + block],
                device_id=where(me + way),
                device_id_type=MESH,
            )

        def finish_all(i):
            n, me, _ = place_in(ops[i][1], sizes)
            out = outs[i]
            for far in range(1, n):
                low, high = me - far, me + far

                @pl.when(low >= 0)
                def _():
                    hop(i, n, out.at[low], low, 1).wait_recv()

                    @pl.when(me < n - 1)
                    def _():
                        hop(i, n, out.at[low], low, 1).start()

                @pl.when(high <= n - 1)
                def _():
                    hop(i, n, out.at[high], high, -1).wait_recv()

                    @pl.when(me > 0)
                    def _():
                        hop(i, n, out.at[high], high, -1).start()

            for far in range(n):
                low, high = me - far, me + far

                @pl.when((low >= 0) & (me < n - 1))
                def _():
                    hop(i, n, ins[i] if far == 0 else out.at[low], low, 1).wait_send()

                @pl.when((high <= n - 1) & (me > 0))
                def _():
                    hop(i, n, ins[i] if far == 0 else out.at[high], high, -1).wait_send()

        def finish_packed(i, along, own):
            grp = lax.axis_index("grp")
            core = lax.axis_index("core")
            zs, zz, _ = place_in("z", sizes)
            out = outs[i]
            base = sems[i] + zs
            over = []

            def spread(j, at):
                for m in range(1, grp_size):
                    over.append(
                        (
                            remote(
                                out.at[at[0], at[1]],
                                out.at[at[0], at[1]],
                                base + j * grp_size + m,
                                {"grp": lax.rem(grp + m, grp_size)},
                            ),
                            j,
                            m,
                        )
                    )

            def to_core(j, m, at):
                sent.append(
                    remote(
                        out.at[at[0], at[1]],
                        out.at[at[0], at[1]],
                        base + zs * grp_size + j * grp_size + m,
                        sib_place,
                    )
                )

            own.wait()
            for j in range(zs):
                if j > 0:
                    along[j - 1].wait_recv()
                at = (grp, lax.rem(zz - j + zs, zs) * 2 + core)
                spread(j, at)
                to_core(j, 0, at)
            for copy, j, m in over:
                copy.wait_recv()
                at = (
                    lax.rem(grp - m + grp_size, grp_size),
                    lax.rem(zz - j + zs, zs) * 2 + core,
                )
                to_core(j, m, at)
            for copy in along:
                copy.wait_send()
            for copy, _, _ in over:
                copy.wait_send()

        pending = []
        for i in range(count):
            got = start(i)
            if got is not None:
                pending.append(got)
        for item in pending:
            finish_packed(*item)
        for i in range(count):
            if ops[i][2] == "all":
                finish_all(i)
        for copy in own_copies:
            copy.wait()
        for copy in sent:
            copy.wait()

    total = sum(math.prod(o.shape) * jnp.dtype(o.dtype).itemsize for o in shapes)
    any_spec = pl.BlockSpec(memory_space=pl.ANY)
    return pl.pallas_call(
        kernel,
        out_shape=tuple(shapes),
        in_specs=[any_spec] * count,
        out_specs=tuple([any_spec] * len(shapes)),
        scratch_shapes=[
            pltpu.SemaphoreType.DMA((total_sems,)),
            pltpu.SemaphoreType.DMA((total_sems,)),
            pltpu.SemaphoreType.DMA((count,)),
        ],
        compiler_params=pltpu.CompilerParams(collective_id=cid, has_side_effects=True),
        cost_estimate=pl.CostEstimate(
            flops=0, bytes_accessed=40 * int(total), transcendentals=0
        ),
    )(*[x for x, _, _ in ops])


ANY_SPEC = pl.BlockSpec(memory_space=pl.ANY)


class Carried:
    def __init__(self, ops, sizes):
        self.sizes = sizes
        self.ops = ops
        self.shapes = []
        self.first = []
        self.total = 0
        for x, group, what in ops:
            n = size_of(group, sizes)
            shape = x.shape if what == "own" else (n,) + x.shape[2:]
            self.shapes.append(sds(shape, x.dtype))
            self.first.append(self.total)
            self.total += n

    def scratch(self):
        if not self.ops:
            return []
        return [
            pltpu.SemaphoreType.DMA((self.total,)),
            pltpu.SemaphoreType.DMA((self.total,)),
            pltpu.SemaphoreType.DMA((len(self.ops),)),
        ]

    def enter(self, groups):
        barrier = pltpu.get_barrier_semaphore()
        total = 0
        for group in groups:
            n, me, where = place_in(group, self.sizes)
            for k in range(1, n):
                pl.semaphore_signal(
                    barrier, inc=1, device_id=where(lax.rem(me + k, n)), device_id_type=MESH
                )
            total += n - 1
        pl.semaphore_wait(barrier, total)

    def copies(self, ins, outs, sems):
        made = []
        for i, (_, group, what) in enumerate(self.ops):
            send, recv, local = sems
            n, me, where = place_in(group, self.sizes)

            def part(j, i=i, what=what):
                if what == "own":
                    return ins[i].at[j]
                return ins[i].at[what, lax.rem(j, ins[i].shape[1])]

            for k in range(1, n):
                peer = lax.rem(me + k, n)
                made.append(
                    pltpu.make_async_remote_copy(
                        src_ref=part(peer),
                        dst_ref=outs[i].at[me],
                        send_sem=send.at[self.first[i] + k],
                        recv_sem=recv.at[self.first[i] + k],
                        device_id=where(peer),
                        device_id_type=MESH,
                    )
                )
            made.append(pltpu.make_async_copy(part(me), outs[i].at[me], local.at[i]))
        return made


def head_copies(buf, out, sems, m, ctx, tok, sizes):
    send, recv, local = sems
    n, me, where = place_in("line", sizes)
    rows = pl.ds(m * tok, tok)
    made = []
    for k in range(1, n):
        peer = lax.rem(me + k, n)
        made.append(
            pltpu.make_async_remote_copy(
                src_ref=buf.at[m, peer],
                dst_ref=out.at[me, rows],
                send_sem=send.at[m * n + k],
                recv_sem=recv.at[m * n + k],
                device_id=where(peer),
                device_id_type=MESH,
            )
        )
    made.append(pltpu.make_async_copy(buf.at[m, me], out.at[me, rows], local.at[m]))
    return made


def head_scratch(micro, ctx, tok, width):
    return [
        pltpu.VMEM((micro, ctx, tok, width), BF),
        pltpu.SemaphoreType.DMA((micro * ctx,)),
        pltpu.SemaphoreType.DMA((micro * ctx,)),
        pltpu.SemaphoreType.DMA((micro,)),
    ]


def swap_halves(x):
    lane = lax.broadcasted_iota(jnp.int32, x.shape, 1)
    width = x.shape[1]
    up = pltpu.roll(x, width - HS // 2, 1)
    down = pltpu.roll(x, HS // 2, 1)
    return jnp.where((lane & (HS - 1)) < HS // 2, up, down)


def inv_rms_of(x):
    return lax.rsqrt(jnp.mean(x * x, axis=-1, keepdims=True) + EPSILON)


def in_order(parts):
    return parts[0] if len(parts) == 1 else jnp.concatenate(parts, axis=1)


def qkv_forward(stream_parts, packed, cos_t, sin_t, ctx, hq):
    first = len(stream_parts) == 1
    rows = stream_parts[0].shape[0]
    dup = ctx // KEY_VALUE_HEADS

    def kernel(*refs):
        if first:
            h_ref, w_ref, t_ref, c_ref, s_ref, out_ref, gains_ref = refs
            x = h_ref[...].astype(F32)
        else:
            h_ref, p_ref, w_ref, t_ref, c_ref, s_ref, out_ref, gains_ref, x_ref = refs
            x = h_ref[...]
            for j in range(p_ref.shape[0]):
                x = x + p_ref[j].astype(F32)
            x_ref[...] = x
        gains = jnp.transpose(t_ref[...].astype(F32))[32:40]
        gains_ref[...] = gains
        normed = (x * inv_rms_of(x) * gains[0:1]).astype(BF)
        cos_v = c_ref[...]
        sin_v = s_ref[...]
        parts = []
        for i in range(8):
            y = dot(normed, w_ref[:, 256 * i : 256 * (i + 1)])
            if i < 6:
                y = y * cos_v + swap_halves(y) * sin_v
            parts.append(y.astype(BF))
        queries, keys, values = in_order(parts[:4]), in_order(parts[4:6]), in_order(parts[6:])
        for i in range(ctx):
            mine = [queries[:, HS * hq * i : HS * hq * (i + 1)]]
            if hq < 2:
                mine.append(jnp.zeros((rows, 128 - HS * hq), BF))
            kv = i // dup
            mine.append(keys[:, HS * kv : HS * (kv + 1)])
            mine.append(values[:, HS * kv : HS * (kv + 1)])
            out_ref[i] = in_order(mine)

    args = list(stream_parts) + [packed, packed, cos_t, sin_t]
    in_specs = [full(a.shape) for a in stream_parts] + [
        pl.BlockSpec((D, 2 * D), lambda i: (0, 0)),
        pl.BlockSpec((D, 128), lambda i: (0, TAIL)),
        full(cos_t.shape),
        full(sin_t.shape),
    ]
    outs = [sds((ctx, rows, 256), BF), sds((8, D), F32)]
    if not first:
        outs.append(sds((rows, D), F32))
    return call(
        kernel,
        outs,
        args,
        4 * rows * D * D,
        in_specs=in_specs,
        out_specs=tuple(full(o.shape) for o in outs),
        grid=(1,),
    )


def block_mask(seg_row, seg_col, qb, length):
    keys = (qb + 1) * QB
    qi = lax.broadcasted_iota(jnp.int32, (QB, keys), 0) + qb * QB
    ki = lax.broadcasted_iota(jnp.int32, (QB, keys), 1)
    sr = seg_row[:, :keys]
    return (ki <= qi) & ((sr == 0) | (sr == seg_col))


def attention_forward(x, seg_row, seg_col, ctx, hq, tok, sizes, cid):
    micro = x.shape[1] // tok
    length = ctx * tok
    per = QB // tok

    meet = Carried([], sizes)

    def kernel(x_ref, sr_ref, sc_ref, o_ref, l_ref, mixed_ref, buf, *sems):
        m = pl.program_id(0)
        xs = x_ref[...].reshape(length, 256)
        ks = xs[:, 128:192]
        vs = xs[:, 192:256]
        for qb in range(length // QB):
            keys = (qb + 1) * QB
            rows = slice(qb * QB, (qb + 1) * QB)
            mask = block_mask(sr_ref[0], sc_ref[0, rows, :], qb, length)
            outs = []
            lses = []
            for h in range(hq):
                q = xs[rows, HS * h : HS * (h + 1)]
                s = jnp.where(mask, dot(q, ks[:keys], 1, 1) * SCALE, -1e30)
                top = jnp.max(s, axis=-1, keepdims=True)
                p = jnp.exp(s - top)
                total = jnp.sum(p, axis=-1, keepdims=True)
                o = dot(p.astype(BF), vs[:keys]) / total
                outs.append(o)
                lses.append(jnp.broadcast_to(top + jnp.log(total), (QB, HS)))
            for _ in range(hq, 2):
                outs.append(jnp.zeros((QB, HS), F32))
                lses.append(jnp.zeros((QB, HS), F32))
            done = jnp.concatenate(outs, axis=1).astype(BF).reshape(per, tok, 128)
            o_ref[qb * per : (qb + 1) * per] = done
            buf[m, qb * per : (qb + 1) * per] = done
            l_ref[0, rows, :] = jnp.concatenate(lses, axis=1)

        @pl.when(m == 0)
        def _():
            meet.enter(["line"])

        for copy in head_copies(buf, mixed_ref, sems, m, ctx, tok, sizes):
            copy.start()

        @pl.when(m == micro - 1)
        def _():
            for j in range(micro):
                for copy in head_copies(buf, mixed_ref, sems, j, ctx, tok, sizes):
                    copy.wait()

    return call(
        kernel,
        [
            sds((ctx, micro * tok, 128), BF),
            sds((micro, length, 128), F32),
            sds((ctx, micro * tok, 128), BF),
        ],
        [x, seg_row, seg_col],
        2 * micro * hq * length * length * HS,
        in_specs=[
            pl.BlockSpec((ctx, tok, 256), lambda m: (0, m, 0)),
            pl.BlockSpec((1, 1, length), lambda m: (m, 0, 0)),
            pl.BlockSpec((1, length, 1), lambda m: (m, 0, 0)),
        ],
        out_specs=(
            pl.BlockSpec((ctx, tok, 128), lambda m: (0, m, 0)),
            pl.BlockSpec((1, length, 128), lambda m: (m, 0, 0)),
            ANY_SPEC,
        ),
        grid=(micro,),
        scratch=head_scratch(micro, ctx, tok, 128),
        cid=cid,
    )


def attention_backward(x, d_out, out, lse, seg_row, seg_col, ctx, hq, tok, ops, sizes, cid):
    micro = x.shape[1] // tok
    length = ctx * tok
    per = QB // tok

    carry = Carried(ops, sizes)
    count = len(ops)

    def kernel(x_ref, d_ref, o_ref, l_ref, sr_ref, sc_ref, *rest):
        ins, out_ref, outs = rest[:count], rest[count], rest[count + 1 : 2 * count + 1]
        dk_ref, dv_ref, buf, *sems = rest[2 * count + 1 :]
        sems, carry_sems = sems[:3], sems[3:]
        m = pl.program_id(0)
        dx_ref = buf.at[m]

        @pl.when(m == 0)
        def _():
            carry.enter(["line"] + [group for _, group, _ in ops if group != "line"])
            for copy in carry.copies(ins, outs, carry_sems):
                copy.start()

        xs = x_ref[...].reshape(length, 256)
        ks = xs[:, 128:192]
        vs = xs[:, 192:256]
        ds_all = d_ref[...].reshape(length, 128)
        os_all = o_ref[...].reshape(length, 128)
        dk_ref[...] = jnp.zeros((length, HS), F32)
        dv_ref[...] = jnp.zeros((length, HS), F32)
        for qb in range(length // QB):
            keys = (qb + 1) * QB
            rows = slice(qb * QB, (qb + 1) * QB)
            mask = block_mask(sr_ref[0], sc_ref[0, rows, :], qb, length)
            dqs = []
            for h in range(hq):
                cols = slice(HS * h, HS * (h + 1))
                q = xs[rows, cols]
                do = ds_all[rows, cols]
                delta = jnp.sum(
                    do.astype(F32) * os_all[rows, cols].astype(F32), axis=-1, keepdims=True
                )
                s = dot(q, ks[:keys], 1, 1) * SCALE - l_ref[0, rows, HS * h : HS * h + 1]
                p = jnp.exp(jnp.where(mask, s, -1e30))
                dp = dot(do, vs[:keys], 1, 1)
                ds = (p * (dp - delta) * SCALE).astype(BF)
                dqs.append(dot(ds, ks[:keys]))
                dk_ref[:keys] += dot(ds, q, 0, 0)
                dv_ref[:keys] += dot(p.astype(BF), do, 0, 0)
            for _ in range(hq, 2):
                dqs.append(jnp.zeros((QB, HS), F32))
            dx_ref[qb * per : (qb + 1) * per, :, 0:128] = (
                jnp.concatenate(dqs, axis=1).astype(BF).reshape(per, tok, 128)
            )
        dx_ref[:, :, 128:256] = (
            jnp.concatenate([dk_ref[...], dv_ref[...]], axis=1)
            .astype(BF)
            .reshape(ctx, tok, 128)
        )
        for copy in head_copies(buf, out_ref, sems, m, ctx, tok, sizes):
            copy.start()

        @pl.when(m == micro - 1)
        def _():
            for j in range(micro):
                for copy in head_copies(buf, out_ref, sems, j, ctx, tok, sizes):
                    copy.wait()
            for copy in carry.copies(ins, outs, carry_sems):
                copy.wait()

    return call(
        kernel,
        [sds((ctx, micro * tok, 256), BF)] + carry.shapes,
        [x, d_out, out, lse, seg_row, seg_col] + [o[0] for o in ops],
        5 * micro * hq * length * length * HS,
        in_specs=[
            pl.BlockSpec((ctx, tok, 256), lambda m: (0, m, 0)),
            pl.BlockSpec((ctx, tok, 128), lambda m: (0, m, 0)),
            pl.BlockSpec((ctx, tok, 128), lambda m: (0, m, 0)),
            pl.BlockSpec((1, length, 128), lambda m: (m, 0, 0)),
            pl.BlockSpec((1, 1, length), lambda m: (m, 0, 0)),
            pl.BlockSpec((1, length, 1), lambda m: (m, 0, 0)),
        ]
        + [ANY_SPEC] * count,
        out_specs=tuple([ANY_SPEC] * (count + 1)),
        grid=(micro,),
        scratch=[pltpu.VMEM((length, HS), F32), pltpu.VMEM((length, HS), F32)]
        + head_scratch(micro, ctx, tok, 256)
        + carry.scratch(),
        cid=cid,
    )


def side_by_side(m_ref, ctx, hq):
    return jnp.concatenate([m_ref[i][:, : HS * hq] for i in range(ctx)], axis=1)


def output_forward(mixed, stream, packed, gains, chosen, ctx, hq, n, held):
    rows = stream.shape[0]

    def kernel(m_ref, x_ref, w_ref, t_ref, g_ref, c_ref, s_ref, n_ref, gate_ref):
        x = x_ref[...].astype(F32) + dot(side_by_side(m_ref, ctx, hq), w_ref[...])
        s_ref[...] = x
        normed = (x * inv_rms_of(x) * g_ref[1:2]).astype(BF)
        n_ref[...] = normed
        logits = dot(t_ref[...], normed, 0, 1)[:E]
        named = c_ref[...] > 0.0
        logits = jnp.where(named, logits, -1e30)
        top = jnp.max(logits, axis=0, keepdims=True)
        p = jnp.where(named, jnp.exp(logits - top), 0.0)
        gates = p / jnp.sum(p, axis=0, keepdims=True)
        for j in range(n):
            gate_ref[j] = gates[held * j : held * (j + 1)]

    outs = [sds((rows, D), F32), sds((rows, D), BF), sds((n, held, rows), F32)]
    return call(
        kernel,
        outs,
        [mixed, stream, packed, packed, gains, chosen],
        2 * rows * D * D,
        in_specs=[
            full(mixed.shape),
            full(stream.shape),
            pl.BlockSpec((D, D), lambda i: (0, 2)),
            pl.BlockSpec((D, 128), lambda i: (0, TAIL)),
            full(gains.shape),
            full(chosen.shape),
        ],
        out_specs=tuple(full(o.shape) for o in outs),
        grid=(1,),
    )


def by_core(x, shard):
    y = x.astype(BF).reshape(x.shape[0] // (2 * shard), 2, shard, x.shape[1])
    return [y[:, c].reshape(x.shape[0] // 2, x.shape[1]) for c in range(2)]


def norm_back(x, gain, d_normed):
    r = inv_rms_of(x)
    grad_gain = jnp.sum(d_normed * x * r, axis=0, keepdims=True)
    q = d_normed * gain
    dx = r * q - x * (r * r * r) * jnp.mean(x * q, axis=-1, keepdims=True)
    return dx, grad_gain


def output_backward(parts, d_gates, gates, g, stream, normed, mixed, packed, gains, ctx, hq, n, shard):
    rows = stream.shape[0]

    def kernel(p_ref, dg_ref, gt_ref, g_ref, x_ref, nm_ref, m_ref, w_ref, t_ref, gain_ref, g1_ref, dm_ref, gw_ref):
        gates_v = jnp.concatenate([gt_ref[j] for j in range(n)], axis=0)
        dgate_v = jnp.concatenate([dg_ref[j] for j in range(n)], axis=0)
        mean = jnp.sum(gates_v * dgate_v, axis=0, keepdims=True)
        d_logits = (gates_v * (dgate_v - mean)).astype(BF)
        d_logits = jnp.concatenate([d_logits, jnp.zeros((128 - E, rows), BF)], axis=0)
        router = t_ref[...]
        d_normed = dot(d_logits, router, 0, 1)
        for j in range(n):
            d_normed = d_normed + p_ref[j].astype(F32)
        x = x_ref[...]
        dx, grad_gain = norm_back(x, gain_ref[1:2], d_normed)
        g1 = g_ref[...].astype(F32) + dx
        g1_ref[...] = g1
        low = g1.astype(BF)
        dm = dot(low, w_ref[...], 1, 1).astype(BF)
        for i in range(ctx):
            part = dm[:, HS * hq * i : HS * hq * (i + 1)]
            if hq < 2:
                part = jnp.concatenate([part, jnp.zeros((rows, 128 - HS * hq), BF)], axis=1)
            dm_ref[i] = part
        grad_out = dot(side_by_side(m_ref, ctx, hq), low, 0, 0)
        for c, value in enumerate(by_core(grad_out, shard)):
            gw_ref[c, :, 0:D] = value
        grad_router = dot(nm_ref[...], d_logits, 0, 1)
        row = lax.broadcasted_iota(jnp.int32, (128, D), 0)
        cols = jnp.where(row == 33, jnp.broadcast_to(grad_gain, (128, D)), 0.0)
        for c, value in enumerate(by_core(grad_router + jnp.transpose(cols), shard)):
            gw_ref[c, :, D : D + 128] = value

    outs = [sds((rows, D), F32), sds((ctx, rows, 128), BF), sds((2, D // 2, D + 128), BF)]
    args = [parts, d_gates, gates, g, stream, normed, mixed, packed, packed, gains]
    in_specs = [full(a.shape) for a in args]
    in_specs[7] = pl.BlockSpec((D, D), lambda i: (0, 2))
    in_specs[8] = pl.BlockSpec((D, 128), lambda i: (0, TAIL))
    return call(
        kernel,
        outs,
        args,
        4 * rows * D * D,
        in_specs=in_specs,
        out_specs=tuple(full(o.shape) for o in outs),
        grid=(1,),
    )


def qkv_backward(dx, g1, stream, packed, gains, cos_t, sin_t, ctx, hq, shard):
    rows = g1.shape[0]
    dup = ctx // KEY_VALUE_HEADS

    def kernel(d_ref, g_ref, x_ref, w_ref, gain_ref, c_ref, s_ref, out_ref, gw_ref):
        x = x_ref[...].astype(F32)
        gain = gain_ref[0:1]
        normed = (x * inv_rms_of(x) * gain).astype(BF)
        cos_v = c_ref[...]
        sin_v = s_ref[...]
        queries = in_order([d_ref[i][:, : HS * hq] for i in range(ctx)])
        both = []
        for head in range(KEY_VALUE_HEADS):
            total = d_ref[head * dup][:, 128:256]
            if dup > 1:
                total = total.astype(F32)
                for r in range(1, dup):
                    total = total + d_ref[head * dup + r][:, 128:256].astype(F32)
            both.append(total)
        keys = in_order([t[:, :HS] for t in both])
        values = in_order([t[:, HS:] for t in both])
        d_normed = jnp.zeros((rows, D), F32)
        for i in range(8):
            if i < 4:
                y = queries[:, 256 * i : 256 * (i + 1)]
            elif i < 6:
                y = keys[:, 256 * (i - 4) : 256 * (i - 3)]
            else:
                y = values[:, 256 * (i - 6) : 256 * (i - 5)]
            if i < 6:
                y = y.astype(F32)
                y = y * cos_v - swap_halves(y) * sin_v
            lin = y.astype(BF)
            cols = slice(256 * i, 256 * (i + 1))
            d_normed = d_normed + dot(lin, w_ref[:, cols], 1, 1)
            for c, value in enumerate(by_core(dot(normed, lin, 0, 0), shard)):
                gw_ref[c, :, cols] = value
        back, grad_gain = norm_back(x, gain, d_normed)
        out_ref[...] = g_ref[...] + back
        row = lax.broadcasted_iota(jnp.int32, (128, D), 0)
        cols = jnp.where(row == 0, jnp.broadcast_to(grad_gain, (128, D)), 0.0)
        for c, value in enumerate(by_core(jnp.transpose(cols), shard)):
            gw_ref[c, :, 2 * D : 2 * D + 128] = value

    outs = [sds((rows, D), F32), sds((2, D // 2, 2 * D + 128), BF)]
    args = [dx, g1, stream, packed, gains, cos_t, sin_t]
    in_specs = [full(a.shape) for a in args]
    in_specs[3] = pl.BlockSpec((D, 2 * D), lambda i: (0, 0))
    return call(
        kernel,
        outs,
        args,
        8 * rows * D * D,
        in_specs=in_specs,
        out_specs=tuple(full(o.shape) for o in outs),
        grid=(1,),
    )


def pick_matrix(slot_row, rows):
    at = lax.broadcasted_iota(jnp.int32, (2 * SLOTS, rows), 0)
    return at == slot_row


def weight_specs(weights):
    return [
        pl.BlockSpec((1,) + w.shape[1:], lambda e: (e, 0, 0, 0)) for w in weights
    ]


def matrices(first_ref, second_ref):
    ctx, depth, _ = first_ref.shape[1:]
    half = F // ctx
    second = second_ref[0]
    return (
        first_ref[0].reshape(D, F),
        second[:, :depth].reshape(D, F),
        second[:, depth : depth + half].reshape(F, D // 2),
        second[:, depth + half :].reshape(F, D // 2),
    )


def experts_forward(x, gates, slots, weights, held, ops=(), sizes=None, cid=None):
    n, rows, _ = x.shape
    lanes = 2 * SLOTS


    carry = Carried(ops, sizes)
    count = len(ops)

    def kernel(x_ref, g_ref, s_ref, w0, w1, *rest):
        ins, out_ref, outs = rest[:count], rest[count], rest[count + 1 : 2 * count + 1]
        acc_ref, row_ref, eo_ref, *sems = rest[2 * count + 1 :]
        e = pl.program_id(0)
        if count:

            @pl.when(e == 0)
            def _():
                carry.enter(sorted(set(group for _, group, _ in ops)))
                for copy in carry.copies(ins, outs, sems):
                    copy.start()

        w_gate, w_up, down_l, down_r = matrices(w0, w1)
        for s in range(n):
            pick = pick_matrix(s_ref[s, pl.ds(e, 1), :], rows).astype(BF)
            row_ref[lanes * s : lanes * (s + 1), :] = dot(pick, x_ref[s]).astype(BF)
        rws = row_ref[...]
        ga = dot(rws, w_gate)
        up = dot(rws, w_up)
        hidden = (ga * jax.nn.sigmoid(ga) * up).astype(BF)
        eo_ref[:, : D // 2] = dot(hidden, down_l).astype(BF)
        eo_ref[:, D // 2 :] = dot(hidden, down_r).astype(BF)
        for s in range(n):
            pick = pick_matrix(s_ref[s, pl.ds(e, 1), :], rows)
            gated = jnp.where(pick, g_ref[s, pl.ds(e, 1), :], 0.0).astype(BF)
            add = dot(gated, eo_ref[lanes * s : lanes * (s + 1), :], 0, 0)

            @pl.when(e == 0)
            def _():
                acc_ref[s] = add.astype(F32)

            @pl.when((e > 0) & (e < held - 1))
            def _():
                acc_ref[s] = (acc_ref[s].astype(F32) + add).astype(F32)

            @pl.when(e == held - 1)
            def _():
                out_ref[s] = (acc_ref[s].astype(F32) + add).astype(BF)

        if count:

            @pl.when(e == held - 1)
            def _():
                for copy in carry.copies(ins, outs, sems):
                    copy.wait()

    flops = 2 * held * n * (lanes * D * F * 3 + 2 * lanes * rows * D)
    return call(
        kernel,
        [sds(x.shape, BF)] + carry.shapes,
        [x, gates, slots] + list(weights) + [o[0] for o in ops],
        flops,
        in_specs=[full(x.shape), full(gates.shape), full(slots.shape)]
        + weight_specs(weights)
        + [ANY_SPEC] * count,
        out_specs=tuple([full(x.shape)] + [ANY_SPEC] * count),
        grid=(held,),
        scratch=[
            pltpu.VMEM(x.shape, F32),
            pltpu.VMEM((n * lanes, D), BF),
            pltpu.VMEM((n * lanes, D), BF),
        ]
        + carry.scratch(),
        cid=cid,
    )


def experts_backward(x, g, gates, slots, weights, held):
    n, rows, _ = x.shape
    lanes = 2 * SLOTS


    def kernel(x_ref, gr_ref, g_ref, s_ref, w0, w1, *rest):
        dx_ref, dg_ref = rest[:2]
        first_grad, second_grad, acc_ref, row_ref, grow_ref = rest[2:]
        e = pl.program_id(0)
        w_gate, w_up, down_l, down_r = matrices(w0, w1)
        slot_gates = []
        for s in range(n):
            mine = slice(lanes * s, lanes * (s + 1))
            pick = pick_matrix(s_ref[s, pl.ds(e, 1), :], rows)
            low = pick.astype(BF)
            row_ref[mine, :] = dot(low, x_ref[s]).astype(BF)
            grow_ref[mine, :] = dot(low, gr_ref[s]).astype(BF)
            gated = jnp.where(pick, g_ref[s, pl.ds(e, 1), :], 0.0)
            slot_gates.append(jnp.sum(gated, axis=1, keepdims=True))
        gate = jnp.concatenate(slot_gates, axis=0)
        rws = row_ref[...]
        grows = grow_ref[...]
        ga = dot(rws, w_gate)
        up = dot(rws, w_up)
        sig = jax.nn.sigmoid(ga)
        act = ga * sig
        hidden_f = act * up
        hidden = hidden_f.astype(BF)
        dhg = dot(grows[:, : D // 2], down_l, 1, 1) + dot(grows[:, D // 2 :], down_r, 1, 1)
        d_gate = jnp.sum(hidden.astype(F32) * dhg, axis=1, keepdims=True)
        dh = dhg * gate
        dga = (dh * up * (sig * (1.0 + ga * (1.0 - sig)))).astype(BF)
        dup = (dh * act).astype(BF)
        drow = (dot(dga, w_gate, 1, 1) + dot(dup, w_up, 1, 1)).astype(BF)
        for s in range(n):
            mine = slice(lanes * s, lanes * (s + 1))
            pick = pick_matrix(s_ref[s, pl.ds(e, 1), :], rows)
            dg_ref[s, pl.ds(e, 1), :] = jnp.sum(
                jnp.where(pick, d_gate[mine], 0.0), axis=0, keepdims=True
            )
            add = dot(pick.astype(BF), drow[mine], 0, 0)

            @pl.when(e == 0)
            def _():
                acc_ref[s] = add

            @pl.when((e > 0) & (e < held - 1))
            def _():
                acc_ref[s] += add

            @pl.when(e == held - 1)
            def _():
                dx_ref[s] = (acc_ref[s] + add).astype(BF)

        dslot = (grows.astype(F32) * gate).astype(BF)
        ctx, depth, _ = first_grad.shape[1:]
        part = F // ctx
        both = dot(rws, jnp.concatenate([dga, dup], axis=1), 0, 0).astype(BF)
        first_grad[0] = both[:, :F].reshape(ctx, depth, F)
        second_grad[0, :, :depth, :] = both[:, F:].reshape(ctx, depth, F)
        down = dot(hidden, dslot, 0, 0).astype(BF)
        for k in range(2):
            at_row = depth + part * k
            second_grad[0, :, at_row : at_row + part, :] = down[
                :, D // 2 * k : D // 2 * (k + 1)
            ].reshape(ctx, part, D // 2)

    outs = [sds(x.shape, BF), sds(gates.shape, F32)] + [sds(w.shape, BF) for w in weights]
    out_specs = [full(x.shape), full(gates.shape)] + weight_specs(weights)
    scratch = [
        pltpu.VMEM(x.shape, F32),
        pltpu.VMEM((n * lanes, D), BF),
        pltpu.VMEM((n * lanes, D), BF),
    ]
    flops = 2 * held * n * (lanes * D * F * 9 + 3 * lanes * rows * D)
    return call(
        kernel,
        outs,
        [x, g, gates, slots] + list(weights),
        flops,
        in_specs=[full(x.shape), full(g.shape), full(gates.shape), full(slots.shape)]
        + weight_specs(weights),
        out_specs=tuple(out_specs),
        grid=(held,),
        scratch=scratch,
    )


def attention_gradients(*parts):
    shard = parts[0].shape[1]
    kv = KEY_VALUE_HEADS * HS
    widths = (D, kv, kv, D, 128, 128)

    def kernel(w0, w1, s0, s1, *outs):
        for layer, (w_ref, s_ref) in enumerate(((w0, s0), (w1, s1))):
            w = w_ref[0].astype(F32)
            s = s_ref[0].astype(F32)
            for j in range(1, w_ref.shape[0]):
                w = w + w_ref[j].astype(F32)
                s = s + s_ref[j].astype(F32)
            outs[0][layer] = w[:, :D]
            outs[1][layer] = w[:, D : D + kv]
            outs[2][layer] = w[:, D + kv : 2 * D]
            outs[3][layer] = s[:, :D]
            outs[4][layer] = w[:, 2 * D :]
            outs[5][layer] = s[:, D:]

    outs = [sds((LAYERS, shard, w), F32) for w in widths]
    return call(
        kernel,
        outs,
        list(parts),
        0,
        in_specs=[full(x.shape) for x in parts],
        out_specs=tuple(full(o.shape) for o in outs),
        grid=(1,),
    )


def expert_gradients(layers, members):
    pairs = [x for pair in layers for x in pair]
    depth = pairs[0].shape[1]
    part = (pairs[1].shape[1] - depth) // 2
    holders = pairs[0].shape[0] // members

    def kernel(*refs):
        ins, (gate_ref, up_ref, down_ref) = refs[:4], refs[4:]
        for layer in range(LAYERS):
            first, second = [
                functools.reduce(
                    lambda x, y: x + y, [r[j, 0].astype(F32) for j in range(holders)]
                )
                for r in ins[2 * layer : 2 * layer + 2]
            ]
            gate_ref[layer, 0] = first
            up_ref[layer, 0] = second[:depth]
            down_ref[layer, 0, :, : D // 2] = second[depth : depth + part]
            down_ref[layer, 0, :, D // 2 :] = second[depth + part :]

    args = [x.reshape((holders, members) + x.shape[1:]) for x in pairs]
    outs = [
        sds((LAYERS, members, depth, F), F32),
        sds((LAYERS, members, depth, F), F32),
        sds((LAYERS, members, part, D), F32),
    ]
    return call(
        kernel,
        outs,
        args,
        0,
        in_specs=[
            pl.BlockSpec((holders, 1) + x.shape[2:], lambda e: (0, e, 0, 0)) for x in args
        ],
        out_specs=tuple(
            pl.BlockSpec((LAYERS, 1) + o.shape[2:], lambda e: (0, e, 0, 0)) for o in outs
        ),
        grid=(members,),
    )


def per_device(
    sizes,
    hidden_in,
    grad_out,
    segments,
    routes,
    attn_gain,
    w_query,
    key_weight,
    value_weight,
    w_output,
    ffn_gain,
    w_router,
    w_gate,
    w_up,
    w_down,
):
    micro, tok, _ = hidden_in.shape
    rows = micro * tok
    grp_size, ctx, planes = sizes
    hq = QUERY_HEADS // ctx
    held = 2 * grp_size
    every = ("grp", "zq", "zp", "core")
    line = ("zq", "zp", "core")
    core = lax.axis_index("core")
    ctx_index = (lax.axis_index("zq") * planes + lax.axis_index("zp")) * 2 + core
    shard = w_query.shape[1]

    def by_plane(x, axis, back=False):
        dims = (planes, grp_size, 2) if back else (grp_size, planes, 2)
        head, tail = x.shape[:axis], x.shape[axis + 1 :]
        y = jnp.swapaxes(x.reshape(head + dims + tail), axis, axis + 1)
        return y.reshape(x.shape)

    def pack(layer):
        return jnp.concatenate(
            [
                w_query[layer],
                key_weight[layer],
                value_weight[layer],
                w_output[layer],
                by_plane(w_router[layer], 1),
                attn_gain[layer][:, None],
                ffn_gain[layer][:, None],
                jnp.zeros((shard, 128 - E - 2), BF),
            ],
            axis=1,
        )

    ids_of = iter(range(1, 100))

    def move(*ops):
        return transfer(ops, next(ids_of), sizes)

    def swap(x):
        return lax.ppermute(x, "core", [(0, 1), (1, 0)])

    def second_shard(layer):
        down = w_down[layer]
        return jnp.concatenate([w_up[layer], down[:, :, : D // 2], down[:, :, D // 2 :]], axis=1)

    def along_line(w):
        copies = ctx // w.shape[0]
        w = jnp.tile(w, (copies, 1, 1)) if copies > 1 else w
        return lax.all_to_all(w, line, 0, 0, tiled=True)

    def plane_gather(w):
        return lax.all_gather(w[None], ("grp", "core"), axis=0, tiled=True)

    grad_rows = grad_out.reshape(rows, D)
    (gate_parts,) = move((w_gate, "line", 0))
    gate_parts, own_pack, own_second = lax.optimization_barrier(
        (gate_parts, pack(0), second_shard(0))
    )
    first, second_parts = move((own_pack, None, "packed"), (own_second[None], "line", 0))
    first, late_pack = lax.optimization_barrier((first, pack(1)))
    packed = [first.reshape(D, -1), lax.all_gather(late_pack, every, axis=0, tiled=True)]
    weights = [[plane_gather(gate_parts), plane_gather(second_parts)], None]

    own_segments = lax.dynamic_slice_in_dim(segments, ctx_index * tok, tok, axis=1)
    prompt = jnp.sum((segments == 0).astype(jnp.int32), axis=1, dtype=jnp.int32)
    before = jnp.sum(
        (segments[:, None, :] < own_segments[:, :, None]).astype(jnp.int32),
        axis=2,
        dtype=jnp.int32,
    )
    places = ctx_index * tok + jnp.arange(tok, dtype=jnp.int32)[None, :]
    places = jnp.where(own_segments == 0, places, prompt[:, None] + places - before)
    places = places.reshape(rows).astype(F32)
    lane = jnp.arange(256, dtype=jnp.int32)
    freqs = jnp.exp(
        (lane % (HS // 2)).astype(F32) * (-2.0 * math.log(10000.0) / HS)
    )
    angles = places[:, None] * freqs[None, :]
    sign = jnp.where((lane % HS) < HS // 2, -1.0, 1.0)[None, :]
    cos_t = jnp.cos(angles)
    sin_t = jnp.sin(angles) * sign
    seg_row = segments[:, None, :]
    seg_col = segments[:, :, None]

    flat = routes.reshape(rows, TOP)
    ids = by_plane(jnp.arange(E, dtype=jnp.int32), 0)
    chosen = jnp.any(ids[:, None, None] == flat[None, :, :], axis=2)
    marks = chosen.astype(BF).reshape(E, micro, tok)
    earlier = (
        jnp.arange(tok)[:, None] < jnp.arange(tok)[None, :]
    ).astype(BF)
    rank = jnp.einsum("emt,ts->ems", marks, earlier, preferred_element_type=F32)
    slot = rank.astype(jnp.int32) + SLOTS * jnp.arange(micro, dtype=jnp.int32)[None, :, None]
    slot = jnp.where(chosen, slot.reshape(E, rows), -1)

    slot = slot.reshape(planes, held, rows)
    chosen_f = chosen.astype(F32)

    saved = []
    parts = (hidden_in.reshape(rows, D),)
    for layer in range(LAYERS):
        got = qkv_forward(parts, packed[layer], cos_t, sin_t, ctx, hq)
        qkv, gains = got[0], got[1]
        stream = parts[0] if layer == 0 else got[2]
        (heads,) = move((qkv, "line", "own"))
        out, lse, mixed = attention_forward(
            heads, seg_row, seg_col, ctx, hq, tok, sizes, next(ids_of)
        )
        stream1, normed, gates = output_forward(
            mixed, stream, packed[layer], gains, chosen_f, ctx, hq, planes, held
        )
        ops = [(normed, "tok", "all"), (gates, "tok", "own")]
        if layer == 0:
            xs, gates_here, slots_here, late_gate = move(
                *ops, (slot, "tok", "own"), (w_gate, "line", 1)
            )
            late_gate = plane_gather(late_gate)
        else:
            xs, gates_here, last_g = move(*ops, (grad_rows, "tok", "all"))
        saved.append((stream, heads, out, lse, mixed, stream1, normed, gates, gains, xs, gates_here))
        if layer == 0:
            sent, late_second = experts_forward(
                xs, gates_here, slots_here, weights[0], held,
                [(second_shard(1)[None], "line", 0)], sizes, next(ids_of),
            )
            (came,) = move((sent, "tok", "own"))
            weights[1] = [late_gate, plane_gather(late_second)]
            parts = (stream1, came)
        else:
            (sent,) = experts_forward(xs, gates_here, slots_here, weights[1], held)

    sent, last_g = lax.optimization_barrier((sent, last_g))
    final_sum = lax.psum_scatter(sent, "zp", scatter_dimension=0, tiled=True)[0]
    last_stream = stream1

    def plane_scatter(r):
        return lax.psum_scatter(r, ("grp", "core"), scatter_dimension=0, tiled=True)[0]

    def between_cores(x):
        theirs = lax.dynamic_index_in_dim(x, 1 - core, 0, keepdims=False)
        return with_other(x, swap(theirs))

    def with_other(x, came):
        ours = lax.dynamic_index_in_dim(x, core, 0, keepdims=False)
        return by_owner((ours.astype(F32) + came.astype(F32)).astype(BF))

    def by_owner(x):
        return x.reshape(grp_size, ctx // 2, shard, x.shape[1])

    def over_grp(x):
        return jnp.sum(x.astype(F32), axis=0).astype(BF)

    g = grad_rows
    for layer in reversed(range(LAYERS)):
        stream, heads, out, lse, mixed, stream1, normed, gates, gains, xs, gates_here = saved[layer]
        last = layer == LAYERS - 1
        if last:
            gs = last_g
        else:
            gs, last_small, came = move(
                (g.astype(BF), "tok", "all"), (over_grp(small), "z", "own"), (wide, "sib", "own")
            )
            wide = with_other(wide, came)
            gs, last_second = lax.optimization_barrier((gs, last_experts[1]))
            last_second = lax.all_to_all(last_second, line, 0, 0, tiled=True)
        res = experts_backward(xs, gs, gates_here, slots_here, weights[layer], held)
        if not last:
            *res, last_second = lax.optimization_barrier((*res, last_second))
        if last:
            *res, final_sum = lax.optimization_barrier((*res, final_sum))
        second_grads = plane_scatter(res[3])
        back = [(res[0], "tok", "own"), (res[1], "tok", "own")]
        if last:
            d_parts, d_gates = move(*back)
            gate_grads, d_parts = lax.optimization_barrier((res[2], d_parts))
            last_experts = [plane_scatter(gate_grads), second_grads]
        else:
            experts = [plane_scatter(res[2]), second_grads]
            d_parts, d_gates, last_wide = move(*back, (wide, "g", "own"))
        g1, d_mixed, small = output_backward(
            d_parts, d_gates, gates, g, stream1, normed, mixed, packed[layer], gains,
            ctx, hq, planes, shard,
        )
        ops = [(d_mixed, "line", "own"), (small, "sib", "own")]
        if last:
            d_out, came = move(*ops)
        else:
            d_out, came, last_wide = move(*ops, (over_grp(last_wide), "z", "own"))
        small = with_other(small, came)
        ops = [(small, "g", "own")]
        if not last:
            ops.append((last_experts[0], "line", "own"))
        dx, small, *came = attention_backward(
            heads, d_out, out, lse, seg_row, seg_col, ctx, hq, tok, ops, sizes, next(ids_of)
        )
        if not last:
            last_gate = came[0]
        g, wide = qkv_backward(
            dx, g1, stream, packed[layer], gains, cos_t, sin_t, ctx, hq, shard
        )
    hidden_out = (last_stream + final_sum.astype(F32)).astype(BF).reshape(micro, tok, D)
    first_wide, first_second, first_small = move(
        (between_cores(wide), "g", "own"),
        (experts[1], "line", "own"),
        (over_grp(small), "z", "own"),
    )
    first_wide, first_gate = move(
        (over_grp(first_wide), "z", "own"), (experts[0], "line", "own")
    )

    grads = attention_gradients(first_wide, last_wide, first_small, last_small)
    gq, gk, gv, go, gain_tail, tail = grads
    tops = expert_gradients(
        [(first_gate, first_second), (last_gate, last_second)], 2 * planes
    )
    return (
        hidden_out,
        g.reshape(micro, tok, D),
        gain_tail[:, :, 0],
        gq,
        gk,
        gv,
        go,
        tail[:, :, 33],
        by_plane(tail[:, :, :E], 2, back=True),
        *tops,
    )


def solution(mesh):
    grp_size = mesh.shape["grp"]
    ctx = mesh.shape["ctx"]
    planes = E // grp_size // 2
    fine = Mesh(
        mesh.devices.reshape(grp_size, ctx // (2 * planes), planes, 2),
        ("grp", "zq", "zp", "core"),
    )
    line = ("zq", "zp", "core")
    every = ("grp",) + line
    row = P("grp", line, None)
    placed = (
        row,
        row,
        P("grp", None),
        row,
        P(None, every),
        P(None, every, None),
        P(None, every, None),
        P(None, every, None),
        P(None, every, None),
        P(None, every),
        P(None, every, None),
        P(None, "grp", line, None),
        P(None, "grp", line, None),
        P(None, "grp", line, None),
    )
    return jax.shard_map(
        functools.partial(per_device, (grp_size, ctx, planes)),
        mesh=fine,
        in_specs=placed,
        out_specs=(
            row,
            row,
            P(None, every),
            P(None, every, None),
            P(None, every, None),
            P(None, every, None),
            P(None, every, None),
            P(None, every),
            P(None, every, None),
            P(None, "grp", line, None),
            P(None, "grp", line, None),
            P(None, "grp", line, None),
        ),
        check_vma=False,
    )
```

```python
import functools
import math

import jax
import jax.numpy as jnp
from jax import lax
from jax.experimental import pallas as pl
from jax.experimental.pallas import tpu as pltpu
from jax.sharding import Mesh, PartitionSpec as P

D = 1024
QUERY_HEADS = 16
KEY_VALUE_HEADS = 8
HS = 64
E = 32
F = 512
TOP = 8
LAYERS = 2
CAP = 42
SLOTS = 48
EPSILON = 1e-06
SCALE = float(HS) ** (-0.5)
QB = 256
BF = jnp.bfloat16
F32 = jnp.float32
MESH = pl.DeviceIdType.MESH
PIECES = 8
VMEM_BYTES = 58 * 1024 * 1024
TAIL = 3 * D // 128


def dot(a, b, ca=1, cb=0):
    return lax.dot_general(a, b, (((ca,), (cb,)), ((), ())), preferred_element_type=F32)


def call(kernel, outs, args, flops, in_specs, out_specs, grid, scratch=(), cid=None):
    nbytes = sum(a.size * a.dtype.itemsize for a in args)
    nbytes += sum(math.prod(o.shape) * jnp.dtype(o.dtype).itemsize for o in outs)
    extra = {} if cid is None else {"collective_id": cid, "has_side_effects": True}
    return pl.pallas_call(
        kernel,
        out_shape=tuple(outs),
        scratch_shapes=list(scratch),
        in_specs=in_specs,
        out_specs=out_specs,
        grid=grid,
        compiler_params=pltpu.CompilerParams(vmem_limit_bytes=VMEM_BYTES, **extra),
        cost_estimate=pl.CostEstimate(
            flops=int(flops), bytes_accessed=int(nbytes), transcendentals=0
        ),
    )(*args)


def sds(shape, dtype):
    return jax.ShapeDtypeStruct(tuple(shape), dtype)


def full(shape):
    n = len(shape)
    return pl.BlockSpec(tuple(shape), lambda *_: (0,) * n)


def size_of(group, sizes):
    grp_size, ctx, planes = sizes
    return {"g": grp_size, "tok": planes, "line": ctx, "z": ctx // 2, "sib": 2}[group]


def place_in(group, sizes):
    planes = sizes[2]
    n = size_of(group, sizes)
    zp = lax.axis_index("zp")
    zz = lax.axis_index("zq") * planes + zp
    core = lax.axis_index("core")
    if group == "g":
        return n, lax.axis_index("grp"), lambda p: {"grp": p}
    if group == "tok":
        return n, zp, lambda p: {"zp": p}
    if group == "line":
        return (
            n,
            zz * 2 + core,
            lambda p: {
                "zq": p // (2 * planes),
                "zp": lax.rem(p // 2, planes),
                "core": lax.rem(p, 2),
            },
        )
    if group == "z":
        return n, zz, lambda p: {"zq": p // planes, "zp": lax.rem(p, planes)}
    return n, core, lambda p: {"core": p}


def transfer(ops, cid, sizes):
    grp_size, ctx, _ = sizes
    groups = []
    for _, group, what in ops:
        for name in ("z", "g", "sib") if what == "packed" else (group,):
            if name not in groups:
                groups.append(name)
    shapes = []
    sems = []
    total_sems = 0
    for x, group, what in ops:
        sems.append(total_sems)
        if what == "packed":
            shapes.append(sds((grp_size, ctx) + x.shape, x.dtype))
            zs = ctx // 2
            total_sems += zs + zs * grp_size * 2
            continue
        n = size_of(group, sizes)
        total_sems += PIECES if group == "sib" else 2 * n if what == "all" else n
        rest = x.shape[1:] if group == "sib" else x.shape
        if what != "own":
            rest = (n,) + (x.shape if what == "all" else x.shape[2:])
        shapes.append(sds(rest, x.dtype))
    count = len(ops)

    def kernel(*refs):
        ins = refs[:count]
        outs = refs[count : count + len(shapes)]
        send, recv, local = refs[count + len(shapes) :]
        barrier = pltpu.get_barrier_semaphore()
        total = 0
        for group in groups:
            n, me, where = place_in(group, sizes)
            for k in range(1, n):
                pl.semaphore_signal(
                    barrier, inc=1, device_id=where(lax.rem(me + k, n)), device_id_type=MESH
                )
            total += n - 1
        pl.semaphore_wait(barrier, total)

        def remote(src, dst, at, place):
            copy = pltpu.make_async_remote_copy(
                src_ref=src,
                dst_ref=dst,
                send_sem=send.at[at],
                recv_sem=recv.at[at],
                device_id=place,
                device_id_type=MESH,
            )
            copy.start()
            return copy

        sib_place = {"core": 1 - lax.axis_index("core")}
        sent = []
        own_copies = []

        def start(i):
            _, group, what = ops[i]
            n, me, where = place_in(group or "g", sizes)
            out = outs[i]
            if what == "all":
                copy = pltpu.make_async_copy(ins[i], out.at[me], local.at[i])
                copy.start()
                own_copies.append(copy)

                @pl.when(me < n - 1)
                def _():
                    hop(i, n, ins[i], me, 1).start()

                @pl.when(me > 0)
                def _():
                    hop(i, n, ins[i], me, -1).start()

                return None
            if what == "packed":
                grp = lax.axis_index("grp")
                core = lax.axis_index("core")
                zs, zz, z_place = place_in("z", sizes)
                copy = pltpu.make_async_copy(ins[i], out.at[grp, zz * 2 + core], local.at[i])
                copy.start()
                along = []
                for k in range(1, zs):
                    along.append(
                        remote(
                            ins[i],
                            out.at[grp, zz * 2 + core],
                            sems[i] + k,
                            z_place(lax.rem(zz + k, zs)),
                        )
                    )
                return (i, along, copy)
            if group == "sib":
                size = ins[i].shape[1] // PIECES
                for j in range(PIECES):
                    part = pl.ds(j * size, size)
                    sent.append(
                        remote(ins[i].at[1 - me, part], out.at[part], sems[i] + j, where(1 - me))
                    )
                return None
            copies = []
            for k in range(1, n):
                peer = lax.rem(me + k, n)
                if what == "own":
                    src = ins[i].at[peer]
                else:
                    src = ins[i].at[what, lax.rem(peer, ins[i].shape[1])]
                copies.append(remote(src, out.at[me], sems[i] + k, where(peer)))
            if what == "own":
                src = ins[i].at[me]
            else:
                src = ins[i].at[what, lax.rem(me, ins[i].shape[1])]
            copy = pltpu.make_async_copy(src, out.at[me], local.at[i])
            copy.start()
            own_copies.append(copy)
            sent.extend(copies)
            return None

        def hop(i, n, src, block, way):
            _, me, where = place_in(ops[i][1], sizes)
            return pltpu.make_async_remote_copy(
                src_ref=src,
                dst_ref=outs[i].at[block],
                send_sem=send.at[sems[i] + block + (0 if way > 0 else n)],
                recv_sem=recv.at[sems[i] + block],
                device_id=where(me + way),
                device_id_type=MESH,
            )

        def finish_all(i):
            n, me, _ = place_in(ops[i][1], sizes)
            out = outs[i]
            for far in range(1, n):
                low, high = me - far, me + far

                @pl.when(low >= 0)
                def _():
                    hop(i, n, out.at[low], low, 1).wait_recv()

                    @pl.when(me < n - 1)
                    def _():
                        hop(i, n, out.at[low], low, 1).start()

                @pl.when(high <= n - 1)
                def _():
                    hop(i, n, out.at[high], high, -1).wait_recv()

                    @pl.when(me > 0)
                    def _():
                        hop(i, n, out.at[high], high, -1).start()

            for far in range(n):
                low, high = me - far, me + far

                @pl.when((low >= 0) & (me < n - 1))
                def _():
                    hop(i, n, ins[i] if far == 0 else out.at[low], low, 1).wait_send()

                @pl.when((high <= n - 1) & (me > 0))
                def _():
                    hop(i, n, ins[i] if far == 0 else out.at[high], high, -1).wait_send()

        def finish_packed(i, along, own):
            grp = lax.axis_index("grp")
            core = lax.axis_index("core")
            zs, zz, _ = place_in("z", sizes)
            out = outs[i]
            base = sems[i] + zs
            over = []

            def spread(j, at):
                for m in range(1, grp_size):
                    over.append(
                        (
                            remote(
                                out.at[at[0], at[1]],
                                out.at[at[0], at[1]],
                                base + j * grp_size + m,
                                {"grp": lax.rem(grp + m, grp_size)},
                            ),
                            j,
                            m,
                        )
                    )

            def to_core(j, m, at):
                sent.append(
                    remote(
                        out.at[at[0], at[1]],
                        out.at[at[0], at[1]],
                        base + zs * grp_size + j * grp_size + m,
                        sib_place,
                    )
                )

            own.wait()
            for j in range(zs):
                if j > 0:
                    along[j - 1].wait_recv()
                at = (grp, lax.rem(zz - j + zs, zs) * 2 + core)
                spread(j, at)
                to_core(j, 0, at)
            for copy, j, m in over:
                copy.wait_recv()
                at = (
                    lax.rem(grp - m + grp_size, grp_size),
                    lax.rem(zz - j + zs, zs) * 2 + core,
                )
                to_core(j, m, at)
            for copy in along:
                copy.wait_send()
            for copy, _, _ in over:
                copy.wait_send()

        pending = []
        for i in range(count):
            got = start(i)
            if got is not None:
                pending.append(got)
        for item in pending:
            finish_packed(*item)
        for i in range(count):
            if ops[i][2] == "all":
                finish_all(i)
        for copy in own_copies:
            copy.wait()
        for copy in sent:
            copy.wait()

    total = sum(math.prod(o.shape) * jnp.dtype(o.dtype).itemsize for o in shapes)
    any_spec = pl.BlockSpec(memory_space=pl.ANY)
    return pl.pallas_call(
        kernel,
        out_shape=tuple(shapes),
        in_specs=[any_spec] * count,
        out_specs=tuple([any_spec] * len(shapes)),
        scratch_shapes=[
            pltpu.SemaphoreType.DMA((total_sems,)),
            pltpu.SemaphoreType.DMA((total_sems,)),
            pltpu.SemaphoreType.DMA((count,)),
        ],
        compiler_params=pltpu.CompilerParams(collective_id=cid, has_side_effects=True),
        cost_estimate=pl.CostEstimate(
            flops=0, bytes_accessed=40 * int(total), transcendentals=0
        ),
    )(*[x for x, _, _ in ops])


ANY_SPEC = pl.BlockSpec(memory_space=pl.ANY)


class Carried:
    def __init__(self, ops, sizes):
        self.sizes = sizes
        self.ops = ops
        self.shapes = []
        self.first = []
        self.total = 0
        for x, group, what in ops:
            n = size_of(group, sizes)
            shape = x.shape if what == "own" else (n,) + x.shape[2:]
            if what == "all":
                shape = (n,) + x.shape
            elif group == "sib":
                shape = x.shape[1:]
            self.shapes.append(sds(shape, x.dtype))
            self.first.append(self.total)
            self.total += n

    def scratch(self):
        if not self.ops:
            return []
        return [
            pltpu.SemaphoreType.DMA((self.total,)),
            pltpu.SemaphoreType.DMA((self.total,)),
            pltpu.SemaphoreType.DMA((len(self.ops),)),
        ]

    def enter(self, groups):
        barrier = pltpu.get_barrier_semaphore()
        total = 0
        for group in groups:
            n, me, where = place_in(group, self.sizes)
            for k in range(1, n):
                pl.semaphore_signal(
                    barrier, inc=1, device_id=where(lax.rem(me + k, n)), device_id_type=MESH
                )
            total += n - 1
        pl.semaphore_wait(barrier, total)

    def copies(self, ins, outs, sems):
        made = []
        for i, (_, group, what) in enumerate(self.ops):
            send, recv, local = sems
            n, me, where = place_in(group, self.sizes)

            def part(j, i=i, what=what):
                if what == "all":
                    return ins[i]
                if what == "own":
                    return ins[i].at[j]
                return ins[i].at[what, lax.rem(j, ins[i].shape[1])]

            for k in range(1, n):
                peer = lax.rem(me + k, n)
                made.append(
                    pltpu.make_async_remote_copy(
                        src_ref=part(peer),
                        dst_ref=outs[i] if group == "sib" else outs[i].at[me],
                        send_sem=send.at[self.first[i] + k],
                        recv_sem=recv.at[self.first[i] + k],
                        device_id=where(peer),
                        device_id_type=MESH,
                    )
                )
            if group != "sib":
                made.append(pltpu.make_async_copy(part(me), outs[i].at[me], local.at[i]))
        return made


def head_copies(buf, out, sems, m, ctx, tok, sizes):
    send, recv, local = sems
    n, me, where = place_in("line", sizes)
    rows = pl.ds(m * tok, tok)
    made = []
    for k in range(1, n):
        peer = lax.rem(me + k, n)
        made.append(
            pltpu.make_async_remote_copy(
                src_ref=buf.at[m, peer],
                dst_ref=out.at[me, rows],
                send_sem=send.at[m * n + k],
                recv_sem=recv.at[m * n + k],
                device_id=where(peer),
                device_id_type=MESH,
            )
        )
    made.append(pltpu.make_async_copy(buf.at[m, me], out.at[me, rows], local.at[m]))
    return made


def head_scratch(micro, ctx, tok, width):
    return [
        pltpu.VMEM((micro, ctx, tok, width), BF),
        pltpu.SemaphoreType.DMA((micro * ctx,)),
        pltpu.SemaphoreType.DMA((micro * ctx,)),
        pltpu.SemaphoreType.DMA((micro,)),
    ]


def swap_halves(x):
    lane = lax.broadcasted_iota(jnp.int32, x.shape, 1)
    width = x.shape[1]
    up = pltpu.roll(x, width - HS // 2, 1)
    down = pltpu.roll(x, HS // 2, 1)
    return jnp.where((lane & (HS - 1)) < HS // 2, up, down)


def inv_rms_of(x):
    return lax.rsqrt(jnp.mean(x * x, axis=-1, keepdims=True) + EPSILON)


def in_order(parts):
    return parts[0] if len(parts) == 1 else jnp.concatenate(parts, axis=1)


def qkv_forward(stream_parts, packed, cos_t, sin_t, ctx, hq, sizes, cid):
    first = len(stream_parts) == 1
    rows = stream_parts[0].shape[0]
    dup = ctx // KEY_VALUE_HEADS

    meet = Carried([], sizes)

    def kernel(*refs):
        refs, (buf, *sems) = refs[:-4], refs[-4:]
        meet.enter(["line"])
        if first:
            h_ref, w_ref, t_ref, c_ref, s_ref, out_ref, gains_ref = refs
            x = h_ref[...].astype(F32)
        else:
            h_ref, p_ref, w_ref, t_ref, c_ref, s_ref, out_ref, gains_ref, x_ref = refs
            x = h_ref[...]
            for j in range(p_ref.shape[0]):
                x = x + p_ref[j].astype(F32)
            x_ref[...] = x
        gains = jnp.transpose(t_ref[...].astype(F32))[32:40]
        gains_ref[...] = gains
        normed = (x * inv_rms_of(x) * gains[0:1]).astype(BF)
        cos_v = c_ref[...]
        sin_v = s_ref[...]
        parts = []
        for i in range(8):
            y = dot(normed, w_ref[:, 256 * i : 256 * (i + 1)])
            if i < 6:
                y = y * cos_v + swap_halves(y) * sin_v
            parts.append(y.astype(BF))
        queries, keys, values = in_order(parts[:4]), in_order(parts[4:6]), in_order(parts[6:])
        for i in range(ctx):
            mine = [queries[:, HS * hq * i : HS * hq * (i + 1)]]
            if hq < 2:
                mine.append(jnp.zeros((rows, 128 - HS * hq), BF))
            kv = i // dup
            mine.append(keys[:, HS * kv : HS * (kv + 1)])
            mine.append(values[:, HS * kv : HS * (kv + 1)])
            buf[0, i] = in_order(mine)
        copies = head_copies(buf, out_ref, sems, 0, ctx, rows, sizes)
        for copy in copies:
            copy.start()
        for copy in copies:
            copy.wait()

    args = list(stream_parts) + [packed, packed, cos_t, sin_t]
    in_specs = [full(a.shape) for a in stream_parts] + [
        pl.BlockSpec((D, 2 * D), lambda i: (0, 0)),
        pl.BlockSpec((D, 128), lambda i: (0, TAIL)),
        full(cos_t.shape),
        full(sin_t.shape),
    ]
    outs = [sds((ctx, rows, 256), BF), sds((8, D), F32)]
    if not first:
        outs.append(sds((rows, D), F32))
    return call(
        kernel,
        outs,
        args,
        4 * rows * D * D,
        in_specs=in_specs,
        out_specs=(ANY_SPEC,) + tuple(full(o.shape) for o in outs[1:]),
        grid=(1,),
        scratch=head_scratch(1, ctx, rows, 256),
        cid=cid,
    )


def block_mask(seg_row, seg_col, qb, length):
    keys = (qb + 1) * QB
    qi = lax.broadcasted_iota(jnp.int32, (QB, keys), 0) + qb * QB
    ki = lax.broadcasted_iota(jnp.int32, (QB, keys), 1)
    sr = seg_row[:, :keys]
    return (ki <= qi) & ((sr == 0) | (sr == seg_col))


def attention_forward(x, seg_row, seg_col, ctx, hq, tok, sizes, cid):
    micro = x.shape[1] // tok
    length = ctx * tok
    per = QB // tok

    meet = Carried([], sizes)

    def kernel(x_ref, sr_ref, sc_ref, o_ref, l_ref, mixed_ref, buf, *sems):
        m = pl.program_id(0)
        xs = x_ref[...].reshape(length, 256)
        ks = xs[:, 128:192]
        vs = xs[:, 192:256]
        for qb in range(length // QB):
            keys = (qb + 1) * QB
            rows = slice(qb * QB, (qb + 1) * QB)
            mask = block_mask(sr_ref[0], sc_ref[0, rows, :], qb, length)
            outs = []
            lses = []
            for h in range(hq):
                q = xs[rows, HS * h : HS * (h + 1)]
                s = jnp.where(mask, dot(q, ks[:keys], 1, 1) * SCALE, -1e30)
                top = jnp.max(s, axis=-1, keepdims=True)
                p = jnp.exp(s - top)
                total = jnp.sum(p, axis=-1, keepdims=True)
                o = dot(p.astype(BF), vs[:keys]) / total
                outs.append(o)
                lses.append(jnp.broadcast_to(top + jnp.log(total), (QB, HS)))
            for _ in range(hq, 2):
                outs.append(jnp.zeros((QB, HS), F32))
                lses.append(jnp.zeros((QB, HS), F32))
            done = jnp.concatenate(outs, axis=1).astype(BF).reshape(per, tok, 128)
            o_ref[qb * per : (qb + 1) * per] = done
            buf[m, qb * per : (qb + 1) * per] = done
            l_ref[0, rows, :] = jnp.concatenate(lses, axis=1)

        @pl.when(m == 0)
        def _():
            meet.enter(["line"])

        for copy in head_copies(buf, mixed_ref, sems, m, ctx, tok, sizes):
            copy.start()

        @pl.when(m == micro - 1)
        def _():
            for j in range(micro):
                for copy in head_copies(buf, mixed_ref, sems, j, ctx, tok, sizes):
                    copy.wait()

    return call(
        kernel,
        [
            sds((ctx, micro * tok, 128), BF),
            sds((micro, length, 128), F32),
            sds((ctx, micro * tok, 128), BF),
        ],
        [x, seg_row, seg_col],
        2 * micro * hq * length * length * HS,
        in_specs=[
            pl.BlockSpec((ctx, tok, 256), lambda m: (0, m, 0)),
            pl.BlockSpec((1, 1, length), lambda m: (m, 0, 0)),
            pl.BlockSpec((1, length, 1), lambda m: (m, 0, 0)),
        ],
        out_specs=(
            pl.BlockSpec((ctx, tok, 128), lambda m: (0, m, 0)),
            pl.BlockSpec((1, length, 128), lambda m: (m, 0, 0)),
            ANY_SPEC,
        ),
        grid=(micro,),
        scratch=head_scratch(micro, ctx, tok, 128),
        cid=cid,
    )


def attention_backward(x, d_out, out, lse, seg_row, seg_col, ctx, hq, tok, ops, sizes, cid):
    micro = x.shape[1] // tok
    length = ctx * tok
    per = QB // tok

    carry = Carried(ops, sizes)
    count = len(ops)

    def kernel(x_ref, d_ref, o_ref, l_ref, sr_ref, sc_ref, *rest):
        ins, out_ref, outs = rest[:count], rest[count], rest[count + 1 : 2 * count + 1]
        dk_ref, dv_ref, buf, *sems = rest[2 * count + 1 :]
        sems, carry_sems = sems[:3], sems[3:]
        m = pl.program_id(0)
        dx_ref = buf.at[m]

        @pl.when(m == 0)
        def _():
            carry.enter(["line"] + [group for _, group, _ in ops if group != "line"])
            for copy in carry.copies(ins, outs, carry_sems):
                copy.start()

        xs = x_ref[...].reshape(length, 256)
        ks = xs[:, 128:192]
        vs = xs[:, 192:256]
        ds_all = d_ref[...].reshape(length, 128)
        os_all = o_ref[...].reshape(length, 128)
        dk_ref[...] = jnp.zeros((length, HS), F32)
        dv_ref[...] = jnp.zeros((length, HS), F32)
        for qb in range(length // QB):
            keys = (qb + 1) * QB
            rows = slice(qb * QB, (qb + 1) * QB)
            mask = block_mask(sr_ref[0], sc_ref[0, rows, :], qb, length)
            dqs = []
            for h in range(hq):
                cols = slice(HS * h, HS * (h + 1))
                q = xs[rows, cols]
                do = ds_all[rows, cols]
                delta = jnp.sum(
                    do.astype(F32) * os_all[rows, cols].astype(F32), axis=-1, keepdims=True
                )
                s = dot(q, ks[:keys], 1, 1) * SCALE - l_ref[0, rows, HS * h : HS * h + 1]
                p = jnp.exp(jnp.where(mask, s, -1e30))
                dp = dot(do, vs[:keys], 1, 1)
                ds = (p * (dp - delta) * SCALE).astype(BF)
                dqs.append(dot(ds, ks[:keys]))
                dk_ref[:keys] += dot(ds, q, 0, 0)
                dv_ref[:keys] += dot(p.astype(BF), do, 0, 0)
            for _ in range(hq, 2):
                dqs.append(jnp.zeros((QB, HS), F32))
            dx_ref[qb * per : (qb + 1) * per, :, 0:128] = (
                jnp.concatenate(dqs, axis=1).astype(BF).reshape(per, tok, 128)
            )
        dx_ref[:, :, 128:256] = (
            jnp.concatenate([dk_ref[...], dv_ref[...]], axis=1)
            .astype(BF)
            .reshape(ctx, tok, 128)
        )
        for copy in head_copies(buf, out_ref, sems, m, ctx, tok, sizes):
            copy.start()

        @pl.when(m == micro - 1)
        def _():
            for j in range(micro):
                for copy in head_copies(buf, out_ref, sems, j, ctx, tok, sizes):
                    copy.wait()
            for copy in carry.copies(ins, outs, carry_sems):
                copy.wait()

    return call(
        kernel,
        [sds((ctx, micro * tok, 256), BF)] + carry.shapes,
        [x, d_out, out, lse, seg_row, seg_col] + [o[0] for o in ops],
        5 * micro * hq * length * length * HS,
        in_specs=[
            pl.BlockSpec((ctx, tok, 256), lambda m: (0, m, 0)),
            pl.BlockSpec((ctx, tok, 128), lambda m: (0, m, 0)),
            pl.BlockSpec((ctx, tok, 128), lambda m: (0, m, 0)),
            pl.BlockSpec((1, length, 128), lambda m: (m, 0, 0)),
            pl.BlockSpec((1, 1, length), lambda m: (m, 0, 0)),
            pl.BlockSpec((1, length, 1), lambda m: (m, 0, 0)),
        ]
        + [ANY_SPEC] * count,
        out_specs=tuple([ANY_SPEC] * (count + 1)),
        grid=(micro,),
        scratch=[pltpu.VMEM((length, HS), F32), pltpu.VMEM((length, HS), F32)]
        + head_scratch(micro, ctx, tok, 256)
        + carry.scratch(),
        cid=cid,
    )


def side_by_side(m_ref, ctx, hq):
    return jnp.concatenate([m_ref[i][:, : HS * hq] for i in range(ctx)], axis=1)


def output_forward(mixed, stream, packed, gains, chosen, ctx, hq, n, held):
    rows = stream.shape[0]

    def kernel(m_ref, x_ref, w_ref, t_ref, g_ref, c_ref, s_ref, n_ref, gate_ref):
        x = x_ref[...].astype(F32) + dot(side_by_side(m_ref, ctx, hq), w_ref[...])
        s_ref[...] = x
        normed = (x * inv_rms_of(x) * g_ref[1:2]).astype(BF)
        n_ref[...] = normed
        logits = dot(t_ref[...], normed, 0, 1)[:E]
        named = c_ref[...] > 0.0
        logits = jnp.where(named, logits, -1e30)
        top = jnp.max(logits, axis=0, keepdims=True)
        p = jnp.where(named, jnp.exp(logits - top), 0.0)
        gates = p / jnp.sum(p, axis=0, keepdims=True)
        for j in range(n):
            gate_ref[j] = gates[held * j : held * (j + 1)]

    outs = [sds((rows, D), F32), sds((rows, D), BF), sds((n, held, rows), F32)]
    return call(
        kernel,
        outs,
        [mixed, stream, packed, packed, gains, chosen],
        2 * rows * D * D,
        in_specs=[
            full(mixed.shape),
            full(stream.shape),
            pl.BlockSpec((D, D), lambda i: (0, 2)),
            pl.BlockSpec((D, 128), lambda i: (0, TAIL)),
            full(gains.shape),
            full(chosen.shape),
        ],
        out_specs=tuple(full(o.shape) for o in outs),
        grid=(1,),
    )


def by_core(x, shard):
    y = x.astype(BF).reshape(x.shape[0] // (2 * shard), 2, shard, x.shape[1])
    return [y[:, c].reshape(x.shape[0] // 2, x.shape[1]) for c in range(2)]


def norm_back(x, gain, d_normed):
    r = inv_rms_of(x)
    grad_gain = jnp.sum(d_normed * x * r, axis=0, keepdims=True)
    q = d_normed * gain
    dx = r * q - x * (r * r * r) * jnp.mean(x * q, axis=-1, keepdims=True)
    return dx, grad_gain


def output_backward(parts, d_gates, gates, g, stream, normed, mixed, packed, gains, ctx, hq, n, shard, ops, sizes, cid):
    rows = stream.shape[0]

    carry = Carried(ops, sizes)
    count = len(ops)

    def kernel(p_ref, dg_ref, gt_ref, g_ref, x_ref, nm_ref, m_ref, w_ref, t_ref, gain_ref, *rest):
        ins, (g1_ref, gw_ref, dm_ref) = rest[:count], rest[count : count + 3]
        carried, rest = rest[count + 3 : 2 * count + 3], rest[2 * count + 3 :]
        buf, sems, carry_sems = rest[0], rest[1:4], rest[4:]
        carry.enter(["line"] + [group for _, group, _ in ops])
        others = carry.copies(ins, carried, carry_sems)
        for copy in others:
            copy.start()
        gates_v = jnp.concatenate([gt_ref[j] for j in range(n)], axis=0)
        dgate_v = jnp.concatenate([dg_ref[j] for j in range(n)], axis=0)
        mean = jnp.sum(gates_v * dgate_v, axis=0, keepdims=True)
        d_logits = (gates_v * (dgate_v - mean)).astype(BF)
        d_logits = jnp.concatenate([d_logits, jnp.zeros((128 - E, rows), BF)], axis=0)
        router = t_ref[...]
        d_normed = dot(d_logits, router, 0, 1)
        for j in range(n):
            d_normed = d_normed + p_ref[j].astype(F32)
        x = x_ref[...]
        dx, grad_gain = norm_back(x, gain_ref[1:2], d_normed)
        g1 = g_ref[...].astype(F32) + dx
        g1_ref[...] = g1
        low = g1.astype(BF)
        dm = dot(low, w_ref[...], 1, 1).astype(BF)
        for i in range(ctx):
            part = dm[:, HS * hq * i : HS * hq * (i + 1)]
            if hq < 2:
                part = jnp.concatenate([part, jnp.zeros((rows, 128 - HS * hq), BF)], axis=1)
            buf[0, i] = part
        copies = head_copies(buf, dm_ref, sems, 0, ctx, rows, sizes)
        for copy in copies:
            copy.start()
        grad_out = dot(side_by_side(m_ref, ctx, hq), low, 0, 0)
        for c, value in enumerate(by_core(grad_out, shard)):
            gw_ref[c, :, 0:D] = value
        grad_router = dot(nm_ref[...], d_logits, 0, 1)
        row = lax.broadcasted_iota(jnp.int32, (128, D), 0)
        cols = jnp.where(row == 33, jnp.broadcast_to(grad_gain, (128, D)), 0.0)
        for c, value in enumerate(by_core(grad_router + jnp.transpose(cols), shard)):
            gw_ref[c, :, D : D + 128] = value
        for copy in copies + others:
            copy.wait()

    outs = [sds((rows, D), F32), sds((2, D // 2, D + 128), BF), sds((ctx, rows, 128), BF)]
    args = [parts, d_gates, gates, g, stream, normed, mixed, packed, packed, gains]
    in_specs = [full(a.shape) for a in args]
    in_specs[7] = pl.BlockSpec((D, D), lambda i: (0, 2))
    in_specs[8] = pl.BlockSpec((D, 128), lambda i: (0, TAIL))
    return call(
        kernel,
        outs + carry.shapes,
        args + [o[0] for o in ops],
        4 * rows * D * D,
        in_specs=in_specs + [ANY_SPEC] * count,
        out_specs=tuple([full(o.shape) for o in outs[:2]] + [ANY_SPEC] * (count + 1)),
        grid=(1,),
        scratch=head_scratch(1, ctx, rows, 128) + carry.scratch(),
        cid=cid,
    )


def qkv_backward(dx, g1, stream, packed, gains, cos_t, sin_t, ctx, hq, shard):
    rows = g1.shape[0]
    dup = ctx // KEY_VALUE_HEADS

    def kernel(d_ref, g_ref, x_ref, w_ref, gain_ref, c_ref, s_ref, out_ref, gw_ref):
        x = x_ref[...].astype(F32)
        gain = gain_ref[0:1]
        normed = (x * inv_rms_of(x) * gain).astype(BF)
        cos_v = c_ref[...]
        sin_v = s_ref[...]
        queries = in_order([d_ref[i][:, : HS * hq] for i in range(ctx)])
        both = []
        for head in range(KEY_VALUE_HEADS):
            total = d_ref[head * dup][:, 128:256]
            if dup > 1:
                total = total.astype(F32)
                for r in range(1, dup):
                    total = total + d_ref[head * dup + r][:, 128:256].astype(F32)
            both.append(total)
        keys = in_order([t[:, :HS] for t in both])
        values = in_order([t[:, HS:] for t in both])
        d_normed = jnp.zeros((rows, D), F32)
        for i in range(8):
            if i < 4:
                y = queries[:, 256 * i : 256 * (i + 1)]
            elif i < 6:
                y = keys[:, 256 * (i - 4) : 256 * (i - 3)]
            else:
                y = values[:, 256 * (i - 6) : 256 * (i - 5)]
            if i < 6:
                y = y.astype(F32)
                y = y * cos_v - swap_halves(y) * sin_v
            lin = y.astype(BF)
            cols = slice(256 * i, 256 * (i + 1))
            d_normed = d_normed + dot(lin, w_ref[:, cols], 1, 1)
            for c, value in enumerate(by_core(dot(normed, lin, 0, 0), shard)):
                gw_ref[c, :, cols] = value
        back, grad_gain = norm_back(x, gain, d_normed)
        out_ref[...] = g_ref[...] + back
        row = lax.broadcasted_iota(jnp.int32, (128, D), 0)
        cols = jnp.where(row == 0, jnp.broadcast_to(grad_gain, (128, D)), 0.0)
        for c, value in enumerate(by_core(jnp.transpose(cols), shard)):
            gw_ref[c, :, 2 * D : 2 * D + 128] = value

    outs = [sds((rows, D), F32), sds((2, D // 2, 2 * D + 128), BF)]
    args = [dx, g1, stream, packed, gains, cos_t, sin_t]
    in_specs = [full(a.shape) for a in args]
    in_specs[3] = pl.BlockSpec((D, 2 * D), lambda i: (0, 0))
    return call(
        kernel,
        outs,
        args,
        8 * rows * D * D,
        in_specs=in_specs,
        out_specs=tuple(full(o.shape) for o in outs),
        grid=(1,),
    )


def pick_matrix(slot_row, rows):
    at = lax.broadcasted_iota(jnp.int32, (2 * SLOTS, rows), 0)
    return at == slot_row


def weight_specs(weights):
    return [
        pl.BlockSpec((1,) + w.shape[1:], lambda e: (e, 0, 0, 0)) for w in weights
    ]


def matrices(first_ref, second_ref):
    ctx, depth, _ = first_ref.shape[1:]
    half = F // ctx
    second = second_ref[0]
    return (
        first_ref[0].reshape(D, F),
        second[:, :depth].reshape(D, F),
        second[:, depth : depth + half].reshape(F, D // 2),
        second[:, depth + half :].reshape(F, D // 2),
    )


def experts_forward(x, gates, slots, weights, held, ops=(), sizes=None, cid=None):
    n, rows, _ = x.shape
    lanes = 2 * SLOTS


    carry = Carried(ops, sizes)
    count = len(ops)

    def kernel(x_ref, g_ref, s_ref, w0, w1, *rest):
        ins, out_ref, outs = rest[:count], rest[count], rest[count + 1 : 2 * count + 1]
        acc_ref, row_ref, eo_ref, *sems = rest[2 * count + 1 :]
        e = pl.program_id(0)
        if count:

            @pl.when(e == 0)
            def _():
                carry.enter(sorted(set(group for _, group, _ in ops)))
                for copy in carry.copies(ins, outs, sems):
                    copy.start()

        w_gate, w_up, down_l, down_r = matrices(w0, w1)
        for s in range(n):
            pick = pick_matrix(s_ref[s, pl.ds(e, 1), :], rows).astype(BF)
            row_ref[lanes * s : lanes * (s + 1), :] = dot(pick, x_ref[s]).astype(BF)
        rws = row_ref[...]
        ga = dot(rws, w_gate)
        up = dot(rws, w_up)
        hidden = (ga * jax.nn.sigmoid(ga) * up).astype(BF)
        eo_ref[:, : D // 2] = dot(hidden, down_l).astype(BF)
        eo_ref[:, D // 2 :] = dot(hidden, down_r).astype(BF)
        for s in range(n):
            pick = pick_matrix(s_ref[s, pl.ds(e, 1), :], rows)
            gated = jnp.where(pick, g_ref[s, pl.ds(e, 1), :], 0.0).astype(BF)
            add = dot(gated, eo_ref[lanes * s : lanes * (s + 1), :], 0, 0)

            @pl.when(e == 0)
            def _():
                acc_ref[s] = add.astype(F32)

            @pl.when((e > 0) & (e < held - 1))
            def _():
                acc_ref[s] = (acc_ref[s].astype(F32) + add).astype(F32)

            @pl.when(e == held - 1)
            def _():
                out_ref[s] = (acc_ref[s].astype(F32) + add).astype(BF)

        if count:

            @pl.when(e == held - 1)
            def _():
                for copy in carry.copies(ins, outs, sems):
                    copy.wait()

    flops = 2 * held * n * (lanes * D * F * 3 + 2 * lanes * rows * D)
    return call(
        kernel,
        [sds(x.shape, BF)] + carry.shapes,
        [x, gates, slots] + list(weights) + [o[0] for o in ops],
        flops,
        in_specs=[full(x.shape), full(gates.shape), full(slots.shape)]
        + weight_specs(weights)
        + [ANY_SPEC] * count,
        out_specs=tuple([full(x.shape)] + [ANY_SPEC] * count),
        grid=(held,),
        scratch=[
            pltpu.VMEM(x.shape, F32),
            pltpu.VMEM((n * lanes, D), BF),
            pltpu.VMEM((n * lanes, D), BF),
        ]
        + carry.scratch(),
        cid=cid if count else None,
    )


def experts_backward(x, g, gates, slots, weights, held, ops=(), sizes=None, cid=None):
    n, rows, _ = x.shape
    lanes = 2 * SLOTS


    carry = Carried(ops, sizes)
    count = len(ops)

    def kernel(x_ref, gr_ref, g_ref, s_ref, w0, w1, *rest):
        ins, rest = rest[:count], rest[count:]
        dx_ref, dg_ref, first_grad, second_grad, *rest = rest
        carried, rest = rest[:count], rest[count:]
        acc_ref, row_ref, grow_ref, *sems = rest
        e = pl.program_id(0)
        if count:

            @pl.when(e == 0)
            def _():
                carry.enter(sorted(set(group for _, group, _ in ops)))
                for copy in carry.copies(ins, carried, sems):
                    copy.start()

        w_gate, w_up, down_l, down_r = matrices(w0, w1)
        slot_gates = []
        for s in range(n):
            mine = slice(lanes * s, lanes * (s + 1))
            pick = pick_matrix(s_ref[s, pl.ds(e, 1), :], rows)
            low = pick.astype(BF)
            row_ref[mine, :] = dot(low, x_ref[s]).astype(BF)
            grow_ref[mine, :] = dot(low, gr_ref[s]).astype(BF)
            gated = jnp.where(pick, g_ref[s, pl.ds(e, 1), :], 0.0)
            slot_gates.append(jnp.sum(gated, axis=1, keepdims=True))
        gate = jnp.concatenate(slot_gates, axis=0)
        rws = row_ref[...]
        grows = grow_ref[...]
        ga = dot(rws, w_gate)
        up = dot(rws, w_up)
        sig = jax.nn.sigmoid(ga)
        act = ga * sig
        hidden_f = act * up
        hidden = hidden_f.astype(BF)
        dhg = dot(grows[:, : D // 2], down_l, 1, 1) + dot(grows[:, D // 2 :], down_r, 1, 1)
        d_gate = jnp.sum(hidden.astype(F32) * dhg, axis=1, keepdims=True)
        dh = dhg * gate
        dga = (dh * up * (sig * (1.0 + ga * (1.0 - sig)))).astype(BF)
        dup = (dh * act).astype(BF)
        drow = (dot(dga, w_gate, 1, 1) + dot(dup, w_up, 1, 1)).astype(BF)
        for s in range(n):
            mine = slice(lanes * s, lanes * (s + 1))
            pick = pick_matrix(s_ref[s, pl.ds(e, 1), :], rows)
            dg_ref[s, pl.ds(e, 1), :] = jnp.sum(
                jnp.where(pick, d_gate[mine], 0.0), axis=0, keepdims=True
            )
            add = dot(pick.astype(BF), drow[mine], 0, 0)

            @pl.when(e == 0)
            def _():
                acc_ref[s] = add

            @pl.when((e > 0) & (e < held - 1))
            def _():
                acc_ref[s] += add

            @pl.when(e == held - 1)
            def _():
                dx_ref[s] = (acc_ref[s] + add).astype(BF)

        dslot = (grows.astype(F32) * gate).astype(BF)
        ctx, depth, _ = first_grad.shape[1:]
        part = F // ctx
        both = dot(rws, jnp.concatenate([dga, dup], axis=1), 0, 0).astype(BF)
        first_grad[0] = both[:, :F].reshape(ctx, depth, F)
        second_grad[0, :, :depth, :] = both[:, F:].reshape(ctx, depth, F)
        down = dot(hidden, dslot, 0, 0).astype(BF)
        for k in range(2):
            at_row = depth + part * k
            second_grad[0, :, at_row : at_row + part, :] = down[
                :, D // 2 * k : D // 2 * (k + 1)
            ].reshape(ctx, part, D // 2)
        if count:

            @pl.when(e == held - 1)
            def _():
                for copy in carry.copies(ins, carried, sems):
                    copy.wait()

    outs = [sds(x.shape, BF), sds(gates.shape, F32)] + [sds(w.shape, BF) for w in weights]
    out_specs = [full(x.shape), full(gates.shape)] + weight_specs(weights)
    scratch = [
        pltpu.VMEM(x.shape, F32),
        pltpu.VMEM((n * lanes, D), BF),
        pltpu.VMEM((n * lanes, D), BF),
    ]
    flops = 2 * held * n * (lanes * D * F * 9 + 3 * lanes * rows * D)
    return call(
        kernel,
        outs + carry.shapes,
        [x, g, gates, slots] + list(weights) + [o[0] for o in ops],
        flops,
        in_specs=[full(x.shape), full(g.shape), full(gates.shape), full(slots.shape)]
        + weight_specs(weights)
        + [ANY_SPEC] * count,
        out_specs=tuple(out_specs + [ANY_SPEC] * count),
        grid=(held,),
        scratch=scratch + carry.scratch(),
        cid=cid if count else None,
    )


def attention_gradients(*parts):
    shard = parts[0].shape[1]
    kv = KEY_VALUE_HEADS * HS
    widths = (D, kv, kv, D, 128, 128)

    def kernel(w0, w1, s0, s1, *outs):
        for layer, (w_ref, s_ref) in enumerate(((w0, s0), (w1, s1))):
            w = w_ref[0].astype(F32)
            s = s_ref[0].astype(F32)
            for j in range(1, w_ref.shape[0]):
                w = w + w_ref[j].astype(F32)
                s = s + s_ref[j].astype(F32)
            outs[0][layer] = w[:, :D]
            outs[1][layer] = w[:, D : D + kv]
            outs[2][layer] = w[:, D + kv : 2 * D]
            outs[3][layer] = s[:, :D]
            outs[4][layer] = w[:, 2 * D :]
            outs[5][layer] = s[:, D:]

    outs = [sds((LAYERS, shard, w), F32) for w in widths]
    return call(
        kernel,
        outs,
        list(parts),
        0,
        in_specs=[full(x.shape) for x in parts],
        out_specs=tuple(full(o.shape) for o in outs),
        grid=(1,),
    )


def expert_gradients(layers, members):
    pairs = [x for pair in layers for x in pair]
    depth = pairs[0].shape[1]
    part = (pairs[1].shape[1] - depth) // 2
    holders = pairs[0].shape[0] // members

    def kernel(*refs):
        ins, (gate_ref, up_ref, down_ref) = refs[:4], refs[4:]
        for layer in range(LAYERS):
            first, second = [
                functools.reduce(
                    lambda x, y: x + y, [r[j, 0].astype(F32) for j in range(holders)]
                )
                for r in ins[2 * layer : 2 * layer + 2]
            ]
            gate_ref[layer, 0] = first
            up_ref[layer, 0] = second[:depth]
            down_ref[layer, 0, :, : D // 2] = second[depth : depth + part]
            down_ref[layer, 0, :, D // 2 :] = second[depth + part :]

    args = [x.reshape((holders, members) + x.shape[1:]) for x in pairs]
    outs = [
        sds((LAYERS, members, depth, F), F32),
        sds((LAYERS, members, depth, F), F32),
        sds((LAYERS, members, part, D), F32),
    ]
    return call(
        kernel,
        outs,
        args,
        0,
        in_specs=[
            pl.BlockSpec((holders, 1) + x.shape[2:], lambda e: (0, e, 0, 0)) for x in args
        ],
        out_specs=tuple(
            pl.BlockSpec((LAYERS, 1) + o.shape[2:], lambda e: (0, e, 0, 0)) for o in outs
        ),
        grid=(members,),
    )


def per_device(
    sizes,
    hidden_in,
    grad_out,
    segments,
    routes,
    attn_gain,
    w_query,
    key_weight,
    value_weight,
    w_output,
    ffn_gain,
    w_router,
    w_gate,
    w_up,
    w_down,
):
    micro, tok, _ = hidden_in.shape
    rows = micro * tok
    grp_size, ctx, planes = sizes
    hq = QUERY_HEADS // ctx
    held = 2 * grp_size
    every = ("grp", "zq", "zp", "core")
    line = ("zq", "zp", "core")
    core = lax.axis_index("core")
    ctx_index = (lax.axis_index("zq") * planes + lax.axis_index("zp")) * 2 + core
    shard = w_query.shape[1]

    def by_plane(x, axis, back=False):
        dims = (planes, grp_size, 2) if back else (grp_size, planes, 2)
        head, tail = x.shape[:axis], x.shape[axis + 1 :]
        y = jnp.swapaxes(x.reshape(head + dims + tail), axis, axis + 1)
        return y.reshape(x.shape)

    def pack(layer):
        return jnp.concatenate(
            [
                w_query[layer],
                key_weight[layer],
                value_weight[layer],
                w_output[layer],
                by_plane(w_router[layer], 1),
                attn_gain[layer][:, None],
                ffn_gain[layer][:, None],
                jnp.zeros((shard, 128 - E - 2), BF),
            ],
            axis=1,
        )

    ids_of = iter(range(1, 100))

    def move(*ops):
        return transfer(ops, next(ids_of), sizes)

    def swap(x):
        return lax.ppermute(x, "core", [(0, 1), (1, 0)])

    def second_shard(layer):
        down = w_down[layer]
        return jnp.concatenate([w_up[layer], down[:, :, : D // 2], down[:, :, D // 2 :]], axis=1)

    def along_line(w):
        copies = ctx // w.shape[0]
        w = jnp.tile(w, (copies, 1, 1)) if copies > 1 else w
        return lax.all_to_all(w, line, 0, 0, tiled=True)

    def plane_gather(w):
        return lax.all_gather(w[None], ("grp", "core"), axis=0, tiled=True)

    grad_rows = grad_out.reshape(rows, D)
    (gate_parts,) = move((w_gate, "line", 0))
    gate_parts, own_pack, own_second = lax.optimization_barrier(
        (gate_parts, pack(0), second_shard(0))
    )
    first, second_parts = move((own_pack, None, "packed"), (own_second[None], "line", 0))
    first, late_pack = lax.optimization_barrier((first, pack(1)))
    packed = [first.reshape(D, -1), lax.all_gather(late_pack, every, axis=0, tiled=True)]
    weights = [[plane_gather(gate_parts), plane_gather(second_parts)], None]

    own_segments = lax.dynamic_slice_in_dim(segments, ctx_index * tok, tok, axis=1)
    prompt = jnp.sum((segments == 0).astype(jnp.int32), axis=1, dtype=jnp.int32)
    before = jnp.sum(
        (segments[:, None, :] < own_segments[:, :, None]).astype(jnp.int32),
        axis=2,
        dtype=jnp.int32,
    )
    places = ctx_index * tok + jnp.arange(tok, dtype=jnp.int32)[None, :]
    places = jnp.where(own_segments == 0, places, prompt[:, None] + places - before)
    places = places.reshape(rows).astype(F32)
    lane = jnp.arange(256, dtype=jnp.int32)
    freqs = jnp.exp(
        (lane % (HS // 2)).astype(F32) * (-2.0 * math.log(10000.0) / HS)
    )
    angles = places[:, None] * freqs[None, :]
    sign = jnp.where((lane % HS) < HS // 2, -1.0, 1.0)[None, :]
    cos_t = jnp.cos(angles)
    sin_t = jnp.sin(angles) * sign
    seg_row = segments[:, None, :]
    seg_col = segments[:, :, None]

    flat = routes.reshape(rows, TOP)
    ids = by_plane(jnp.arange(E, dtype=jnp.int32), 0)
    chosen = jnp.any(ids[:, None, None] == flat[None, :, :], axis=2)
    marks = chosen.astype(BF).reshape(E, micro, tok)
    earlier = (
        jnp.arange(tok)[:, None] < jnp.arange(tok)[None, :]
    ).astype(BF)
    rank = jnp.einsum("emt,ts->ems", marks, earlier, preferred_element_type=F32)
    slot = rank.astype(jnp.int32) + SLOTS * jnp.arange(micro, dtype=jnp.int32)[None, :, None]
    slot = jnp.where(chosen, slot.reshape(E, rows), -1)

    slot = slot.reshape(planes, held, rows)
    chosen_f = chosen.astype(F32)

    saved = []
    parts = (hidden_in.reshape(rows, D),)
    for layer in range(LAYERS):
        got = qkv_forward(
            parts, packed[layer], cos_t, sin_t, ctx, hq, sizes, next(ids_of)
        )
        heads, gains = got[0], got[1]
        stream = parts[0] if layer == 0 else got[2]
        out, lse, mixed = attention_forward(
            heads, seg_row, seg_col, ctx, hq, tok, sizes, next(ids_of)
        )
        stream1, normed, gates = output_forward(
            mixed, stream, packed[layer], gains, chosen_f, ctx, hq, planes, held
        )
        ops = [(normed, "tok", "all"), (gates, "tok", "own")]
        if layer == 0:
            xs, gates_here, slots_here, late_gate = move(
                *ops, (slot, "tok", "own"), (w_gate, "line", 1)
            )
            late_gate = plane_gather(late_gate)
        else:
            xs, gates_here = move(*ops)
        saved.append((stream, heads, out, lse, mixed, stream1, normed, gates, gains, xs, gates_here))
        if layer == 0:
            sent, late_second = experts_forward(
                xs, gates_here, slots_here, weights[0], held,
                [(second_shard(1)[None], "line", 0)], sizes, next(ids_of),
            )
            (came,) = move((sent, "tok", "own"))
            weights[1] = [late_gate, plane_gather(late_second)]
            parts = (stream1, came)
        else:
            sent, last_g = experts_forward(
                xs, gates_here, slots_here, weights[1], held,
                [(grad_rows, "tok", "all")], sizes, next(ids_of),
            )

    sent, last_g = lax.optimization_barrier((sent, last_g))
    final_sum = lax.psum_scatter(sent, "zp", scatter_dimension=0, tiled=True)[0]
    last_stream = stream1

    def plane_scatter(r):
        return lax.psum_scatter(r, ("grp", "core"), scatter_dimension=0, tiled=True)[0]

    def between_cores(x):
        theirs = lax.dynamic_index_in_dim(x, 1 - core, 0, keepdims=False)
        return with_other(x, swap(theirs))

    def with_other(x, came):
        ours = lax.dynamic_index_in_dim(x, core, 0, keepdims=False)
        return by_owner((ours.astype(F32) + came.astype(F32)).astype(BF))

    def by_owner(x):
        return x.reshape(grp_size, ctx // 2, shard, x.shape[1])

    def over_grp(x):
        return jnp.sum(x.astype(F32), axis=0).astype(BF)

    g = grad_rows
    for layer in reversed(range(LAYERS)):
        stream, heads, out, lse, mixed, stream1, normed, gates, gains, xs, gates_here = saved[layer]
        last = layer == LAYERS - 1
        if last:
            gs = last_g
        else:
            gs, last_small, came = move(
                (g.astype(BF), "tok", "all"), (small, "g", "own"), (wide, "sib", "own")
            )
            wide = with_other(wide, came)
        ops = [] if last else [(last_experts[1], "line", "own")]
        res = experts_backward(
            xs, gs, gates_here, slots_here, weights[layer], held, ops, sizes, next(ids_of)
        )
        if last:
            *res, final_sum = lax.optimization_barrier((*res, final_sum))
        else:
            last_second = res[4]
        second_grads = plane_scatter(res[3])
        back = [(res[0], "tok", "own"), (res[1], "tok", "own")]
        if last:
            d_parts, d_gates = move(*back)
            gate_grads, d_parts = lax.optimization_barrier((res[2], d_parts))
            last_experts = [plane_scatter(gate_grads), second_grads]
        else:
            experts = [plane_scatter(res[2]), second_grads]
            d_parts, d_gates, last_wide, last_small = move(
                *back, (wide, "g", "own"), (over_grp(last_small), "z", "own")
            )
        ops = [] if last else [(over_grp(last_wide), "z", "own")]
        g1, small, d_out, *came = output_backward(
            d_parts, d_gates, gates, g, stream1, normed, mixed, packed[layer], gains,
            ctx, hq, planes, shard, ops, sizes, next(ids_of),
        )
        ops = [(small, "sib", "own")]
        if not last:
            last_wide = came[0]
            ops.append((last_experts[0], "line", "own"))
        dx, came, *more = attention_backward(
            heads, d_out, out, lse, seg_row, seg_col, ctx, hq, tok, ops, sizes, next(ids_of)
        )
        small = with_other(small, came)
        if not last:
            last_gate = more[0]
        g, wide = qkv_backward(
            dx, g1, stream, packed[layer], gains, cos_t, sin_t, ctx, hq, shard
        )
    hidden_out = (last_stream + final_sum.astype(F32)).astype(BF).reshape(micro, tok, D)
    first_wide, first_second, first_small = move(
        (between_cores(wide), "g", "own"),
        (experts[1], "line", "own"),
        (small, "g", "own"),
    )
    first_wide, first_gate, first_small = move(
        (over_grp(first_wide), "z", "own"),
        (experts[0], "line", "own"),
        (over_grp(first_small), "z", "own"),
    )

    grads = attention_gradients(first_wide, last_wide, first_small, last_small)
    gq, gk, gv, go, gain_tail, tail = grads
    tops = expert_gradients(
        [(first_gate, first_second), (last_gate, last_second)], 2 * planes
    )
    return (
        hidden_out,
        g.reshape(micro, tok, D),
        gain_tail[:, :, 0],
        gq,
        gk,
        gv,
        go,
        tail[:, :, 33],
        by_plane(tail[:, :, :E], 2, back=True),
        *tops,
    )


def solution(mesh):
    grp_size = mesh.shape["grp"]
    ctx = mesh.shape["ctx"]
    planes = E // grp_size // 2
    fine = Mesh(
        mesh.devices.reshape(grp_size, ctx // (2 * planes), planes, 2),
        ("grp", "zq", "zp", "core"),
    )
    line = ("zq", "zp", "core")
    every = ("grp",) + line
    row = P("grp", line, None)
    placed = (
        row,
        row,
        P("grp", None),
        row,
        P(None, every),
        P(None, every, None),
        P(None, every, None),
        P(None, every, None),
        P(None, every, None),
        P(None, every),
        P(None, every, None),
        P(None, "grp", line, None),
        P(None, "grp", line, None),
        P(None, "grp", line, None),
    )
    return jax.shard_map(
        functools.partial(per_device, (grp_size, ctx, planes)),
        mesh=fine,
        in_specs=placed,
        out_specs=(
            row,
            row,
            P(None, every),
            P(None, every, None),
            P(None, every, None),
            P(None, every, None),
            P(None, every, None),
            P(None, every),
            P(None, every, None),
            P(None, "grp", line, None),
            P(None, "grp", line, None),
            P(None, "grp", line, None),
        ),
        check_vma=False,
    )
```

```python
import functools
import math

import jax
import jax.numpy as jnp
from jax import lax
from jax.experimental import pallas as pl
from jax.experimental.pallas import tpu as pltpu
from jax.sharding import Mesh, PartitionSpec as P

D = 1024
QUERY_HEADS = 16
KEY_VALUE_HEADS = 8
HS = 64
E = 32
F = 512
TOP = 8
LAYERS = 2
CAP = 42
SLOTS = 48
EPSILON = 1e-06
SCALE = float(HS) ** (-0.5)
QB = 256
BF = jnp.bfloat16
F32 = jnp.float32
MESH = pl.DeviceIdType.MESH
PIECES = 8
VMEM_BYTES = 58 * 1024 * 1024
TAIL = 3 * D // 128


def dot(a, b, ca=1, cb=0):
    return lax.dot_general(a, b, (((ca,), (cb,)), ((), ())), preferred_element_type=F32)


def call(kernel, outs, args, flops, in_specs, out_specs, grid, scratch=(), cid=None):
    nbytes = sum(a.size * a.dtype.itemsize for a in args)
    nbytes += sum(math.prod(o.shape) * jnp.dtype(o.dtype).itemsize for o in outs)
    extra = {} if cid is None else {"collective_id": cid, "has_side_effects": True}
    return pl.pallas_call(
        kernel,
        out_shape=tuple(outs),
        scratch_shapes=list(scratch),
        in_specs=in_specs,
        out_specs=out_specs,
        grid=grid,
        compiler_params=pltpu.CompilerParams(vmem_limit_bytes=VMEM_BYTES, **extra),
        cost_estimate=pl.CostEstimate(
            flops=int(flops), bytes_accessed=int(nbytes), transcendentals=0
        ),
    )(*args)


def sds(shape, dtype):
    return jax.ShapeDtypeStruct(tuple(shape), dtype)


def full(shape):
    n = len(shape)
    return pl.BlockSpec(tuple(shape), lambda *_: (0,) * n)


def size_of(group, sizes):
    grp_size, ctx, planes = sizes
    return {"g": grp_size, "tok": planes, "line": ctx, "z": ctx // 2, "sib": 2}[group]


def place_in(group, sizes):
    planes = sizes[2]
    n = size_of(group, sizes)
    zp = lax.axis_index("zp")
    zz = lax.axis_index("zq") * planes + zp
    core = lax.axis_index("core")
    if group == "g":
        return n, lax.axis_index("grp"), lambda p: {"grp": p}
    if group == "tok":
        return n, zp, lambda p: {"zp": p}
    if group == "line":
        return (
            n,
            zz * 2 + core,
            lambda p: {
                "zq": p // (2 * planes),
                "zp": lax.rem(p // 2, planes),
                "core": lax.rem(p, 2),
            },
        )
    if group == "z":
        return n, zz, lambda p: {"zq": p // planes, "zp": lax.rem(p, planes)}
    return n, core, lambda p: {"core": p}


def transfer(ops, cid, sizes):
    grp_size, ctx, _ = sizes
    groups = []
    for _, group, what in ops:
        for name in ("z", "g", "sib") if what == "packed" else (group,):
            if name not in groups:
                groups.append(name)
    shapes = []
    sems = []
    total_sems = 0
    for x, group, what in ops:
        sems.append(total_sems)
        if what == "packed":
            shapes.append(sds((grp_size, ctx) + x.shape, x.dtype))
            zs = ctx // 2
            total_sems += zs + zs * grp_size * 2
            continue
        n = size_of(group, sizes)
        total_sems += PIECES if group == "sib" else 2 * n if what == "all" else n
        rest = x.shape[1:] if group == "sib" else x.shape
        if what != "own":
            rest = (n,) + (x.shape if what == "all" else x.shape[2:])
        shapes.append(sds(rest, x.dtype))
    count = len(ops)

    def kernel(*refs):
        ins = refs[:count]
        outs = refs[count : count + len(shapes)]
        send, recv, local = refs[count + len(shapes) :]
        barrier = pltpu.get_barrier_semaphore()
        total = 0
        for group in groups:
            n, me, where = place_in(group, sizes)
            for k in range(1, n):
                pl.semaphore_signal(
                    barrier, inc=1, device_id=where(lax.rem(me + k, n)), device_id_type=MESH
                )
            total += n - 1
        pl.semaphore_wait(barrier, total)

        def remote(src, dst, at, place):
            copy = pltpu.make_async_remote_copy(
                src_ref=src,
                dst_ref=dst,
                send_sem=send.at[at],
                recv_sem=recv.at[at],
                device_id=place,
                device_id_type=MESH,
            )
            copy.start()
            return copy

        sib_place = {"core": 1 - lax.axis_index("core")}
        sent = []
        own_copies = []

        def start(i):
            _, group, what = ops[i]
            n, me, where = place_in(group or "g", sizes)
            out = outs[i]
            if what == "all":
                copy = pltpu.make_async_copy(ins[i], out.at[me], local.at[i])
                copy.start()
                own_copies.append(copy)

                @pl.when(me < n - 1)
                def _():
                    hop(i, n, ins[i], me, 1).start()

                @pl.when(me > 0)
                def _():
                    hop(i, n, ins[i], me, -1).start()

                return None
            if what == "packed":
                grp = lax.axis_index("grp")
                core = lax.axis_index("core")
                zs, zz, z_place = place_in("z", sizes)
                copy = pltpu.make_async_copy(ins[i], out.at[grp, zz * 2 + core], local.at[i])
                copy.start()
                along = []
                for k in range(1, zs):
                    along.append(
                        remote(
                            ins[i],
                            out.at[grp, zz * 2 + core],
                            sems[i] + k,
                            z_place(lax.rem(zz + k, zs)),
                        )
                    )
                return (i, along, copy)
            if group == "sib":
                size = ins[i].shape[1] // PIECES
                for j in range(PIECES):
                    part = pl.ds(j * size, size)
                    sent.append(
                        remote(ins[i].at[1 - me, part], out.at[part], sems[i] + j, where(1 - me))
                    )
                return None
            copies = []
            for k in range(1, n):
                peer = lax.rem(me + k, n)
                if what == "own":
                    src = ins[i].at[peer]
                else:
                    src = ins[i].at[what, lax.rem(peer, ins[i].shape[1])]
                copies.append(remote(src, out.at[me], sems[i] + k, where(peer)))
            if what == "own":
                src = ins[i].at[me]
            else:
                src = ins[i].at[what, lax.rem(me, ins[i].shape[1])]
            copy = pltpu.make_async_copy(src, out.at[me], local.at[i])
            copy.start()
            own_copies.append(copy)
            sent.extend(copies)
            return None

        def hop(i, n, src, block, way):
            _, me, where = place_in(ops[i][1], sizes)
            return pltpu.make_async_remote_copy(
                src_ref=src,
                dst_ref=outs[i].at[block],
                send_sem=send.at[sems[i] + block + (0 if way > 0 else n)],
                recv_sem=recv.at[sems[i] + block],
                device_id=where(me + way),
                device_id_type=MESH,
            )

        def finish_all(i):
            n, me, _ = place_in(ops[i][1], sizes)
            out = outs[i]
            for far in range(1, n):
                low, high = me - far, me + far

                @pl.when(low >= 0)
                def _():
                    hop(i, n, out.at[low], low, 1).wait_recv()

                    @pl.when(me < n - 1)
                    def _():
                        hop(i, n, out.at[low], low, 1).start()

                @pl.when(high <= n - 1)
                def _():
                    hop(i, n, out.at[high], high, -1).wait_recv()

                    @pl.when(me > 0)
                    def _():
                        hop(i, n, out.at[high], high, -1).start()

            for far in range(n):
                low, high = me - far, me + far

                @pl.when((low >= 0) & (me < n - 1))
                def _():
                    hop(i, n, ins[i] if far == 0 else out.at[low], low, 1).wait_send()

                @pl.when((high <= n - 1) & (me > 0))
                def _():
                    hop(i, n, ins[i] if far == 0 else out.at[high], high, -1).wait_send()

        def finish_packed(i, along, own):
            grp = lax.axis_index("grp")
            core = lax.axis_index("core")
            zs, zz, _ = place_in("z", sizes)
            out = outs[i]
            base = sems[i] + zs
            over = []

            def spread(j, at):
                for m in range(1, grp_size):
                    over.append(
                        (
                            remote(
                                out.at[at[0], at[1]],
                                out.at[at[0], at[1]],
                                base + j * grp_size + m,
                                {"grp": lax.rem(grp + m, grp_size)},
                            ),
                            j,
                            m,
                        )
                    )

            def to_core(j, m, at):
                sent.append(
                    remote(
                        out.at[at[0], at[1]],
                        out.at[at[0], at[1]],
                        base + zs * grp_size + j * grp_size + m,
                        sib_place,
                    )
                )

            own.wait()
            for j in range(zs):
                if j > 0:
                    along[j - 1].wait_recv()
                at = (grp, lax.rem(zz - j + zs, zs) * 2 + core)
                spread(j, at)
                to_core(j, 0, at)
            for copy, j, m in over:
                copy.wait_recv()
                at = (
                    lax.rem(grp - m + grp_size, grp_size),
                    lax.rem(zz - j + zs, zs) * 2 + core,
                )
                to_core(j, m, at)
            for copy in along:
                copy.wait_send()
            for copy, _, _ in over:
                copy.wait_send()

        pending = []
        for i in range(count):
            got = start(i)
            if got is not None:
                pending.append(got)
        for item in pending:
            finish_packed(*item)
        for i in range(count):
            if ops[i][2] == "all":
                finish_all(i)
        for copy in own_copies:
            copy.wait()
        for copy in sent:
            copy.wait()

    total = sum(math.prod(o.shape) * jnp.dtype(o.dtype).itemsize for o in shapes)
    any_spec = pl.BlockSpec(memory_space=pl.ANY)
    return pl.pallas_call(
        kernel,
        out_shape=tuple(shapes),
        in_specs=[any_spec] * count,
        out_specs=tuple([any_spec] * len(shapes)),
        scratch_shapes=[
            pltpu.SemaphoreType.DMA((total_sems,)),
            pltpu.SemaphoreType.DMA((total_sems,)),
            pltpu.SemaphoreType.DMA((count,)),
        ],
        compiler_params=pltpu.CompilerParams(collective_id=cid, has_side_effects=True),
        cost_estimate=pl.CostEstimate(
            flops=0, bytes_accessed=40 * int(total), transcendentals=0
        ),
    )(*[x for x, _, _ in ops])


ANY_SPEC = pl.BlockSpec(memory_space=pl.ANY)


class Carried:
    def __init__(self, ops, sizes):
        self.sizes = sizes
        self.ops = ops
        self.shapes = []
        self.first = []
        self.total = 0
        for x, group, what in ops:
            n = size_of(group, sizes)
            shape = x.shape if what == "own" else (n,) + x.shape[2:]
            if what == "all":
                shape = (n,) + x.shape
            elif group == "sib":
                shape = x.shape[1:]
            self.shapes.append(sds(shape, x.dtype))
            self.first.append(self.total)
            self.total += n

    def scratch(self):
        if not self.ops:
            return []
        return [
            pltpu.SemaphoreType.DMA((self.total,)),
            pltpu.SemaphoreType.DMA((self.total,)),
            pltpu.SemaphoreType.DMA((len(self.ops),)),
        ]

    def enter(self, groups):
        self.wait(self.greet(groups))

    def wait(self, total):
        pl.semaphore_wait(pltpu.get_barrier_semaphore(), total)

    def greet(self, groups):
        barrier = pltpu.get_barrier_semaphore()
        total = 0
        for group in groups:
            n, me, where = place_in(group, self.sizes)
            for k in range(1, n):
                pl.semaphore_signal(
                    barrier, inc=1, device_id=where(lax.rem(me + k, n)), device_id_type=MESH
                )
            total += n - 1
        return total

    def copies(self, ins, outs, sems):
        made = []
        for i, (_, group, what) in enumerate(self.ops):
            send, recv, local = sems
            n, me, where = place_in(group, self.sizes)

            def part(j, i=i, what=what):
                if what == "all":
                    return ins[i]
                if what == "own":
                    return ins[i].at[j]
                return ins[i].at[what, lax.rem(j, ins[i].shape[1])]

            for k in range(1, n):
                peer = lax.rem(me + k, n)
                made.append(
                    pltpu.make_async_remote_copy(
                        src_ref=part(peer),
                        dst_ref=outs[i] if group == "sib" else outs[i].at[me],
                        send_sem=send.at[self.first[i] + k],
                        recv_sem=recv.at[self.first[i] + k],
                        device_id=where(peer),
                        device_id_type=MESH,
                    )
                )
            if group != "sib":
                made.append(pltpu.make_async_copy(part(me), outs[i].at[me], local.at[i]))
        return made


def head_copies(buf, out, sems, m, ctx, tok, sizes):
    send, recv, local = sems
    n, me, where = place_in("line", sizes)
    rows = pl.ds(m * tok, tok)
    made = []
    for k in range(1, n):
        peer = lax.rem(me + k, n)
        made.append(
            pltpu.make_async_remote_copy(
                src_ref=buf.at[m, peer],
                dst_ref=out.at[me, rows],
                send_sem=send.at[m * n + k],
                recv_sem=recv.at[m * n + k],
                device_id=where(peer),
                device_id_type=MESH,
            )
        )
    made.append(pltpu.make_async_copy(buf.at[m, me], out.at[me, rows], local.at[m]))
    return made


def head_scratch(micro, ctx, tok, width):
    return [
        pltpu.VMEM((micro, ctx, tok, width), BF),
        pltpu.SemaphoreType.DMA((micro * ctx,)),
        pltpu.SemaphoreType.DMA((micro * ctx,)),
        pltpu.SemaphoreType.DMA((micro,)),
    ]


def swap_halves(x):
    lane = lax.broadcasted_iota(jnp.int32, x.shape, 1)
    width = x.shape[1]
    up = pltpu.roll(x, width - HS // 2, 1)
    down = pltpu.roll(x, HS // 2, 1)
    return jnp.where((lane & (HS - 1)) < HS // 2, up, down)


def inv_rms_of(x):
    return lax.rsqrt(jnp.mean(x * x, axis=-1, keepdims=True) + EPSILON)


def in_order(parts):
    return parts[0] if len(parts) == 1 else jnp.concatenate(parts, axis=1)


def qkv_forward(stream_parts, packed, cos_t, sin_t, ctx, hq, sizes, cid):
    first = len(stream_parts) == 1
    rows = stream_parts[0].shape[0]
    dup = ctx // KEY_VALUE_HEADS

    meet = Carried([], sizes)

    def kernel(*refs):
        refs, (buf, *sems) = refs[:-4], refs[-4:]
        greeted = meet.greet(["line"])
        if first:
            h_ref, w_ref, t_ref, c_ref, s_ref, out_ref, gains_ref = refs
            x = h_ref[...].astype(F32)
        else:
            h_ref, p_ref, w_ref, t_ref, c_ref, s_ref, out_ref, gains_ref, x_ref = refs
            x = h_ref[...]
            for j in range(p_ref.shape[0]):
                x = x + p_ref[j].astype(F32)
            x_ref[...] = x
        gains = jnp.transpose(t_ref[...].astype(F32))[32:40]
        gains_ref[...] = gains
        normed = (x * inv_rms_of(x) * gains[0:1]).astype(BF)
        cos_v = c_ref[...]
        sin_v = s_ref[...]
        parts = []
        for i in range(8):
            y = dot(normed, w_ref[:, 256 * i : 256 * (i + 1)])
            if i < 6:
                y = y * cos_v + swap_halves(y) * sin_v
            parts.append(y.astype(BF))
        queries, keys, values = in_order(parts[:4]), in_order(parts[4:6]), in_order(parts[6:])
        for i in range(ctx):
            mine = [queries[:, HS * hq * i : HS * hq * (i + 1)]]
            if hq < 2:
                mine.append(jnp.zeros((rows, 128 - HS * hq), BF))
            kv = i // dup
            mine.append(keys[:, HS * kv : HS * (kv + 1)])
            mine.append(values[:, HS * kv : HS * (kv + 1)])
            buf[0, i] = in_order(mine)
        meet.wait(greeted)
        copies = head_copies(buf, out_ref, sems, 0, ctx, rows, sizes)
        for copy in copies:
            copy.start()
        for copy in copies:
            copy.wait()

    args = list(stream_parts) + [packed, packed, cos_t, sin_t]
    in_specs = [full(a.shape) for a in stream_parts] + [
        pl.BlockSpec((D, 2 * D), lambda i: (0, 0)),
        pl.BlockSpec((D, 128), lambda i: (0, TAIL)),
        full(cos_t.shape),
        full(sin_t.shape),
    ]
    outs = [sds((ctx, rows, 256), BF), sds((8, D), F32)]
    if not first:
        outs.append(sds((rows, D), F32))
    return call(
        kernel,
        outs,
        args,
        4 * rows * D * D,
        in_specs=in_specs,
        out_specs=(ANY_SPEC,) + tuple(full(o.shape) for o in outs[1:]),
        grid=(1,),
        scratch=head_scratch(1, ctx, rows, 256),
        cid=cid,
    )


def block_mask(seg_row, seg_col, qb, length):
    keys = (qb + 1) * QB
    qi = lax.broadcasted_iota(jnp.int32, (QB, keys), 0) + qb * QB
    ki = lax.broadcasted_iota(jnp.int32, (QB, keys), 1)
    sr = seg_row[:, :keys]
    return (ki <= qi) & ((sr == 0) | (sr == seg_col))


def attention_forward(x, seg_row, seg_col, ctx, hq, tok, sizes, cid):
    micro = x.shape[1] // tok
    length = ctx * tok
    per = QB // tok

    meet = Carried([], sizes)

    def kernel(x_ref, sr_ref, sc_ref, o_ref, l_ref, mixed_ref, buf, *sems):
        m = pl.program_id(0)
        xs = x_ref[...].reshape(length, 256)
        ks = xs[:, 128:192]
        vs = xs[:, 192:256]
        for qb in range(length // QB):
            keys = (qb + 1) * QB
            rows = slice(qb * QB, (qb + 1) * QB)
            mask = block_mask(sr_ref[0], sc_ref[0, rows, :], qb, length)
            outs = []
            lses = []
            for h in range(hq):
                q = xs[rows, HS * h : HS * (h + 1)]
                s = jnp.where(mask, dot(q, ks[:keys], 1, 1) * SCALE, -1e30)
                top = jnp.max(s, axis=-1, keepdims=True)
                p = jnp.exp(s - top)
                total = jnp.sum(p, axis=-1, keepdims=True)
                o = dot(p.astype(BF), vs[:keys]) / total
                outs.append(o)
                lses.append(jnp.broadcast_to(top + jnp.log(total), (QB, HS)))
            for _ in range(hq, 2):
                outs.append(jnp.zeros((QB, HS), F32))
                lses.append(jnp.zeros((QB, HS), F32))
            done = jnp.concatenate(outs, axis=1).astype(BF).reshape(per, tok, 128)
            o_ref[qb * per : (qb + 1) * per] = done
            buf[m, qb * per : (qb + 1) * per] = done
            l_ref[0, rows, :] = jnp.concatenate(lses, axis=1)

        @pl.when(m == 0)
        def _():
            meet.enter(["line"])

        for copy in head_copies(buf, mixed_ref, sems, m, ctx, tok, sizes):
            copy.start()

        @pl.when(m == micro - 1)
        def _():
            for j in range(micro):
                for copy in head_copies(buf, mixed_ref, sems, j, ctx, tok, sizes):
                    copy.wait()

    return call(
        kernel,
        [
            sds((ctx, micro * tok, 128), BF),
            sds((micro, length, 128), F32),
            sds((ctx, micro * tok, 128), BF),
        ],
        [x, seg_row, seg_col],
        2 * micro * hq * length * length * HS,
        in_specs=[
            pl.BlockSpec((ctx, tok, 256), lambda m: (0, m, 0)),
            pl.BlockSpec((1, 1, length), lambda m: (m, 0, 0)),
            pl.BlockSpec((1, length, 1), lambda m: (m, 0, 0)),
        ],
        out_specs=(
            pl.BlockSpec((ctx, tok, 128), lambda m: (0, m, 0)),
            pl.BlockSpec((1, length, 128), lambda m: (m, 0, 0)),
            ANY_SPEC,
        ),
        grid=(micro,),
        scratch=head_scratch(micro, ctx, tok, 128),
        cid=cid,
    )


def attention_backward(x, d_out, out, lse, seg_row, seg_col, ctx, hq, tok, ops, sizes, cid):
    micro = x.shape[1] // tok
    length = ctx * tok
    per = QB // tok

    carry = Carried(ops, sizes)
    count = len(ops)

    def kernel(x_ref, d_ref, o_ref, l_ref, sr_ref, sc_ref, *rest):
        ins, out_ref, outs = rest[:count], rest[count], rest[count + 1 : 2 * count + 1]
        dk_ref, dv_ref, buf, *sems = rest[2 * count + 1 :]
        sems, carry_sems = sems[:3], sems[3:]
        m = pl.program_id(0)
        dx_ref = buf.at[m]

        @pl.when(m == 0)
        def _():
            carry.enter(["line"] + [group for _, group, _ in ops if group != "line"])
            for copy in carry.copies(ins, outs, carry_sems):
                copy.start()

        xs = x_ref[...].reshape(length, 256)
        ks = xs[:, 128:192]
        vs = xs[:, 192:256]
        ds_all = d_ref[...].reshape(length, 128)
        os_all = o_ref[...].reshape(length, 128)
        dk_ref[...] = jnp.zeros((length, HS), F32)
        dv_ref[...] = jnp.zeros((length, HS), F32)
        for qb in range(length // QB):
            keys = (qb + 1) * QB
            rows = slice(qb * QB, (qb + 1) * QB)
            mask = block_mask(sr_ref[0], sc_ref[0, rows, :], qb, length)
            dqs = []
            for h in range(hq):
                cols = slice(HS * h, HS * (h + 1))
                q = xs[rows, cols]
                do = ds_all[rows, cols]
                delta = jnp.sum(
                    do.astype(F32) * os_all[rows, cols].astype(F32), axis=-1, keepdims=True
                )
                s = dot(q, ks[:keys], 1, 1) * SCALE - l_ref[0, rows, HS * h : HS * h + 1]
                p = jnp.exp(jnp.where(mask, s, -1e30))
                dp = dot(do, vs[:keys], 1, 1)
                ds = (p * (dp - delta) * SCALE).astype(BF)
                dqs.append(dot(ds, ks[:keys]))
                dk_ref[:keys] += dot(ds, q, 0, 0)
                dv_ref[:keys] += dot(p.astype(BF), do, 0, 0)
            for _ in range(hq, 2):
                dqs.append(jnp.zeros((QB, HS), F32))
            dx_ref[qb * per : (qb + 1) * per, :, 0:128] = (
                jnp.concatenate(dqs, axis=1).astype(BF).reshape(per, tok, 128)
            )
        dx_ref[:, :, 128:256] = (
            jnp.concatenate([dk_ref[...], dv_ref[...]], axis=1)
            .astype(BF)
            .reshape(ctx, tok, 128)
        )
        for copy in head_copies(buf, out_ref, sems, m, ctx, tok, sizes):
            copy.start()

        @pl.when(m == micro - 1)
        def _():
            for j in range(micro):
                for copy in head_copies(buf, out_ref, sems, j, ctx, tok, sizes):
                    copy.wait()
            for copy in carry.copies(ins, outs, carry_sems):
                copy.wait()

    return call(
        kernel,
        [sds((ctx, micro * tok, 256), BF)] + carry.shapes,
        [x, d_out, out, lse, seg_row, seg_col] + [o[0] for o in ops],
        5 * micro * hq * length * length * HS,
        in_specs=[
            pl.BlockSpec((ctx, tok, 256), lambda m: (0, m, 0)),
            pl.BlockSpec((ctx, tok, 128), lambda m: (0, m, 0)),
            pl.BlockSpec((ctx, tok, 128), lambda m: (0, m, 0)),
            pl.BlockSpec((1, length, 128), lambda m: (m, 0, 0)),
            pl.BlockSpec((1, 1, length), lambda m: (m, 0, 0)),
            pl.BlockSpec((1, length, 1), lambda m: (m, 0, 0)),
        ]
        + [ANY_SPEC] * count,
        out_specs=tuple([ANY_SPEC] * (count + 1)),
        grid=(micro,),
        scratch=[pltpu.VMEM((length, HS), F32), pltpu.VMEM((length, HS), F32)]
        + head_scratch(micro, ctx, tok, 256)
        + carry.scratch(),
        cid=cid,
    )


def side_by_side(m_ref, ctx, hq):
    return jnp.concatenate([m_ref[i][:, : HS * hq] for i in range(ctx)], axis=1)


def output_forward(mixed, stream, packed, gains, chosen, ctx, hq, n, held):
    rows = stream.shape[0]

    def kernel(m_ref, x_ref, w_ref, t_ref, g_ref, c_ref, s_ref, n_ref, gate_ref):
        x = x_ref[...].astype(F32) + dot(side_by_side(m_ref, ctx, hq), w_ref[...])
        s_ref[...] = x
        normed = (x * inv_rms_of(x) * g_ref[1:2]).astype(BF)
        n_ref[...] = normed
        logits = dot(t_ref[...], normed, 0, 1)[:E]
        named = c_ref[...] > 0.0
        logits = jnp.where(named, logits, -1e30)
        top = jnp.max(logits, axis=0, keepdims=True)
        p = jnp.where(named, jnp.exp(logits - top), 0.0)
        gates = p / jnp.sum(p, axis=0, keepdims=True)
        for j in range(n):
            gate_ref[j] = gates[held * j : held * (j + 1)]

    outs = [sds((rows, D), F32), sds((rows, D), BF), sds((n, held, rows), F32)]
    return call(
        kernel,
        outs,
        [mixed, stream, packed, packed, gains, chosen],
        2 * rows * D * D,
        in_specs=[
            full(mixed.shape),
            full(stream.shape),
            pl.BlockSpec((D, D), lambda i: (0, 2)),
            pl.BlockSpec((D, 128), lambda i: (0, TAIL)),
            full(gains.shape),
            full(chosen.shape),
        ],
        out_specs=tuple(full(o.shape) for o in outs),
        grid=(1,),
    )


def by_core(x, shard):
    y = x.astype(BF).reshape(x.shape[0] // (2 * shard), 2, shard, x.shape[1])
    return [y[:, c].reshape(x.shape[0] // 2, x.shape[1]) for c in range(2)]


def norm_back(x, gain, d_normed):
    r = inv_rms_of(x)
    grad_gain = jnp.sum(d_normed * x * r, axis=0, keepdims=True)
    q = d_normed * gain
    dx = r * q - x * (r * r * r) * jnp.mean(x * q, axis=-1, keepdims=True)
    return dx, grad_gain


def output_backward(parts, d_gates, gates, g, stream, normed, mixed, packed, gains, ctx, hq, n, shard, ops, sizes, cid):
    rows = stream.shape[0]

    carry = Carried(ops, sizes)
    count = len(ops)

    def kernel(p_ref, dg_ref, gt_ref, g_ref, x_ref, nm_ref, m_ref, w_ref, t_ref, gain_ref, *rest):
        ins, (g1_ref, gw_ref, dm_ref) = rest[:count], rest[count : count + 3]
        carried, rest = rest[count + 3 : 2 * count + 3], rest[2 * count + 3 :]
        buf, sems, carry_sems = rest[0], rest[1:4], rest[4:]
        carry.enter(["line"] + [group for _, group, _ in ops])
        others = carry.copies(ins, carried, carry_sems)
        for copy in others:
            copy.start()
        gates_v = jnp.concatenate([gt_ref[j] for j in range(n)], axis=0)
        dgate_v = jnp.concatenate([dg_ref[j] for j in range(n)], axis=0)
        mean = jnp.sum(gates_v * dgate_v, axis=0, keepdims=True)
        d_logits = (gates_v * (dgate_v - mean)).astype(BF)
        d_logits = jnp.concatenate([d_logits, jnp.zeros((128 - E, rows), BF)], axis=0)
        router = t_ref[...]
        d_normed = dot(d_logits, router, 0, 1)
        for j in range(n):
            d_normed = d_normed + p_ref[j].astype(F32)
        x = x_ref[...]
        dx, grad_gain = norm_back(x, gain_ref[1:2], d_normed)
        g1 = g_ref[...].astype(F32) + dx
        g1_ref[...] = g1
        low = g1.astype(BF)
        dm = dot(low, w_ref[...], 1, 1).astype(BF)
        for i in range(ctx):
            part = dm[:, HS * hq * i : HS * hq * (i + 1)]
            if hq < 2:
                part = jnp.concatenate([part, jnp.zeros((rows, 128 - HS * hq), BF)], axis=1)
            buf[0, i] = part
        copies = head_copies(buf, dm_ref, sems, 0, ctx, rows, sizes)
        for copy in copies:
            copy.start()
        grad_out = dot(side_by_side(m_ref, ctx, hq), low, 0, 0)
        for c, value in enumerate(by_core(grad_out, shard)):
            gw_ref[c, :, 0:D] = value
        grad_router = dot(nm_ref[...], d_logits, 0, 1)
        row = lax.broadcasted_iota(jnp.int32, (128, D), 0)
        cols = jnp.where(row == 33, jnp.broadcast_to(grad_gain, (128, D)), 0.0)
        for c, value in enumerate(by_core(grad_router + jnp.transpose(cols), shard)):
            gw_ref[c, :, D : D + 128] = value
        for copy in copies + others:
            copy.wait()

    outs = [sds((rows, D), F32), sds((2, D // 2, D + 128), BF), sds((ctx, rows, 128), BF)]
    args = [parts, d_gates, gates, g, stream, normed, mixed, packed, packed, gains]
    in_specs = [full(a.shape) for a in args]
    in_specs[7] = pl.BlockSpec((D, D), lambda i: (0, 2))
    in_specs[8] = pl.BlockSpec((D, 128), lambda i: (0, TAIL))
    return call(
        kernel,
        outs + carry.shapes,
        args + [o[0] for o in ops],
        4 * rows * D * D,
        in_specs=in_specs + [ANY_SPEC] * count,
        out_specs=tuple([full(o.shape) for o in outs[:2]] + [ANY_SPEC] * (count + 1)),
        grid=(1,),
        scratch=head_scratch(1, ctx, rows, 128) + carry.scratch(),
        cid=cid,
    )


def qkv_backward(dx, g1, stream, packed, gains, cos_t, sin_t, ctx, hq, shard):
    rows = g1.shape[0]
    dup = ctx // KEY_VALUE_HEADS

    def kernel(d_ref, g_ref, x_ref, w_ref, gain_ref, c_ref, s_ref, out_ref, gw_ref, low_ref):
        x = x_ref[...].astype(F32)
        gain = gain_ref[0:1]
        normed = (x * inv_rms_of(x) * gain).astype(BF)
        cos_v = c_ref[...]
        sin_v = s_ref[...]
        queries = in_order([d_ref[i][:, : HS * hq] for i in range(ctx)])
        both = []
        for head in range(KEY_VALUE_HEADS):
            total = d_ref[head * dup][:, 128:256]
            if dup > 1:
                total = total.astype(F32)
                for r in range(1, dup):
                    total = total + d_ref[head * dup + r][:, 128:256].astype(F32)
            both.append(total)
        keys = in_order([t[:, :HS] for t in both])
        values = in_order([t[:, HS:] for t in both])
        d_normed = jnp.zeros((rows, D), F32)
        for i in range(8):
            if i < 4:
                y = queries[:, 256 * i : 256 * (i + 1)]
            elif i < 6:
                y = keys[:, 256 * (i - 4) : 256 * (i - 3)]
            else:
                y = values[:, 256 * (i - 6) : 256 * (i - 5)]
            if i < 6:
                y = y.astype(F32)
                y = y * cos_v - swap_halves(y) * sin_v
            lin = y.astype(BF)
            cols = slice(256 * i, 256 * (i + 1))
            d_normed = d_normed + dot(lin, w_ref[:, cols], 1, 1)
            for c, value in enumerate(by_core(dot(normed, lin, 0, 0), shard)):
                gw_ref[c, :, cols] = value
        back, grad_gain = norm_back(x, gain, d_normed)
        total = g_ref[...] + back
        out_ref[...] = total
        low_ref[...] = total.astype(BF)
        row = lax.broadcasted_iota(jnp.int32, (128, D), 0)
        cols = jnp.where(row == 0, jnp.broadcast_to(grad_gain, (128, D)), 0.0)
        for c, value in enumerate(by_core(jnp.transpose(cols), shard)):
            gw_ref[c, :, 2 * D : 2 * D + 128] = value

    outs = [sds((rows, D), F32), sds((2, D // 2, 2 * D + 128), BF), sds((rows, D), BF)]
    args = [dx, g1, stream, packed, gains, cos_t, sin_t]
    in_specs = [full(a.shape) for a in args]
    in_specs[3] = pl.BlockSpec((D, 2 * D), lambda i: (0, 0))
    return call(
        kernel,
        outs,
        args,
        8 * rows * D * D,
        in_specs=in_specs,
        out_specs=tuple(full(o.shape) for o in outs),
        grid=(1,),
    )


def pick_matrix(slot_row, rows):
    at = lax.broadcasted_iota(jnp.int32, (2 * SLOTS, rows), 0)
    return at == slot_row


def weight_specs(weights):
    return [
        pl.BlockSpec((1,) + w.shape[1:], lambda e: (e, 0, 0, 0)) for w in weights
    ]


def matrices(first_ref, second_ref):
    ctx, depth, _ = first_ref.shape[1:]
    half = F // ctx
    second = second_ref[0]
    return (
        first_ref[0].reshape(D, F),
        second[:, :depth].reshape(D, F),
        second[:, depth : depth + half].reshape(F, D // 2),
        second[:, depth + half :].reshape(F, D // 2),
    )


def experts_forward(x, gates, slots, weights, held, ops=(), sizes=None, cid=None):
    n, rows, _ = x.shape
    lanes = 2 * SLOTS


    carry = Carried(ops, sizes)
    count = len(ops)

    def kernel(x_ref, g_ref, s_ref, w0, w1, *rest):
        ins, out_ref, outs = rest[:count], rest[count], rest[count + 1 : 2 * count + 1]
        acc_ref, row_ref, eo_ref, *sems = rest[2 * count + 1 :]
        e = pl.program_id(0)
        if count:

            @pl.when(e == 0)
            def _():
                carry.enter(sorted(set(group for _, group, _ in ops)))
                for copy in carry.copies(ins, outs, sems):
                    copy.start()

        w_gate, w_up, down_l, down_r = matrices(w0, w1)
        for s in range(n):
            pick = pick_matrix(s_ref[s, pl.ds(e, 1), :], rows).astype(BF)
            row_ref[lanes * s : lanes * (s + 1), :] = dot(pick, x_ref[s]).astype(BF)
        rws = row_ref[...]
        ga = dot(rws, w_gate)
        up = dot(rws, w_up)
        hidden = (ga * jax.nn.sigmoid(ga) * up).astype(BF)
        eo_ref[:, : D // 2] = dot(hidden, down_l).astype(BF)
        eo_ref[:, D // 2 :] = dot(hidden, down_r).astype(BF)
        for s in range(n):
            pick = pick_matrix(s_ref[s, pl.ds(e, 1), :], rows)
            gated = jnp.where(pick, g_ref[s, pl.ds(e, 1), :], 0.0).astype(BF)
            add = dot(gated, eo_ref[lanes * s : lanes * (s + 1), :], 0, 0)

            @pl.when(e == 0)
            def _():
                acc_ref[s] = add.astype(F32)

            @pl.when((e > 0) & (e < held - 1))
            def _():
                acc_ref[s] = (acc_ref[s].astype(F32) + add).astype(F32)

            @pl.when(e == held - 1)
            def _():
                out_ref[s] = (acc_ref[s].astype(F32) + add).astype(BF)

        if count:

            @pl.when(e == held - 1)
            def _():
                for copy in carry.copies(ins, outs, sems):
                    copy.wait()

    flops = 2 * held * n * (lanes * D * F * 3 + 2 * lanes * rows * D)
    return call(
        kernel,
        [sds(x.shape, BF)] + carry.shapes,
        [x, gates, slots] + list(weights) + [o[0] for o in ops],
        flops,
        in_specs=[full(x.shape), full(gates.shape), full(slots.shape)]
        + weight_specs(weights)
        + [ANY_SPEC] * count,
        out_specs=tuple([full(x.shape)] + [ANY_SPEC] * count),
        grid=(held,),
        scratch=[
            pltpu.VMEM(x.shape, F32),
            pltpu.VMEM((n * lanes, D), BF),
            pltpu.VMEM((n * lanes, D), BF),
        ]
        + carry.scratch(),
        cid=cid if count else None,
    )


def experts_backward(x, g, gates, slots, weights, held, ops=(), sizes=None, cid=None):
    n, rows, _ = x.shape
    lanes = 2 * SLOTS


    carry = Carried(ops, sizes)
    count = len(ops)

    def kernel(x_ref, gr_ref, g_ref, s_ref, w0, w1, *rest):
        ins, rest = rest[:count], rest[count:]
        dx_ref, dg_ref, first_grad, second_grad, *rest = rest
        carried, rest = rest[:count], rest[count:]
        acc_ref, row_ref, grow_ref, *sems = rest
        e = pl.program_id(0)
        if count:

            @pl.when(e == 0)
            def _():
                carry.enter(sorted(set(group for _, group, _ in ops)))
                for copy in carry.copies(ins, carried, sems):
                    copy.start()

        w_gate, w_up, down_l, down_r = matrices(w0, w1)
        slot_gates = []
        for s in range(n):
            mine = slice(lanes * s, lanes * (s + 1))
            pick = pick_matrix(s_ref[s, pl.ds(e, 1), :], rows)
            low = pick.astype(BF)
            row_ref[mine, :] = dot(low, x_ref[s]).astype(BF)
            grow_ref[mine, :] = dot(low, gr_ref[s]).astype(BF)
            gated = jnp.where(pick, g_ref[s, pl.ds(e, 1), :], 0.0)
            slot_gates.append(jnp.sum(gated, axis=1, keepdims=True))
        gate = jnp.concatenate(slot_gates, axis=0)
        rws = row_ref[...]
        grows = grow_ref[...]
        ga = dot(rws, w_gate)
        up = dot(rws, w_up)
        sig = jax.nn.sigmoid(ga)
        act = ga * sig
        hidden_f = act * up
        hidden = hidden_f.astype(BF)
        dhg = dot(grows[:, : D // 2], down_l, 1, 1) + dot(grows[:, D // 2 :], down_r, 1, 1)
        d_gate = jnp.sum(hidden.astype(F32) * dhg, axis=1, keepdims=True)
        dh = dhg * gate
        dga = (dh * up * (sig * (1.0 + ga * (1.0 - sig)))).astype(BF)
        dup = (dh * act).astype(BF)
        drow = (dot(dga, w_gate, 1, 1) + dot(dup, w_up, 1, 1)).astype(BF)
        for s in range(n):
            mine = slice(lanes * s, lanes * (s + 1))
            pick = pick_matrix(s_ref[s, pl.ds(e, 1), :], rows)
            dg_ref[s, pl.ds(e, 1), :] = jnp.sum(
                jnp.where(pick, d_gate[mine], 0.0), axis=0, keepdims=True
            )
            add = dot(pick.astype(BF), drow[mine], 0, 0)

            @pl.when(e == 0)
            def _():
                acc_ref[s] = add

            @pl.when((e > 0) & (e < held - 1))
            def _():
                acc_ref[s] += add

            @pl.when(e == held - 1)
            def _():
                dx_ref[s] = (acc_ref[s] + add).astype(BF)

        dslot = (grows.astype(F32) * gate).astype(BF)
        ctx, depth, _ = first_grad.shape[1:]
        part = F // ctx
        both = dot(rws, jnp.concatenate([dga, dup], axis=1), 0, 0).astype(BF)
        first_grad[0] = both[:, :F].reshape(ctx, depth, F)
        second_grad[0, :, :depth, :] = both[:, F:].reshape(ctx, depth, F)
        down = dot(hidden, dslot, 0, 0).astype(BF)
        for k in range(2):
            at_row = depth + part * k
            second_grad[0, :, at_row : at_row + part, :] = down[
                :, D // 2 * k : D // 2 * (k + 1)
            ].reshape(ctx, part, D // 2)
        if count:

            @pl.when(e == held - 1)
            def _():
                for copy in carry.copies(ins, carried, sems):
                    copy.wait()

    outs = [sds(x.shape, BF), sds(gates.shape, F32)] + [sds(w.shape, BF) for w in weights]
    out_specs = [full(x.shape), full(gates.shape)] + weight_specs(weights)
    scratch = [
        pltpu.VMEM(x.shape, F32),
        pltpu.VMEM((n * lanes, D), BF),
        pltpu.VMEM((n * lanes, D), BF),
    ]
    flops = 2 * held * n * (lanes * D * F * 9 + 3 * lanes * rows * D)
    return call(
        kernel,
        outs + carry.shapes,
        [x, g, gates, slots] + list(weights) + [o[0] for o in ops],
        flops,
        in_specs=[full(x.shape), full(g.shape), full(gates.shape), full(slots.shape)]
        + weight_specs(weights)
        + [ANY_SPEC] * count,
        out_specs=tuple(out_specs + [ANY_SPEC] * count),
        grid=(held,),
        scratch=scratch + carry.scratch(),
        cid=cid if count else None,
    )


def attention_gradients(*parts):
    shard = parts[0].shape[1]
    kv = KEY_VALUE_HEADS * HS
    widths = (D, kv, kv, D, 128, 128)

    def kernel(w0, w1, s0, s1, *outs):
        for layer, (w_ref, s_ref) in enumerate(((w0, s0), (w1, s1))):
            w = w_ref[0].astype(F32)
            s = s_ref[0].astype(F32)
            for j in range(1, w_ref.shape[0]):
                w = w + w_ref[j].astype(F32)
                s = s + s_ref[j].astype(F32)
            outs[0][layer] = w[:, :D]
            outs[1][layer] = w[:, D : D + kv]
            outs[2][layer] = w[:, D + kv : 2 * D]
            outs[3][layer] = s[:, :D]
            outs[4][layer] = w[:, 2 * D :]
            outs[5][layer] = s[:, D:]

    outs = [sds((LAYERS, shard, w), F32) for w in widths]
    return call(
        kernel,
        outs,
        list(parts),
        0,
        in_specs=[full(x.shape) for x in parts],
        out_specs=tuple(full(o.shape) for o in outs),
        grid=(1,),
    )


def expert_gradients(layers, members):
    pairs = [x for pair in layers for x in pair]
    depth = pairs[0].shape[1]
    part = (pairs[1].shape[1] - depth) // 2
    holders = pairs[0].shape[0] // members

    def kernel(*refs):
        ins, (gate_ref, up_ref, down_ref) = refs[:4], refs[4:]
        for layer in range(LAYERS):
            first, second = [
                functools.reduce(
                    lambda x, y: x + y, [r[j, 0].astype(F32) for j in range(holders)]
                )
                for r in ins[2 * layer : 2 * layer + 2]
            ]
            gate_ref[layer, 0] = first
            up_ref[layer, 0] = second[:depth]
            down_ref[layer, 0, :, : D // 2] = second[depth : depth + part]
            down_ref[layer, 0, :, D // 2 :] = second[depth + part :]

    args = [x.reshape((holders, members) + x.shape[1:]) for x in pairs]
    outs = [
        sds((LAYERS, members, depth, F), F32),
        sds((LAYERS, members, depth, F), F32),
        sds((LAYERS, members, part, D), F32),
    ]
    return call(
        kernel,
        outs,
        args,
        0,
        in_specs=[
            pl.BlockSpec((holders, 1) + x.shape[2:], lambda e: (0, e, 0, 0)) for x in args
        ],
        out_specs=tuple(
            pl.BlockSpec((LAYERS, 1) + o.shape[2:], lambda e: (0, e, 0, 0)) for o in outs
        ),
        grid=(members,),
    )


def per_device(
    sizes,
    hidden_in,
    grad_out,
    segments,
    routes,
    attn_gain,
    w_query,
    key_weight,
    value_weight,
    w_output,
    ffn_gain,
    w_router,
    w_gate,
    w_up,
    w_down,
):
    micro, tok, _ = hidden_in.shape
    rows = micro * tok
    grp_size, ctx, planes = sizes
    hq = QUERY_HEADS // ctx
    held = 2 * grp_size
    every = ("grp", "zq", "zp", "core")
    line = ("zq", "zp", "core")
    core = lax.axis_index("core")
    ctx_index = (lax.axis_index("zq") * planes + lax.axis_index("zp")) * 2 + core
    shard = w_query.shape[1]

    def by_plane(x, axis, back=False):
        dims = (planes, grp_size, 2) if back else (grp_size, planes, 2)
        head, tail = x.shape[:axis], x.shape[axis + 1 :]
        y = jnp.swapaxes(x.reshape(head + dims + tail), axis, axis + 1)
        return y.reshape(x.shape)

    def pack(layer):
        return jnp.concatenate(
            [
                w_query[layer],
                key_weight[layer],
                value_weight[layer],
                w_output[layer],
                by_plane(w_router[layer], 1),
                attn_gain[layer][:, None],
                ffn_gain[layer][:, None],
                jnp.zeros((shard, 128 - E - 2), BF),
            ],
            axis=1,
        )

    ids_of = iter(range(1, 100))

    def move(*ops):
        return transfer(ops, next(ids_of), sizes)

    def swap(x):
        return lax.ppermute(x, "core", [(0, 1), (1, 0)])

    def second_shard(layer):
        down = w_down[layer]
        return jnp.concatenate([w_up[layer], down[:, :, : D // 2], down[:, :, D // 2 :]], axis=1)

    def along_line(w):
        copies = ctx // w.shape[0]
        w = jnp.tile(w, (copies, 1, 1)) if copies > 1 else w
        return lax.all_to_all(w, line, 0, 0, tiled=True)

    def plane_gather(w):
        return lax.all_gather(w[None], ("grp", "core"), axis=0, tiled=True)

    grad_rows = grad_out.reshape(rows, D)
    (gate_parts,) = move((w_gate, "line", 0))
    gate_parts, own_pack, own_second = lax.optimization_barrier(
        (gate_parts, pack(0), second_shard(0))
    )
    first, second_parts = move((own_pack, None, "packed"), (own_second[None], "line", 0))
    first, late_pack = lax.optimization_barrier((first, pack(1)))
    packed = [first.reshape(D, -1), lax.all_gather(late_pack, every, axis=0, tiled=True)]
    weights = [[plane_gather(gate_parts), plane_gather(second_parts)], None]

    own_segments = lax.dynamic_slice_in_dim(segments, ctx_index * tok, tok, axis=1)
    prompt = jnp.sum((segments == 0).astype(jnp.int32), axis=1, dtype=jnp.int32)
    before = jnp.sum(
        (segments[:, None, :] < own_segments[:, :, None]).astype(jnp.int32),
        axis=2,
        dtype=jnp.int32,
    )
    places = ctx_index * tok + jnp.arange(tok, dtype=jnp.int32)[None, :]
    places = jnp.where(own_segments == 0, places, prompt[:, None] + places - before)
    places = places.reshape(rows).astype(F32)
    lane = jnp.arange(256, dtype=jnp.int32)
    freqs = jnp.exp(
        (lane % (HS // 2)).astype(F32) * (-2.0 * math.log(10000.0) / HS)
    )
    angles = places[:, None] * freqs[None, :]
    sign = jnp.where((lane % HS) < HS // 2, -1.0, 1.0)[None, :]
    cos_t = jnp.cos(angles)
    sin_t = jnp.sin(angles) * sign
    seg_row = segments[:, None, :]
    seg_col = segments[:, :, None]

    flat = routes.reshape(rows, TOP)
    ids = by_plane(jnp.arange(E, dtype=jnp.int32), 0)
    chosen = jnp.any(ids[:, None, None] == flat[None, :, :], axis=2)
    marks = chosen.astype(BF).reshape(E, micro, tok)
    earlier = (
        jnp.arange(tok)[:, None] < jnp.arange(tok)[None, :]
    ).astype(BF)
    rank = jnp.einsum("emt,ts->ems", marks, earlier, preferred_element_type=F32)
    slot = rank.astype(jnp.int32) + SLOTS * jnp.arange(micro, dtype=jnp.int32)[None, :, None]
    slot = jnp.where(chosen, slot.reshape(E, rows), -1)

    slot = slot.reshape(planes, held, rows)
    chosen_f = chosen.astype(F32)

    saved = []
    parts = (hidden_in.reshape(rows, D),)
    for layer in range(LAYERS):
        got = qkv_forward(
            parts, packed[layer], cos_t, sin_t, ctx, hq, sizes, next(ids_of)
        )
        heads, gains = got[0], got[1]
        stream = parts[0] if layer == 0 else got[2]
        out, lse, mixed = attention_forward(
            heads, seg_row, seg_col, ctx, hq, tok, sizes, next(ids_of)
        )
        stream1, normed, gates = output_forward(
            mixed, stream, packed[layer], gains, chosen_f, ctx, hq, planes, held
        )
        ops = [(normed, "tok", "all"), (gates, "tok", "own")]
        if layer == 0:
            xs, gates_here, slots_here, late_gate = move(
                *ops, (slot, "tok", "own"), (w_gate, "line", 1)
            )
            late_gate = plane_gather(late_gate)
        else:
            xs, gates_here = move(*ops)
        saved.append((stream, heads, out, lse, mixed, stream1, normed, gates, gains, xs, gates_here))
        if layer == 0:
            sent, late_second = experts_forward(
                xs, gates_here, slots_here, weights[0], held,
                [(second_shard(1)[None], "line", 0)], sizes, next(ids_of),
            )
            (came,) = move((sent, "tok", "own"))
            weights[1] = [late_gate, plane_gather(late_second)]
            parts = (stream1, came)
        else:
            sent, last_g = experts_forward(
                xs, gates_here, slots_here, weights[1], held,
                [(grad_rows, "tok", "all")], sizes, next(ids_of),
            )

    sent, last_g = lax.optimization_barrier((sent, last_g))
    final_sum = lax.psum_scatter(sent, "zp", scatter_dimension=0, tiled=True)[0]
    last_stream = stream1

    def plane_scatter(r):
        return lax.psum_scatter(r, ("grp", "core"), scatter_dimension=0, tiled=True)[0]

    def between_cores(x):
        theirs = lax.dynamic_index_in_dim(x, 1 - core, 0, keepdims=False)
        return with_other(x, swap(theirs))

    def with_other(x, came):
        ours = lax.dynamic_index_in_dim(x, core, 0, keepdims=False)
        return by_owner((ours.astype(F32) + came.astype(F32)).astype(BF))

    def by_owner(x):
        return x.reshape(grp_size, ctx // 2, shard, x.shape[1])

    def over_grp(x):
        return jnp.sum(x.astype(F32), axis=0).astype(BF)

    g = grad_rows
    for layer in reversed(range(LAYERS)):
        stream, heads, out, lse, mixed, stream1, normed, gates, gains, xs, gates_here = saved[layer]
        last = layer == LAYERS - 1
        if last:
            gs = last_g
        else:
            gs, last_small, came = move(
                (low_g, "tok", "all"), (small, "g", "own"), (wide, "sib", "own")
            )
            wide = with_other(wide, came)
        ops = [] if last else [(last_experts[1], "line", "own")]
        res = experts_backward(
            xs, gs, gates_here, slots_here, weights[layer], held, ops, sizes, next(ids_of)
        )
        if last:
            *res, final_sum = lax.optimization_barrier((*res, final_sum))
        else:
            last_second = res[4]
        second_grads = plane_scatter(res[3])
        back = [(res[0], "tok", "own"), (res[1], "tok", "own")]
        if last:
            d_parts, d_gates = move(*back)
            gate_grads, d_parts = lax.optimization_barrier((res[2], d_parts))
            last_experts = [plane_scatter(gate_grads), second_grads]
        else:
            experts = [plane_scatter(res[2]), second_grads]
            d_parts, d_gates, last_wide, last_small = move(
                *back, (wide, "g", "own"), (over_grp(last_small), "z", "own")
            )
        ops = [] if last else [(over_grp(last_wide), "z", "own")]
        g1, small, d_out, *came = output_backward(
            d_parts, d_gates, gates, g, stream1, normed, mixed, packed[layer], gains,
            ctx, hq, planes, shard, ops, sizes, next(ids_of),
        )
        ops = [(small, "sib", "own")]
        if not last:
            last_wide = came[0]
            ops.append((last_experts[0], "line", "own"))
        dx, came, *more = attention_backward(
            heads, d_out, out, lse, seg_row, seg_col, ctx, hq, tok, ops, sizes, next(ids_of)
        )
        small = with_other(small, came)
        if not last:
            last_gate = more[0]
        g, wide, low_g = qkv_backward(
            dx, g1, stream, packed[layer], gains, cos_t, sin_t, ctx, hq, shard
        )
    hidden_out = (last_stream + final_sum.astype(F32)).astype(BF).reshape(micro, tok, D)
    first_wide, first_second, first_small = move(
        (between_cores(wide), "g", "own"),
        (experts[1], "line", "own"),
        (small, "g", "own"),
    )
    first_wide, first_gate, first_small = move(
        (over_grp(first_wide), "z", "own"),
        (experts[0], "line", "own"),
        (over_grp(first_small), "z", "own"),
    )

    grads = attention_gradients(first_wide, last_wide, first_small, last_small)
    gq, gk, gv, go, gain_tail, tail = grads
    tops = expert_gradients(
        [(first_gate, first_second), (last_gate, last_second)], 2 * planes
    )
    return (
        hidden_out,
        g.reshape(micro, tok, D),
        gain_tail[:, :, 0],
        gq,
        gk,
        gv,
        go,
        tail[:, :, 33],
        by_plane(tail[:, :, :E], 2, back=True),
        *tops,
    )


def solution(mesh):
    grp_size = mesh.shape["grp"]
    ctx = mesh.shape["ctx"]
    planes = E // grp_size // 2
    fine = Mesh(
        mesh.devices.reshape(grp_size, ctx // (2 * planes), planes, 2),
        ("grp", "zq", "zp", "core"),
    )
    line = ("zq", "zp", "core")
    every = ("grp",) + line
    row = P("grp", line, None)
    placed = (
        row,
        row,
        P("grp", None),
        row,
        P(None, every),
        P(None, every, None),
        P(None, every, None),
        P(None, every, None),
        P(None, every, None),
        P(None, every),
        P(None, every, None),
        P(None, "grp", line, None),
        P(None, "grp", line, None),
        P(None, "grp", line, None),
    )
    return jax.shard_map(
        functools.partial(per_device, (grp_size, ctx, planes)),
        mesh=fine,
        in_specs=placed,
        out_specs=(
            row,
            row,
            P(None, every),
            P(None, every, None),
            P(None, every, None),
            P(None, every, None),
            P(None, every, None),
            P(None, every),
            P(None, every, None),
            P(None, "grp", line, None),
            P(None, "grp", line, None),
            P(None, "grp", line, None),
        ),
        check_vma=False,
    )
```
